256 devices in a mesh: ctx: 32 (over z, y_hi, core), exp: 8 (over y_lo, x).
Axes of the slice: x: 4, y: 4 (y_hi: 2, y_lo: 2; y = y_hi * 2 + y_lo), z: 8, core: 2. Of those that a mesh axis runs over, the one named last changes fastest.
Arguments:
- hidden_in: bfloat16 [8, 6144, 1024], P('exp', 'ctx'), may hold values from -6 to 6
- queries: bfloat16 [8, 6144, 1024], P('exp', 'ctx'), may hold values from -128 to 128
- key_proj: bfloat16 [8, 6144, 256], P('exp', 'ctx'), may hold values from -16 to 16
- value_proj: bfloat16 [8, 6144, 256], P('exp', 'ctx'), may hold values from -6 to 6
- tile_mask: int32 [8, 192, 192], P('exp', 'ctx'), may hold values from 0 to 1, as said below
- out_weight: bfloat16 [1024, 1024], replicated, may hold values from -0.1875 to 0.1875
- moe_gain: float32 [1024], replicated, may hold values from 0.1 to 1.9
- gate_weight: bfloat16 [8, 1024, 1792], P('exp', 'ctx'), may hold values from -0.1875 to 0.1875
- up_weight: bfloat16 [8, 1024, 1792], P('exp', 'ctx'), may hold values from -0.1875 to 0.1875
- down_weight: bfloat16 [8, 1024, 1792], P('exp', 'ctx'), may hold values from -0.125 to 0.125
- expert_ids: int32 [8, 6144, 2], P('exp', 'ctx'), may hold values from 0 to 7, all different within a row; in each aligned block of 192 rows (0 to 191, 192 to 383, ..., all dimensions but the last counted through in order) at most 72 rows name the same one
- gate_probs: float32 [8, 6144, 2], P('exp', 'ctx'), may hold values from 0.05 to 0.95, as said below
Outputs:
- attention_out: bfloat16 [8, 6144, 1024], P('exp', 'ctx')
- layer_out: bfloat16 [8, 6144, 1024], P('exp', 'ctx')
The draws below stay inside these ranges and needn't reach their ends.
Inputs may be any that keep to these rules, and one draw needn't show every extreme that they name: `expert_ids`: within one block of 192 tokens of a sequence (the tokens of one device), no expert is named by more than 72 pairs; the 2 ids of a token differ. tile_mask[s, i, i] = 1 for every tile i. `gate_probs`: the 2 weights of a token sum to 1.
All inputs are finite; a program needn't handle non-finite values.
Results may differ from the reference program's by a relative error of at most 0.0065.
Values may be sent and summed in bfloat16 or wider, within the bound.
A program may use at most 128 MiB of HBM per device.

```python
import math
import jax
import jax.numpy as jnp
import numpy as np
from jax import lax

D = 1024
HEADS = 8
KV_HEADS = 2
FF = 1792
EXPERTS = 8
TOP = 2
TILE = 32
TOK_DEV = 192
KVW = 256
SEQS = 8
LEN = 6144
NT = 192
CAP = 72
N_CTX = 32


def paired_keys(key):
    base = jax.random.normal(jax.random.fold_in(key, 11), (SEQS, LEN, KVW), jnp.float32)
    base = jnp.clip(base, -6.0, 6.0)
    return base


def draw_key_proj(key, part):
    return paired_keys(key).astype(jnp.bfloat16)


def draw_queries(key, part):
    base = jax.random.normal(jax.random.fold_in(key, 21), (SEQS, LEN, D), jnp.float32)
    base = jnp.clip(base, -6.0, 6.0)
    return base.astype(jnp.bfloat16)


def draw_tile_mask(key, part):
    density_level = jax.random.randint(jax.random.fold_in(key, 31), (SEQS, NT, 1), 1, 7)
    coin_draw = jax.random.randint(jax.random.fold_in(key, 32), (SEQS, NT, NT), 0, 128)
    tile_index = jnp.arange(NT)
    distance = jnp.abs(tile_index[:, None] - tile_index[None, :])
    on_diagonal = distance == 0
    near_band = distance <= 2
    near_on = near_band[None] & (coin_draw < 16 * density_level)
    far_on = jnp.logical_not(near_band)[None] & (coin_draw < 1)
    return jnp.where(on_diagonal[None] | near_on | far_on, 1, 0).astype(jnp.int32)


def draw_gate_probs(key, part):
    logit_gap = jnp.clip(jax.random.normal(jax.random.fold_in(key, 42), (SEQS, LEN, 1), jnp.float32), -2.9, 2.9)
    first = 1.0 / (1.0 + jnp.exp(-logit_gap))
    return jnp.concatenate([first, 1.0 - first], axis=2)


def block_scale(own_key, extent, shards, least, high):
    def one(axis_at, shards_of):
        draws = jax.random.uniform(jax.random.fold_in(jax.random.fold_in(own_key, 6), axis_at), (shards_of,), jnp.float32, least / len(shards), high / len(shards))
        return jnp.repeat(jnp.exp(draws), extent[axis_at] // shards_of).reshape((-1,) + (1,) * (len(extent) - axis_at - 1))

    factor_of = one(*shards[0])
    for cut in shards[1:]:
        factor_of = factor_of * one(*cut)
    return factor_of


def assign_block(stream_key, own, number, rows, amount, top, bound, lean):
    order = jax.random.permutation(stream_key, amount)
    packed, common = shares(amount, rows * top, bound, lean, True), shares(amount, rows * top, bound, lean, False)
    places = jnp.arange(amount)

    def named(tallies, offset_by):
        used = int((tallies > 0).sum())
        fixed = max(1, used // 4)
        moved = fixed + (places - fixed + offset_by * (used - fixed)) % max(1, amount - fixed)
        return jnp.zeros((amount,), jnp.int32).at[order[jnp.where(places < fixed, places, moved)]].set(jnp.asarray(tallies, jnp.int32))

    tallies = jnp.where(number % 4 == 0, named(packed, number // 4), named(common, number - number // 4 - 1))
    mixed = jax.random.permutation(jax.random.fold_in(own, 3), amount)
    donor, taker = mixed[0:amount // 2 * 2:2], mixed[1:amount // 2 * 2:2]
    slack = jnp.minimum(tallies[donor] - 1, bound - tallies[taker]) // 2
    slack = jnp.where((donor == order[0]) | (taker == order[0]) | (tallies[taker] == 0), 0, jnp.maximum(slack, 0))
    moved = jax.random.randint(jax.random.fold_in(own, 4), (amount // 2,), 0, 1 << 20) % (slack + 1)
    tallies = tallies.at[donor].add(-moved).at[taker].add(moved)
    labels = jnp.searchsorted(jnp.cumsum(tallies), jnp.arange(rows * top), side="right").astype(jnp.int32)
    listing = labels.reshape(top, rows).T
    listing = listing[jax.random.permutation(jax.random.fold_in(own, 1), rows)]
    offset_by = jax.random.randint(jax.random.fold_in(own, 2), (rows, 1), 0, top)
    return jnp.take_along_axis(listing, (jnp.arange(top)[None, :] + offset_by) % top, axis=1)


def shares(amount, total, most, slope, full):
    loads = [(1 << 20) // math.isqrt(rank ** slope) + 1 for rank in range(1, amount + 1)]
    largest = most if full else min(most, max(-(-total // amount), total * loads[0] // sum(loads)))
    least = 1 if total - largest >= amount - 1 else 0
    counts, surplus = [largest] + [least] * (amount - 1), total - largest - least * (amount - 1)
    while surplus > 0:
        free = [i for i in range(1, amount) if counts[i] < largest] or [i for i in range(1, amount) if counts[i] < most]
        mass, remaining = sum([loads[i] for i in free]), surplus
        for i in free:
            extra = min(most - counts[i], max(1, remaining * loads[i] // mass), surplus)
            counts[i] = counts[i] + extra
            surplus = surplus - extra
    return np.array(counts)


def scatter_about(key, extent, spread, reach, split=(), kind=jnp.bfloat16):
    values = jax.random.normal(key, extent, jnp.float32) * spread
    if len(split) > 0:
        values = block_scale(key, extent, split, -0.22, 0.18) * values
    return jnp.clip(values, min=-reach, max=reach).astype(kind)


def setup_inputs(seed: int = 0) -> dict:
    key_of = jax.random.split(jax.random.key(seed), 13)
    hidden_in = scatter_about(key_of[0], (SEQS, LEN, D), 1.0, 6.0, ((0, 8), (1, 32)))
    queries = draw_queries(jax.random.fold_in(key_of[12], 71), 0)
    key_proj = draw_key_proj(jax.random.fold_in(key_of[12], 71), 0)
    value_proj = scatter_about(key_of[3], (SEQS, LEN, KVW), 1.0, 6.0, ((0, 8), (1, 32)))
    tile_mask = draw_tile_mask(jax.random.fold_in(key_of[12], 71), 0)
    out_weight = scatter_about(key_of[5], (D, D), D ** -0.5, 0.1875)
    moe_gain = jnp.clip(1.0 + 0.18 * jax.random.normal(key_of[6], (D,), jnp.float32), 0.1, 1.9)
    gate_weight = scatter_about(key_of[7], (EXPERTS, D, FF), D ** -0.5, 0.1875, ((0, 8), (1, 32)))
    up_weight = scatter_about(key_of[8], (EXPERTS, D, FF), D ** -0.5, 0.1875, ((0, 8), (1, 32)))
    down_weight = scatter_about(key_of[9], (EXPERTS, D, FF), FF ** -0.5, 0.125, ((0, 8), (1, 32)))
    expert_ids_keys = jax.random.split(jax.random.fold_in(key_of[10], 1), SEQS * LEN // TOK_DEV)
    expert_ids_turns = jax.random.permutation(jax.random.fold_in(key_of[10], 3), SEQS * LEN // TOK_DEV)
    expert_ids = jax.vmap(lambda own, number: assign_block(jax.random.fold_in(key_of[10], 2), own, number, TOK_DEV, EXPERTS, TOP, CAP, 2))(expert_ids_keys, expert_ids_turns).reshape((SEQS, LEN, TOP))
    gate_probs = draw_gate_probs(jax.random.fold_in(key_of[12], 71), 0)
    return dict(hidden_in=hidden_in, queries=queries, key_proj=key_proj, value_proj=value_proj, tile_mask=tile_mask, out_weight=out_weight, moe_gain=moe_gain, gate_weight=gate_weight, up_weight=up_weight, down_weight=down_weight, expert_ids=expert_ids, gate_probs=gate_probs)


def rms_scale(row_block, gain):
    widened = row_block.astype(jnp.float32)
    inverse = lax.rsqrt(lax.optimization_barrier(jnp.mean(widened * widened, axis=-1, keepdims=True)) + 1e-05)
    return widened * inverse * gain.astype(jnp.float32)

def attend_block(query_rows, key_rows, value_rows, mask_rows):
    row_count = query_rows.shape[0]
    groups = HEADS // KV_HEADS
    head_size = D // HEADS
    query_heads = query_rows.reshape(row_count, KV_HEADS, groups, head_size).astype(jnp.float32)
    key_heads = key_rows.reshape(-1, KV_HEADS, head_size).astype(jnp.float32)
    value_heads = value_rows.reshape(-1, KV_HEADS, head_size).astype(jnp.float32)
    scores = jnp.einsum('qkgd,rkd->kgqr', query_heads, key_heads) * head_size ** (-0.5)
    allowed = jnp.repeat(jnp.repeat(mask_rows, TILE, axis=0), TILE, axis=1) > 0
    scores = jnp.where(allowed, scores, -1e+30)
    highest = lax.optimization_barrier(jnp.max(scores, axis=-1, keepdims=True))
    weights = jnp.where(allowed, jnp.exp(scores - highest), 0.0)
    denominator = lax.optimization_barrier(jnp.sum(weights, axis=-1, keepdims=True))
    rounded = lax.optimization_barrier(weights.astype(jnp.bfloat16))
    attended = jnp.einsum('kgqr,rkd->kgqd', rounded.astype(jnp.float32), value_heads) / denominator
    return attended.transpose(2, 0, 1, 3).reshape(row_count, D).astype(jnp.bfloat16)

def slot_rank(id_row):
    onehot = (id_row[:, None] == jnp.arange(EXPERTS, dtype=jnp.int32)[None, :]).astype(jnp.int32)
    before = jnp.cumsum(onehot, axis=0) - onehot
    return lax.optimization_barrier(jnp.sum(before * onehot, axis=1)).astype(jnp.int32)

def fill_slots(row_block, id_row, slot_row):
    repeated = jnp.repeat(row_block, TOP, axis=0)
    return jnp.zeros((EXPERTS, CAP, D), jnp.bfloat16).at[id_row, slot_row].set(repeated)

def run_expert(bundle):
    slot_rows, gate_w, up_w, down_w = bundle
    gated = jnp.dot(slot_rows, gate_w, preferred_element_type=jnp.float32)
    up_values = jnp.dot(slot_rows, up_w, preferred_element_type=jnp.float32)
    hidden = (jax.nn.silu(gated) * up_values).astype(jnp.bfloat16)
    return jnp.dot(hidden, down_w.T, preferred_element_type=jnp.float32).astype(jnp.bfloat16)

def reference(hidden_in, queries, key_proj, value_proj, tile_mask, out_weight, moe_gain, gate_weight, up_weight, down_weight, expert_ids, gate_probs):

    def one_sequence(bundle):
        query_seq, key_seq, value_seq, mask_seq = bundle
        query_blocks = query_seq.reshape(N_CTX, TOK_DEV, D)
        mask_blocks = mask_seq.reshape(N_CTX, TOK_DEV // TILE, NT)

        def one_block(couple):
            return attend_block(couple[0], key_seq, value_seq, couple[1])
        return lax.map(one_block, (query_blocks, mask_blocks)).reshape(LEN, D)
    attended = lax.map(one_sequence, (queries, key_proj, value_proj, tile_mask))
    projected = jnp.dot(attended.reshape(-1, D), out_weight, preferred_element_type=jnp.float32)
    attention_out = projected.astype(jnp.bfloat16).reshape(SEQS, LEN, D)
    residual = (hidden_in.reshape(-1, D).astype(jnp.float32) + projected).astype(jnp.bfloat16)
    normed = rms_scale(residual, moe_gain).astype(jnp.bfloat16)
    block_count = SEQS * N_CTX
    row_blocks = normed.reshape(block_count, TOK_DEV, D)
    id_rows = expert_ids.reshape(block_count, TOK_DEV * TOP).astype(jnp.int32)
    slot_rows = jax.vmap(slot_rank)(id_rows)
    buffers = jax.vmap(fill_slots)(row_blocks, id_rows, slot_rows)
    per_expert = jnp.moveaxis(buffers, 1, 0).reshape(EXPERTS, block_count * CAP, D)
    outputs = lax.map(run_expert, (per_expert, gate_weight, up_weight, down_weight))
    outputs = jnp.moveaxis(outputs.reshape(EXPERTS, block_count, CAP, D), 0, 1).reshape(block_count, EXPERTS * CAP, D)

    def pick_rows(output_block, id_row, slot_row):
        return jnp.take(output_block, id_row * CAP + slot_row, axis=0)
    picked = jax.vmap(pick_rows)(outputs, id_rows, slot_rows).reshape(block_count, TOK_DEV, TOP, D)
    probs = gate_probs.reshape(block_count, TOK_DEV, TOP).astype(jnp.float32)
    mixture = lax.optimization_barrier(jnp.sum(picked.astype(jnp.float32) * probs[..., None], axis=2))
    layer_out = (residual.reshape(block_count, TOK_DEV, D).astype(jnp.float32) + mixture).astype(jnp.bfloat16)
    return (attention_out, layer_out.reshape(SEQS, LEN, D))
```

```python
import jax
import jax.numpy as jnp
from jax import lax
from jax.sharding import PartitionSpec as P

D = 1024
HEADS = 8
KV_HEADS = 2
EXPERTS = 8
TOP = 2
TILE = 32
CAP = 72


def rms_scale(row_block, gain):
    widened = row_block.astype(jnp.float32)
    inverse = lax.rsqrt(jnp.mean(widened * widened, axis=-1, keepdims=True) + 1e-05)
    return widened * inverse * gain


def shards(
    hidden_in,
    queries,
    key_proj,
    value_proj,
    tile_mask,
    out_weight,
    moe_gain,
    gate_weight,
    up_weight,
    down_weight,
    expert_ids,
    gate_probs,
):
    query_rows = queries[0]
    row_count = query_rows.shape[0]
    groups = HEADS // KV_HEADS
    head_size = D // HEADS
    query_heads = query_rows.reshape(row_count, KV_HEADS, groups, head_size)
    mask_block = tile_mask[0]
    kv_width = key_proj.shape[-1]
    kv_piece = lax.all_gather(
        jnp.concatenate([key_proj[0], value_proj[0]], axis=-1), "ctx", axis=0, tiled=True
    )
    key_piece = kv_piece[:, :kv_width]
    value_piece = kv_piece[:, kv_width:]
    piece_rows = key_piece.shape[0]
    running_max = jnp.full((KV_HEADS, groups, row_count, 1), -1e30, jnp.float32)
    allowed = jnp.repeat(jnp.repeat(mask_block, TILE, axis=0), TILE, axis=1) > 0
    key_heads = key_piece.reshape(piece_rows, KV_HEADS, head_size)
    value_heads = value_piece.reshape(piece_rows, KV_HEADS, head_size)
    scores = jnp.einsum(
        "qkgd,rkd->kgqr", query_heads, key_heads, preferred_element_type=jnp.float32
    ) * head_size ** (-0.5)
    scores = jnp.where(allowed, scores, -1e30)
    newest_max = jnp.maximum(running_max, jnp.max(scores, axis=-1, keepdims=True))
    weights = jnp.where(allowed, jnp.exp(scores - newest_max), 0.0)
    denominator = jnp.sum(weights, axis=-1, keepdims=True)
    accumulated = jnp.einsum(
        "kgqr,rkd->kgqd",
        weights.astype(jnp.bfloat16),
        value_heads,
        preferred_element_type=jnp.float32,
    )
    running_max, denominator, accumulated = (newest_max, denominator, accumulated)
    attended = (
        (accumulated / denominator).transpose(2, 0, 1, 3).reshape(row_count, D).astype(jnp.bfloat16)
    )
    projected = jnp.dot(attended, out_weight, preferred_element_type=jnp.float32)
    attention_out = projected.astype(jnp.bfloat16)
    residual = (hidden_in[0].astype(jnp.float32) + projected).astype(jnp.bfloat16)
    normed = rms_scale(residual, moe_gain).astype(jnp.bfloat16)
    id_row = expert_ids[0].reshape(-1)
    onehot = (id_row[:, None] == jnp.arange(EXPERTS, dtype=jnp.int32)[None, :]).astype(jnp.int32)
    before = jnp.cumsum(onehot, axis=0) - onehot
    slot_index = jnp.sum(before * onehot, axis=1)
    target = id_row * CAP + slot_index
    selector = (jnp.arange(EXPERTS * CAP, dtype=jnp.int32)[:, None] == target[None, :]).astype(
        jnp.bfloat16
    )
    repeated = jnp.repeat(normed, TOP, axis=0)
    outgoing = (
        jnp.dot(selector, repeated, preferred_element_type=jnp.float32)
        .astype(jnp.bfloat16)
        .reshape(EXPERTS, CAP, D)
    )
    arrived = lax.all_to_all(outgoing, "exp", split_axis=0, concat_axis=1, tiled=True)
    ff = gate_weight.shape[-1]
    weight_piece = lax.all_gather(
        jnp.concatenate([gate_weight, up_weight, down_weight], axis=-1), "ctx", axis=1, tiled=True
    )
    gate_piece = weight_piece[..., :ff]
    up_piece = weight_piece[..., ff : 2 * ff]
    down_piece = weight_piece[..., 2 * ff :]
    gate_sum = jnp.einsum("esd,edf->esf", arrived, gate_piece, preferred_element_type=jnp.float32)
    up_sum = jnp.einsum("esd,edf->esf", arrived, up_piece, preferred_element_type=jnp.float32)
    hidden = (jax.nn.silu(gate_sum) * up_sum).astype(jnp.bfloat16)
    expert_rows = jnp.einsum(
        "esf,edf->esd",
        hidden,
        down_piece,
        preferred_element_type=jnp.float32,
    ).astype(jnp.bfloat16)
    returned = lax.all_to_all(expert_rows, "exp", split_axis=1, concat_axis=0, tiled=True)
    picked = jnp.take(returned.reshape(EXPERTS * CAP, D), target, axis=0).reshape(row_count, TOP, D)
    mixture = jnp.sum(picked.astype(jnp.float32) * gate_probs[0][:, :, None], axis=1)
    layer_out = (residual.astype(jnp.float32) + mixture).astype(jnp.bfloat16)
    return (attention_out[None], layer_out[None])


def solution(mesh):
    return jax.shard_map(
        shards,
        mesh=mesh,
        in_specs=(
            P("exp", "ctx", None),
            P("exp", "ctx", None),
            P("exp", "ctx", None),
            P("exp", "ctx", None),
            P("exp", "ctx", None),
            P(),
            P(),
            P("exp", "ctx", None),
            P("exp", "ctx", None),
            P("exp", "ctx", None),
            P("exp", "ctx", None),
            P("exp", "ctx", None),
        ),
        out_specs=(P("exp", "ctx", None), P("exp", "ctx", None)),
        check_vma=False,
    )
```

```python
import jax
import jax.numpy as jnp
from jax import lax
from jax.sharding import PartitionSpec as P

D = 1024
HEADS = 8
KV_HEADS = 2
EXPERTS = 8
TOP = 2
TILE = 32
CAP = 72


def rms_scale(row_block, gain):
    widened = row_block.astype(jnp.float32)
    inverse = lax.rsqrt(jnp.mean(widened * widened, axis=-1, keepdims=True) + 1e-05)
    return widened * inverse * gain


CTX_AXES = ("z", "yh", "core")


def gather_ctx(block, axis):
    for name in reversed(CTX_AXES):
        block = lax.all_gather(block, name, axis=axis, tiled=True)
    return block


def shards(
    hidden_in,
    queries,
    key_proj,
    value_proj,
    tile_mask,
    out_weight,
    moe_gain,
    gate_weight,
    up_weight,
    down_weight,
    expert_ids,
    gate_probs,
):
    query_rows = queries[0]
    row_count = query_rows.shape[0]
    groups = HEADS // KV_HEADS
    head_size = D // HEADS
    query_heads = query_rows.reshape(row_count, KV_HEADS, groups, head_size)
    mask_block = tile_mask[0]
    kv_width = key_proj.shape[-1]
    kv_piece = gather_ctx(jnp.concatenate([key_proj[0], value_proj[0]], axis=-1), 0)
    key_piece = kv_piece[:, :kv_width]
    value_piece = kv_piece[:, kv_width:]
    piece_rows = key_piece.shape[0]
    running_max = jnp.full((KV_HEADS, groups, row_count, 1), -1e30, jnp.float32)
    allowed = jnp.repeat(jnp.repeat(mask_block, TILE, axis=0), TILE, axis=1) > 0
    key_heads = key_piece.reshape(piece_rows, KV_HEADS, head_size)
    value_heads = value_piece.reshape(piece_rows, KV_HEADS, head_size)
    scores = jnp.einsum(
        "qkgd,rkd->kgqr", query_heads, key_heads, preferred_element_type=jnp.float32
    ) * head_size ** (-0.5)
    scores = jnp.where(allowed, scores, -1e30)
    newest_max = jnp.maximum(running_max, jnp.max(scores, axis=-1, keepdims=True))
    weights = jnp.where(allowed, jnp.exp(scores - newest_max), 0.0)
    denominator = jnp.sum(weights, axis=-1, keepdims=True)
    accumulated = jnp.einsum(
        "kgqr,rkd->kgqd",
        weights.astype(jnp.bfloat16),
        value_heads,
        preferred_element_type=jnp.float32,
    )
    running_max, denominator, accumulated = (newest_max, denominator, accumulated)
    attended = (
        (accumulated / denominator).transpose(2, 0, 1, 3).reshape(row_count, D).astype(jnp.bfloat16)
    )
    projected = jnp.dot(attended, out_weight, preferred_element_type=jnp.float32)
    attention_out = projected.astype(jnp.bfloat16)
    residual = (hidden_in[0].astype(jnp.float32) + projected).astype(jnp.bfloat16)
    normed = rms_scale(residual, moe_gain).astype(jnp.bfloat16)
    id_row = expert_ids[0].reshape(-1)
    onehot = (id_row[:, None] == jnp.arange(EXPERTS, dtype=jnp.int32)[None, :]).astype(jnp.int32)
    before = jnp.cumsum(onehot, axis=0) - onehot
    slot_index = jnp.sum(before * onehot, axis=1)
    target = id_row * CAP + slot_index
    selector = (jnp.arange(EXPERTS * CAP, dtype=jnp.int32)[:, None] == target[None, :]).astype(
        jnp.bfloat16
    )
    repeated = jnp.repeat(normed, TOP, axis=0)
    outgoing = (
        jnp.dot(selector, repeated, preferred_element_type=jnp.float32)
        .astype(jnp.bfloat16)
        .reshape(EXPERTS, CAP, D)
    )
    arrived = lax.all_to_all(outgoing, "exp", split_axis=0, concat_axis=1, tiled=True)
    ff = gate_weight.shape[-1]
    weight_piece = gather_ctx(jnp.concatenate([gate_weight, up_weight, down_weight], axis=-1), 1)
    gate_piece = weight_piece[..., :ff]
    up_piece = weight_piece[..., ff : 2 * ff]
    down_piece = weight_piece[..., 2 * ff :]
    gate_sum = jnp.einsum("esd,edf->esf", arrived, gate_piece, preferred_element_type=jnp.float32)
    up_sum = jnp.einsum("esd,edf->esf", arrived, up_piece, preferred_element_type=jnp.float32)
    hidden = (jax.nn.silu(gate_sum) * up_sum).astype(jnp.bfloat16)
    expert_rows = jnp.einsum(
        "esf,edf->esd",
        hidden,
        down_piece,
        preferred_element_type=jnp.float32,
    ).astype(jnp.bfloat16)
    returned = lax.all_to_all(expert_rows, "exp", split_axis=1, concat_axis=0, tiled=True)
    picked = jnp.take(returned.reshape(EXPERTS * CAP, D), target, axis=0).reshape(row_count, TOP, D)
    mixture = jnp.sum(picked.astype(jnp.float32) * gate_probs[0][:, :, None], axis=1)
    layer_out = (residual.astype(jnp.float32) + mixture).astype(jnp.bfloat16)
    return (attention_out[None], layer_out[None])


def solution(mesh):
    n_ctx = mesh.shape["ctx"]
    split = jax.sharding.Mesh(
        mesh.devices.reshape(n_ctx // 4, 2, 2, mesh.shape["exp"]), CTX_AXES + ("exp",)
    )
    return jax.shard_map(
        shards,
        mesh=split,
        in_specs=(
            P("exp", CTX_AXES, None),
            P("exp", CTX_AXES, None),
            P("exp", CTX_AXES, None),
            P("exp", CTX_AXES, None),
            P("exp", CTX_AXES, None),
            P(),
            P(),
            P("exp", CTX_AXES, None),
            P("exp", CTX_AXES, None),
            P("exp", CTX_AXES, None),
            P("exp", CTX_AXES, None),
            P("exp", CTX_AXES, None),
        ),
        out_specs=(P("exp", CTX_AXES, None), P("exp", CTX_AXES, None)),
        check_vma=False,
    )
```

```python
import functools

import jax
import jax.numpy as jnp
from jax import lax
from jax.experimental import pallas as pl
from jax.experimental.pallas import tpu as pltpu
from jax.sharding import PartitionSpec as P

D = 1024
HEADS = 8
KV_HEADS = 2
EXPERTS = 8
TOP = 2
TILE = 32
CAP = 72


def rms_scale(row_block, gain):
    widened = row_block.astype(jnp.float32)
    inverse = lax.rsqrt(jnp.mean(widened * widened, axis=-1, keepdims=True) + 1e-05)
    return widened * inverse * gain


CTX_AXES = ("z", "yh", "core")


MESH = pl.DeviceIdType.MESH


def gather_kernel(n_z, shard_ref, out_ref, local_sem, send_sem, recv_sem):
    z = lax.axis_index("z")
    yh = lax.axis_index("yh")
    core = lax.axis_index("core")
    ex = lax.axis_index("exp")

    def slot(zz, hh, cc):
        return (zz * 2 + hh) * 2 + cc

    def ring(offset):
        return lax.rem(z + offset + 4 * n_z, n_z)

    partner_h = 1 - yh
    sibling_c = 1 - core
    to_right = (ring(1), yh, core, ex)
    to_left = (ring(-1), yh, core, ex)
    to_partner = (z, partner_h, core, ex)
    to_sibling = (z, yh, sibling_c, ex)
    barrier = pltpu.get_barrier_semaphore()
    for dev in (to_right, to_left, to_partner, to_sibling):
        pl.semaphore_signal(barrier, 1, device_id=dev, device_id_type=MESH)
    pl.semaphore_wait(barrier, 4)

    me = slot(z, yh, core)
    own = pltpu.make_async_copy(shard_ref, out_ref.at[me], local_sem)
    own.start()
    sends = []

    def send(src, s, dev, k):
        copy = pltpu.make_async_remote_copy(
            src, out_ref.at[s], send_sem.at[k, s], recv_sem.at[s], device_id=dev, device_id_type=MESH
        )
        copy.start()
        sends.append(copy)

    def arrive(s):
        pltpu.make_async_remote_copy(
            out_ref.at[s], out_ref.at[s], send_sem.at[0, s], recv_sem.at[s],
            device_id=to_right, device_id_type=MESH,
        ).wait_recv()

    for k, dev in enumerate((to_right, to_left, to_partner, to_sibling)):
        send(shard_ref, me, dev, k)
    half = n_z // 2
    for t in range(1, half + 1):
        s = slot(ring(-t), yh, core)
        arrive(s)
        if t < half:
            send(out_ref.at[s], s, to_right, 0)
        send(out_ref.at[s], s, to_partner, 2)
        send(out_ref.at[s], s, to_sibling, 3)
        if t < n_z - half:
            s = slot(ring(t), yh, core)
            arrive(s)
            if t < n_z - half - 1:
                send(out_ref.at[s], s, to_left, 1)
            send(out_ref.at[s], s, to_partner, 2)
            send(out_ref.at[s], s, to_sibling, 3)
    partner_order = [0]
    for t in range(1, half + 1):
        partner_order.append(-t)
        if t < n_z - half:
            partner_order.append(t)
    for offset in partner_order:
        s = slot(ring(offset), partner_h, core)
        arrive(s)
        send(out_ref.at[s], s, to_sibling, 3)
    for hh in (yh, partner_h):
        for offset in partner_order:
            arrive(slot(ring(offset), hh, sibling_c))
    own.wait()
    for copy in sends:
        copy.wait_send()


def gather_ctx_kernel(block):
    n_z = lax.axis_size("z")
    n_all = n_z * 4
    return pl.pallas_call(
        functools.partial(gather_kernel, n_z),
        out_shape=jax.ShapeDtypeStruct((n_all,) + block.shape, block.dtype),
        in_specs=[pl.BlockSpec(memory_space=pl.ANY)],
        out_specs=pl.BlockSpec(memory_space=pl.ANY),
        scratch_shapes=[
            pltpu.SemaphoreType.DMA(()),
            pltpu.SemaphoreType.DMA((4, n_all)),
            pltpu.SemaphoreType.DMA((n_all,)),
        ],
        compiler_params=pltpu.CompilerParams(collective_id=0, has_side_effects=True),
    )(block)


def shards(
    hidden_in,
    queries,
    key_proj,
    value_proj,
    tile_mask,
    out_weight,
    moe_gain,
    gate_weight,
    up_weight,
    down_weight,
    expert_ids,
    gate_probs,
):
    query_rows = queries[0]
    row_count = query_rows.shape[0]
    groups = HEADS // KV_HEADS
    head_size = D // HEADS
    query_heads = query_rows.reshape(row_count, KV_HEADS, groups, head_size)
    mask_block = tile_mask[0]
    kv_width = key_proj.shape[-1]
    kv_local = jnp.concatenate([key_proj[0], value_proj[0]], axis=-1)
    kv_piece = gather_ctx_kernel(kv_local).reshape(-1, 2 * kv_width)
    key_piece = kv_piece[:, :kv_width]
    value_piece = kv_piece[:, kv_width:]
    piece_rows = key_piece.shape[0]
    running_max = jnp.full((KV_HEADS, groups, row_count, 1), -1e30, jnp.float32)
    allowed = jnp.repeat(jnp.repeat(mask_block, TILE, axis=0), TILE, axis=1) > 0
    key_heads = key_piece.reshape(piece_rows, KV_HEADS, head_size)
    value_heads = value_piece.reshape(piece_rows, KV_HEADS, head_size)
    scores = jnp.einsum(
        "qkgd,rkd->kgqr", query_heads, key_heads, preferred_element_type=jnp.float32
    ) * head_size ** (-0.5)
    scores = jnp.where(allowed, scores, -1e30)
    newest_max = jnp.maximum(running_max, jnp.max(scores, axis=-1, keepdims=True))
    weights = jnp.where(allowed, jnp.exp(scores - newest_max), 0.0)
    denominator = jnp.sum(weights, axis=-1, keepdims=True)
    accumulated = jnp.einsum(
        "kgqr,rkd->kgqd",
        weights.astype(jnp.bfloat16),
        value_heads,
        preferred_element_type=jnp.float32,
    )
    running_max, denominator, accumulated = (newest_max, denominator, accumulated)
    attended = (
        (accumulated / denominator).transpose(2, 0, 1, 3).reshape(row_count, D).astype(jnp.bfloat16)
    )
    projected = jnp.dot(attended, out_weight, preferred_element_type=jnp.float32)
    attention_out = projected.astype(jnp.bfloat16)
    residual = (hidden_in[0].astype(jnp.float32) + projected).astype(jnp.bfloat16)
    normed = rms_scale(residual, moe_gain).astype(jnp.bfloat16)
    id_row = expert_ids[0].reshape(-1)
    onehot = (id_row[:, None] == jnp.arange(EXPERTS, dtype=jnp.int32)[None, :]).astype(jnp.int32)
    before = jnp.cumsum(onehot, axis=0) - onehot
    slot_index = jnp.sum(before * onehot, axis=1)
    target = id_row * CAP + slot_index
    selector = (jnp.arange(EXPERTS * CAP, dtype=jnp.int32)[:, None] == target[None, :]).astype(
        jnp.bfloat16
    )
    repeated = jnp.repeat(normed, TOP, axis=0)
    outgoing = (
        jnp.dot(selector, repeated, preferred_element_type=jnp.float32)
        .astype(jnp.bfloat16)
        .reshape(EXPERTS, CAP, D)
    )
    arrived = lax.all_to_all(outgoing, "exp", split_axis=0, concat_axis=1, tiled=True)
    ff = gate_weight.shape[-1]
    weight_piece = lax.all_gather(
        jnp.concatenate([gate_weight, up_weight, down_weight], axis=-1), CTX_AXES, axis=1, tiled=True
    )
    gate_piece = weight_piece[..., :ff]
    up_piece = weight_piece[..., ff : 2 * ff]
    down_piece = weight_piece[..., 2 * ff :]
    gate_sum = jnp.einsum("esd,edf->esf", arrived, gate_piece, preferred_element_type=jnp.float32)
    up_sum = jnp.einsum("esd,edf->esf", arrived, up_piece, preferred_element_type=jnp.float32)
    hidden = (jax.nn.silu(gate_sum) * up_sum).astype(jnp.bfloat16)
    expert_rows = jnp.einsum(
        "esf,edf->esd",
        hidden,
        down_piece,
        preferred_element_type=jnp.float32,
    ).astype(jnp.bfloat16)
    returned = lax.all_to_all(expert_rows, "exp", split_axis=1, concat_axis=0, tiled=True)
    picked = jnp.take(returned.reshape(EXPERTS * CAP, D), target, axis=0).reshape(row_count, TOP, D)
    mixture = jnp.sum(picked.astype(jnp.float32) * gate_probs[0][:, :, None], axis=1)
    layer_out = (residual.astype(jnp.float32) + mixture).astype(jnp.bfloat16)
    return (attention_out[None], layer_out[None])


def solution(mesh):
    n_ctx = mesh.shape["ctx"]
    split = jax.sharding.Mesh(
        mesh.devices.reshape(n_ctx // 4, 2, 2, mesh.shape["exp"]), CTX_AXES + ("exp",)
    )
    return jax.shard_map(
        shards,
        mesh=split,
        in_specs=(
            P("exp", CTX_AXES, None),
            P("exp", CTX_AXES, None),
            P("exp", CTX_AXES, None),
            P("exp", CTX_AXES, None),
            P("exp", CTX_AXES, None),
            P(),
            P(),
            P("exp", CTX_AXES, None),
            P("exp", CTX_AXES, None),
            P("exp", CTX_AXES, None),
            P("exp", CTX_AXES, None),
            P("exp", CTX_AXES, None),
        ),
        out_specs=(P("exp", CTX_AXES, None), P("exp", CTX_AXES, None)),
        check_vma=False,
    )
```

```python
import functools

import jax
import jax.numpy as jnp
from jax import lax
from jax.experimental import pallas as pl
from jax.experimental.pallas import tpu as pltpu
from jax.sharding import PartitionSpec as P

D = 1024
HEADS = 8
KV_HEADS = 2
EXPERTS = 8
TOP = 2
TILE = 32
CAP = 72


def rms_scale(row_block, gain):
    widened = row_block.astype(jnp.float32)
    inverse = lax.rsqrt(jnp.mean(widened * widened, axis=-1, keepdims=True) + 1e-05)
    return widened * inverse * gain


CTX_AXES = ("z", "yh", "core")


MESH = pl.DeviceIdType.MESH


def gather_kernel(n_z, shard_ref, out_ref, local_sem, send_sem, recv_sem):
    z = lax.axis_index("z")
    yh = lax.axis_index("yh")
    core = lax.axis_index("core")
    ex = lax.axis_index("exp")

    def slot(zz, hh, cc):
        return (zz * 2 + hh) * 2 + cc

    def ring(offset):
        return lax.rem(z + offset + 4 * n_z, n_z)

    partner_h = 1 - yh
    sibling_c = 1 - core
    to_right = (ring(1), yh, core, ex)
    to_left = (ring(-1), yh, core, ex)
    to_partner = (z, partner_h, core, ex)
    to_sibling = (z, yh, sibling_c, ex)
    barrier = pltpu.get_barrier_semaphore()
    for dev in (to_right, to_left, to_partner, to_sibling):
        pl.semaphore_signal(barrier, 1, device_id=dev, device_id_type=MESH)
    pl.semaphore_wait(barrier, 4)

    me = slot(z, yh, core)
    own = pltpu.make_async_copy(shard_ref, out_ref.at[me], local_sem)
    own.start()
    sends = []

    def send(src, s, dev, k):
        copy = pltpu.make_async_remote_copy(
            src, out_ref.at[s], send_sem.at[k, s], recv_sem.at[s], device_id=dev, device_id_type=MESH
        )
        copy.start()
        sends.append(copy)

    def arrive(s):
        pltpu.make_async_remote_copy(
            out_ref.at[s], out_ref.at[s], send_sem.at[0, s], recv_sem.at[s],
            device_id=to_right, device_id_type=MESH,
        ).wait_recv()

    for k, dev in enumerate((to_right, to_left, to_partner, to_sibling)):
        send(shard_ref, me, dev, k)
    half = n_z // 2
    for t in range(1, half + 1):
        s = slot(ring(-t), yh, core)
        arrive(s)
        if t < half:
            send(out_ref.at[s], s, to_right, 0)
        send(out_ref.at[s], s, to_partner, 2)
        send(out_ref.at[s], s, to_sibling, 3)
        if t < n_z - half:
            s = slot(ring(t), yh, core)
            arrive(s)
            if t < n_z - half - 1:
                send(out_ref.at[s], s, to_left, 1)
            send(out_ref.at[s], s, to_partner, 2)
            send(out_ref.at[s], s, to_sibling, 3)
    partner_order = [0]
    for t in range(1, half + 1):
        partner_order.append(-t)
        if t < n_z - half:
            partner_order.append(t)
    for offset in partner_order:
        s = slot(ring(offset), partner_h, core)
        arrive(s)
        send(out_ref.at[s], s, to_sibling, 3)
    for hh in (yh, partner_h):
        for offset in partner_order:
            arrive(slot(ring(offset), hh, sibling_c))
    own.wait()
    for copy in sends:
        copy.wait_send()


def gather_ctx_kernel(block):
    n_z = lax.axis_size("z")
    n_all = n_z * 4
    return pl.pallas_call(
        functools.partial(gather_kernel, n_z),
        out_shape=jax.ShapeDtypeStruct((n_all,) + block.shape, block.dtype),
        in_specs=[pl.BlockSpec(memory_space=pl.ANY)],
        out_specs=pl.BlockSpec(memory_space=pl.ANY),
        scratch_shapes=[
            pltpu.SemaphoreType.DMA(()),
            pltpu.SemaphoreType.DMA((4, n_all)),
            pltpu.SemaphoreType.DMA((n_all,)),
        ],
        compiler_params=pltpu.CompilerParams(collective_id=0, has_side_effects=True),
    )(block)


KEY_BLOCK = 128


def attention_kernel(groups, head_size, flag_ref, q_ref, kv_ref, mask_ref, out_ref, top_ref, sum_ref, acc_ref):
    n_blocks = flag_ref.shape[0]
    kv_heads = kv_ref.shape[1] // (2 * head_size)
    heads = kv_heads * groups
    value_at = kv_heads * head_size
    scale = head_size ** (-0.5)
    top_ref[...] = jnp.full(top_ref.shape, -1e30, jnp.float32)
    sum_ref[...] = jnp.zeros(sum_ref.shape, jnp.float32)
    acc_ref[...] = jnp.zeros(acc_ref.shape, jnp.float32)

    def scores(j, h):
        rows = pl.ds(pl.multiple_of(j * KEY_BLOCK, KEY_BLOCK), KEY_BLOCK)
        key = kv_ref[rows, pl.ds((h // groups) * head_size, head_size)]
        query = q_ref[:, pl.ds(h * head_size, head_size)]
        raw = lax.dot_general(
            query, key, (((1,), (1,)), ((), ())), preferred_element_type=jnp.float32
        )
        return raw * scale, mask_ref[:, rows] > 0

    def first_pass(j, carry):
        @pl.when(flag_ref[j] > 0)
        def _():
            for h in range(heads):
                s, allowed = scores(j, h)
                top_ref[h] = jnp.maximum(top_ref[h], jnp.where(allowed, s, -1e30))
        return carry

    lax.fori_loop(0, n_blocks, first_pass, 0)
    for h in range(heads):
        top_ref[h] = jnp.broadcast_to(jnp.max(top_ref[h], axis=1, keepdims=True), top_ref.shape[1:])

    def second_pass(j, carry):
        @pl.when(flag_ref[j] > 0)
        def _():
            rows = pl.ds(pl.multiple_of(j * KEY_BLOCK, KEY_BLOCK), KEY_BLOCK)
            for h in range(heads):
                s, allowed = scores(j, h)
                weights = jnp.where(allowed, jnp.exp(s - top_ref[h]), 0.0)
                sum_ref[h] += weights
                value = kv_ref[rows, pl.ds(value_at + (h // groups) * head_size, head_size)]
                acc_ref[h] += jnp.dot(
                    weights.astype(jnp.bfloat16), value, preferred_element_type=jnp.float32
                )
        return carry

    lax.fori_loop(0, n_blocks, second_pass, 0)
    for h in range(heads):
        denominator = jnp.sum(sum_ref[h], axis=1, keepdims=True)
        out_ref[:, pl.ds(h * head_size, head_size)] = (acc_ref[h] / denominator).astype(out_ref.dtype)


def block_attention(query_rows, kv_rows, mask_block, groups, head_size):
    row_count = query_rows.shape[0]
    key_count = kv_rows.shape[0]
    heads = query_rows.shape[1] // head_size
    allowed = jnp.repeat(jnp.repeat(mask_block, TILE, axis=0), TILE, axis=1).astype(jnp.bfloat16)
    tiles_per_block = KEY_BLOCK // TILE
    flags = jnp.max(
        mask_block.reshape(mask_block.shape[0], -1, tiles_per_block), axis=(0, 2)
    ).astype(jnp.int32)
    vmem = pl.BlockSpec(memory_space=pltpu.VMEM)
    return pl.pallas_call(
        functools.partial(attention_kernel, groups, head_size),
        out_shape=jax.ShapeDtypeStruct((row_count, heads * head_size), jnp.bfloat16),
        in_specs=[pl.BlockSpec(memory_space=pltpu.SMEM), vmem, vmem, vmem],
        out_specs=vmem,
        scratch_shapes=[
            pltpu.VMEM((heads, row_count, KEY_BLOCK), jnp.float32),
            pltpu.VMEM((heads, row_count, KEY_BLOCK), jnp.float32),
            pltpu.VMEM((heads, row_count, head_size), jnp.float32),
        ],
    )(flags, query_rows, kv_rows, allowed)


def shards(
    hidden_in,
    queries,
    key_proj,
    value_proj,
    tile_mask,
    out_weight,
    moe_gain,
    gate_weight,
    up_weight,
    down_weight,
    expert_ids,
    gate_probs,
):
    query_rows = queries[0]
    row_count = query_rows.shape[0]
    groups = HEADS // KV_HEADS
    head_size = D // HEADS
    query_heads = query_rows.reshape(row_count, KV_HEADS, groups, head_size)
    mask_block = tile_mask[0]
    kv_width = key_proj.shape[-1]
    kv_local = jnp.concatenate([key_proj[0], value_proj[0]], axis=-1)
    kv_piece = gather_ctx_kernel(kv_local).reshape(-1, 2 * kv_width)
    attended = block_attention(query_rows, kv_piece, mask_block, groups, head_size)
    projected = jnp.dot(attended, out_weight, preferred_element_type=jnp.float32)
    attention_out = projected.astype(jnp.bfloat16)
    residual = (hidden_in[0].astype(jnp.float32) + projected).astype(jnp.bfloat16)
    normed = rms_scale(residual, moe_gain).astype(jnp.bfloat16)
    id_row = expert_ids[0].reshape(-1)
    onehot = (id_row[:, None] == jnp.arange(EXPERTS, dtype=jnp.int32)[None, :]).astype(jnp.int32)
    before = jnp.cumsum(onehot, axis=0) - onehot
    slot_index = jnp.sum(before * onehot, axis=1)
    target = id_row * CAP + slot_index
    selector = (jnp.arange(EXPERTS * CAP, dtype=jnp.int32)[:, None] == target[None, :]).astype(
        jnp.bfloat16
    )
    repeated = jnp.repeat(normed, TOP, axis=0)
    outgoing = (
        jnp.dot(selector, repeated, preferred_element_type=jnp.float32)
        .astype(jnp.bfloat16)
        .reshape(EXPERTS, CAP, D)
    )
    arrived = lax.all_to_all(outgoing, "exp", split_axis=0, concat_axis=1, tiled=True)
    ff = gate_weight.shape[-1]
    weight_piece = lax.all_gather(
        jnp.concatenate([gate_weight, up_weight, down_weight], axis=-1), CTX_AXES, axis=1, tiled=True
    )
    gate_piece = weight_piece[..., :ff]
    up_piece = weight_piece[..., ff : 2 * ff]
    down_piece = weight_piece[..., 2 * ff :]
    gate_sum = jnp.einsum("esd,edf->esf", arrived, gate_piece, preferred_element_type=jnp.float32)
    up_sum = jnp.einsum("esd,edf->esf", arrived, up_piece, preferred_element_type=jnp.float32)
    hidden = (jax.nn.silu(gate_sum) * up_sum).astype(jnp.bfloat16)
    expert_rows = jnp.einsum(
        "esf,edf->esd",
        hidden,
        down_piece,
        preferred_element_type=jnp.float32,
    ).astype(jnp.bfloat16)
    returned = lax.all_to_all(expert_rows, "exp", split_axis=1, concat_axis=0, tiled=True)
    picked = jnp.take(returned.reshape(EXPERTS * CAP, D), target, axis=0).reshape(row_count, TOP, D)
    mixture = jnp.sum(picked.astype(jnp.float32) * gate_probs[0][:, :, None], axis=1)
    layer_out = (residual.astype(jnp.float32) + mixture).astype(jnp.bfloat16)
    return (attention_out[None], layer_out[None])


def solution(mesh):
    n_ctx = mesh.shape["ctx"]
    split = jax.sharding.Mesh(
        mesh.devices.reshape(n_ctx // 4, 2, 2, mesh.shape["exp"]), CTX_AXES + ("exp",)
    )
    return jax.shard_map(
        shards,
        mesh=split,
        in_specs=(
            P("exp", CTX_AXES, None),
            P("exp", CTX_AXES, None),
            P("exp", CTX_AXES, None),
            P("exp", CTX_AXES, None),
            P("exp", CTX_AXES, None),
            P(),
            P(),
            P("exp", CTX_AXES, None),
            P("exp", CTX_AXES, None),
            P("exp", CTX_AXES, None),
            P("exp", CTX_AXES, None),
            P("exp", CTX_AXES, None),
        ),
        out_specs=(P("exp", CTX_AXES, None), P("exp", CTX_AXES, None)),
        check_vma=False,
    )
```

```python
import functools

import jax
import jax.numpy as jnp
from jax import lax
from jax.experimental import pallas as pl
from jax.experimental.pallas import tpu as pltpu
from jax.sharding import PartitionSpec as P

D = 1024
HEADS = 8
KV_HEADS = 2
EXPERTS = 8
TOP = 2
TILE = 32
CAP = 72


def rms_scale(row_block, gain):
    widened = row_block.astype(jnp.float32)
    inverse = lax.rsqrt(jnp.mean(widened * widened, axis=-1, keepdims=True) + 1e-05)
    return widened * inverse * gain


CTX_AXES = ("z", "yh", "core")


MESH = pl.DeviceIdType.MESH


def gather_kernel(n_z, shard_ref, out_ref, local_sem, send_sem, recv_sem):
    z = lax.axis_index("z")
    yh = lax.axis_index("yh")
    core = lax.axis_index("core")
    ex = lax.axis_index("exp")

    def slot(zz, hh, cc):
        return (zz * 2 + hh) * 2 + cc

    def ring(offset):
        return lax.rem(z + offset + 4 * n_z, n_z)

    partner_h = 1 - yh
    sibling_c = 1 - core
    to_right = (ring(1), yh, core, ex)
    to_left = (ring(-1), yh, core, ex)
    to_partner = (z, partner_h, core, ex)
    to_sibling = (z, yh, sibling_c, ex)
    barrier = pltpu.get_barrier_semaphore()
    for dev in (to_right, to_left, to_partner, to_sibling):
        pl.semaphore_signal(barrier, 1, device_id=dev, device_id_type=MESH)
    pl.semaphore_wait(barrier, 4)

    me = slot(z, yh, core)
    own = pltpu.make_async_copy(shard_ref, out_ref.at[me], local_sem)
    own.start()
    sends = []

    def send(src, s, dev, k):
        copy = pltpu.make_async_remote_copy(
            src, out_ref.at[s], send_sem.at[k, s], recv_sem.at[s], device_id=dev, device_id_type=MESH
        )
        copy.start()
        sends.append(copy)

    def arrive(s):
        pltpu.make_async_remote_copy(
            out_ref.at[s], out_ref.at[s], send_sem.at[0, s], recv_sem.at[s],
            device_id=to_right, device_id_type=MESH,
        ).wait_recv()

    for k, dev in enumerate((to_right, to_left, to_partner, to_sibling)):
        send(shard_ref, me, dev, k)
    half = n_z // 2
    for t in range(1, half + 1):
        s = slot(ring(-t), yh, core)
        arrive(s)
        if t < half:
            send(out_ref.at[s], s, to_right, 0)
        send(out_ref.at[s], s, to_partner, 2)
        send(out_ref.at[s], s, to_sibling, 3)
        if t < n_z - half:
            s = slot(ring(t), yh, core)
            arrive(s)
            if t < n_z - half - 1:
                send(out_ref.at[s], s, to_left, 1)
            send(out_ref.at[s], s, to_partner, 2)
            send(out_ref.at[s], s, to_sibling, 3)
    partner_order = [0]
    for t in range(1, half + 1):
        partner_order.append(-t)
        if t < n_z - half:
            partner_order.append(t)
    for offset in partner_order:
        s = slot(ring(offset), partner_h, core)
        arrive(s)
        send(out_ref.at[s], s, to_sibling, 3)
    for hh in (yh, partner_h):
        for offset in partner_order:
            arrive(slot(ring(offset), hh, sibling_c))
    own.wait()
    for copy in sends:
        copy.wait_send()


def gather_ctx_kernel(block):
    n_z = lax.axis_size("z")
    n_all = n_z * 4
    return pl.pallas_call(
        functools.partial(gather_kernel, n_z),
        out_shape=jax.ShapeDtypeStruct((n_all,) + block.shape, block.dtype),
        in_specs=[pl.BlockSpec(memory_space=pl.ANY)],
        out_specs=pl.BlockSpec(memory_space=pl.ANY),
        scratch_shapes=[
            pltpu.SemaphoreType.DMA(()),
            pltpu.SemaphoreType.DMA((4, n_all)),
            pltpu.SemaphoreType.DMA((n_all,)),
        ],
        compiler_params=pltpu.CompilerParams(collective_id=0, has_side_effects=True),
    )(block)


def exchange_kernel(n_exp, chunk_ref, out_ref, local_sem, send_sem, recv_sem):
    me = lax.axis_index("exp")
    z = lax.axis_index("z")
    yh = lax.axis_index("yh")
    core = lax.axis_index("core")

    def peer(offset):
        return lax.rem(me + offset, n_exp)

    barrier = pltpu.get_barrier_semaphore()
    for offset in range(1, n_exp):
        pl.semaphore_signal(barrier, 1, device_id=(z, yh, core, peer(offset)), device_id_type=MESH)
    pl.semaphore_wait(barrier, n_exp - 1)
    own = pltpu.make_async_copy(chunk_ref.at[me], out_ref.at[me], local_sem)
    own.start()
    sends = []
    for offset in range(1, n_exp):
        target = peer(offset)
        copy = pltpu.make_async_remote_copy(
            chunk_ref.at[target], out_ref.at[me], send_sem.at[offset], recv_sem.at[me],
            device_id=(z, yh, core, target), device_id_type=MESH,
        )
        copy.start()
        sends.append(copy)
    for offset in range(1, n_exp):
        source = peer(n_exp - offset)
        pltpu.make_async_remote_copy(
            out_ref.at[source], out_ref.at[source], send_sem.at[offset], recv_sem.at[source],
            device_id=(z, yh, core, source), device_id_type=MESH,
        ).wait_recv()
    own.wait()
    for copy in sends:
        copy.wait_send()


def exchange_exp(chunks, collective_id):
    n_exp = chunks.shape[0]
    return pl.pallas_call(
        functools.partial(exchange_kernel, n_exp),
        out_shape=jax.ShapeDtypeStruct(chunks.shape, chunks.dtype),
        in_specs=[pl.BlockSpec(memory_space=pl.ANY)],
        out_specs=pl.BlockSpec(memory_space=pl.ANY),
        scratch_shapes=[
            pltpu.SemaphoreType.DMA(()),
            pltpu.SemaphoreType.DMA((n_exp,)),
            pltpu.SemaphoreType.DMA((n_exp,)),
        ],
        compiler_params=pltpu.CompilerParams(collective_id=collective_id, has_side_effects=True),
    )(chunks)


KEY_BLOCK = 128


def attention_kernel(groups, head_size, flag_ref, q_ref, kv_ref, mask_ref, out_ref, top_ref, sum_ref, acc_ref):
    n_blocks = flag_ref.shape[0]
    kv_heads = kv_ref.shape[1] // (2 * head_size)
    heads = kv_heads * groups
    value_at = kv_heads * head_size
    scale = head_size ** (-0.5)
    top_ref[...] = jnp.full(top_ref.shape, -1e30, jnp.float32)
    sum_ref[...] = jnp.zeros(sum_ref.shape, jnp.float32)
    acc_ref[...] = jnp.zeros(acc_ref.shape, jnp.float32)

    def scores(j, h):
        rows = pl.ds(pl.multiple_of(j * KEY_BLOCK, KEY_BLOCK), KEY_BLOCK)
        key = kv_ref[rows, pl.ds((h // groups) * head_size, head_size)]
        query = q_ref[:, pl.ds(h * head_size, head_size)]
        raw = lax.dot_general(
            query, key, (((1,), (1,)), ((), ())), preferred_element_type=jnp.float32
        )
        return raw * scale, mask_ref[:, rows] > 0

    def first_pass(j, carry):
        @pl.when(flag_ref[j] > 0)
        def _():
            for h in range(heads):
                s, allowed = scores(j, h)
                top_ref[h] = jnp.maximum(top_ref[h], jnp.where(allowed, s, -1e30))
        return carry

    lax.fori_loop(0, n_blocks, first_pass, 0)
    for h in range(heads):
        top_ref[h] = jnp.broadcast_to(jnp.max(top_ref[h], axis=1, keepdims=True), top_ref.shape[1:])

    def second_pass(j, carry):
        @pl.when(flag_ref[j] > 0)
        def _():
            rows = pl.ds(pl.multiple_of(j * KEY_BLOCK, KEY_BLOCK), KEY_BLOCK)
            for h in range(heads):
                s, allowed = scores(j, h)
                weights = jnp.where(allowed, jnp.exp(s - top_ref[h]), 0.0)
                sum_ref[h] += weights
                value = kv_ref[rows, pl.ds(value_at + (h // groups) * head_size, head_size)]
                acc_ref[h] += jnp.dot(
                    weights.astype(jnp.bfloat16), value, preferred_element_type=jnp.float32
                )
        return carry

    lax.fori_loop(0, n_blocks, second_pass, 0)
    for h in range(heads):
        denominator = jnp.sum(sum_ref[h], axis=1, keepdims=True)
        out_ref[:, pl.ds(h * head_size, head_size)] = (acc_ref[h] / denominator).astype(out_ref.dtype)


def block_attention(query_rows, kv_rows, mask_block, groups, head_size):
    row_count = query_rows.shape[0]
    key_count = kv_rows.shape[0]
    heads = query_rows.shape[1] // head_size
    allowed = jnp.repeat(jnp.repeat(mask_block, TILE, axis=0), TILE, axis=1).astype(jnp.bfloat16)
    tiles_per_block = KEY_BLOCK // TILE
    flags = jnp.max(
        mask_block.reshape(mask_block.shape[0], -1, tiles_per_block), axis=(0, 2)
    ).astype(jnp.int32)
    vmem = pl.BlockSpec(memory_space=pltpu.VMEM)
    return pl.pallas_call(
        functools.partial(attention_kernel, groups, head_size),
        out_shape=jax.ShapeDtypeStruct((row_count, heads * head_size), jnp.bfloat16),
        in_specs=[pl.BlockSpec(memory_space=pltpu.SMEM), vmem, vmem, vmem],
        out_specs=vmem,
        scratch_shapes=[
            pltpu.VMEM((heads, row_count, KEY_BLOCK), jnp.float32),
            pltpu.VMEM((heads, row_count, KEY_BLOCK), jnp.float32),
            pltpu.VMEM((heads, row_count, head_size), jnp.float32),
        ],
    )(flags, query_rows, kv_rows, allowed)


def shards(
    hidden_in,
    queries,
    key_proj,
    value_proj,
    tile_mask,
    out_weight,
    moe_gain,
    gate_weight,
    up_weight,
    down_weight,
    expert_ids,
    gate_probs,
):
    query_rows = queries[0]
    row_count = query_rows.shape[0]
    groups = HEADS // KV_HEADS
    head_size = D // HEADS
    query_heads = query_rows.reshape(row_count, KV_HEADS, groups, head_size)
    mask_block = tile_mask[0]
    kv_width = key_proj.shape[-1]
    kv_local = jnp.concatenate([key_proj[0], value_proj[0]], axis=-1)
    kv_piece = gather_ctx_kernel(kv_local).reshape(-1, 2 * kv_width)
    attended = block_attention(query_rows, kv_piece, mask_block, groups, head_size)
    projected = jnp.dot(attended, out_weight, preferred_element_type=jnp.float32)
    attention_out = projected.astype(jnp.bfloat16)
    residual = (hidden_in[0].astype(jnp.float32) + projected).astype(jnp.bfloat16)
    normed = rms_scale(residual, moe_gain).astype(jnp.bfloat16)
    id_row = expert_ids[0].reshape(-1)
    onehot = (id_row[:, None] == jnp.arange(EXPERTS, dtype=jnp.int32)[None, :]).astype(jnp.int32)
    before = jnp.cumsum(onehot, axis=0) - onehot
    slot_index = jnp.sum(before * onehot, axis=1)
    target = id_row * CAP + slot_index
    selector = (jnp.arange(EXPERTS * CAP, dtype=jnp.int32)[:, None] == target[None, :]).astype(
        jnp.bfloat16
    )
    repeated = jnp.repeat(normed, TOP, axis=0)
    outgoing = (
        jnp.dot(selector, repeated, preferred_element_type=jnp.float32)
        .astype(jnp.bfloat16)
        .reshape(EXPERTS, CAP, D)
    )
    arrived = exchange_exp(outgoing, 1).reshape(1, EXPERTS * CAP, D)
    ff = gate_weight.shape[-1]
    weight_piece = lax.all_gather(
        jnp.concatenate([gate_weight, up_weight, down_weight], axis=-1), CTX_AXES, axis=1, tiled=True
    )
    gate_piece = weight_piece[..., :ff]
    up_piece = weight_piece[..., ff : 2 * ff]
    down_piece = weight_piece[..., 2 * ff :]
    gate_sum = jnp.einsum("esd,edf->esf", arrived, gate_piece, preferred_element_type=jnp.float32)
    up_sum = jnp.einsum("esd,edf->esf", arrived, up_piece, preferred_element_type=jnp.float32)
    hidden = (jax.nn.silu(gate_sum) * up_sum).astype(jnp.bfloat16)
    expert_rows = jnp.einsum(
        "esf,edf->esd",
        hidden,
        down_piece,
        preferred_element_type=jnp.float32,
    ).astype(jnp.bfloat16)
    returned = exchange_exp(expert_rows.reshape(EXPERTS, CAP, D), 2)
    picked = jnp.take(returned.reshape(EXPERTS * CAP, D), target, axis=0).reshape(row_count, TOP, D)
    mixture = jnp.sum(picked.astype(jnp.float32) * gate_probs[0][:, :, None], axis=1)
    layer_out = (residual.astype(jnp.float32) + mixture).astype(jnp.bfloat16)
    return (attention_out[None], layer_out[None])


def solution(mesh):
    n_ctx = mesh.shape["ctx"]
    split = jax.sharding.Mesh(
        mesh.devices.reshape(n_ctx // 4, 2, 2, mesh.shape["exp"]), CTX_AXES + ("exp",)
    )
    return jax.shard_map(
        shards,
        mesh=split,
        in_specs=(
            P("exp", CTX_AXES, None),
            P("exp", CTX_AXES, None),
            P("exp", CTX_AXES, None),
            P("exp", CTX_AXES, None),
            P("exp", CTX_AXES, None),
            P(),
            P(),
            P("exp", CTX_AXES, None),
            P("exp", CTX_AXES, None),
            P("exp", CTX_AXES, None),
            P("exp", CTX_AXES, None),
            P("exp", CTX_AXES, None),
        ),
        out_specs=(P("exp", CTX_AXES, None), P("exp", CTX_AXES, None)),
        check_vma=False,
    )
```

```python
import functools

import jax
import jax.numpy as jnp
from jax import lax
from jax.experimental import pallas as pl
from jax.experimental.pallas import tpu as pltpu
from jax.sharding import PartitionSpec as P

D = 1024
HEADS = 8
KV_HEADS = 2
EXPERTS = 8
TOP = 2
TILE = 32
CAP = 72


def rms_scale(row_block, gain):
    widened = row_block.astype(jnp.float32)
    inverse = lax.rsqrt(jnp.mean(widened * widened, axis=-1, keepdims=True) + 1e-05)
    return widened * inverse * gain


CTX_AXES = ("z", "yh", "core")


MESH = pl.DeviceIdType.MESH


def gather_kernel(n_z, shard_ref, out_ref, local_sem, send_sem, recv_sem):
    z = lax.axis_index("z")
    yh = lax.axis_index("yh")
    core = lax.axis_index("core")
    ex = lax.axis_index("exp")

    def slot(zz, hh, cc):
        return (zz * 2 + hh) * 2 + cc

    def ring(offset):
        return lax.rem(z + offset + 4 * n_z, n_z)

    partner_h = 1 - yh
    sibling_c = 1 - core
    to_right = (ring(1), yh, core, ex)
    to_left = (ring(-1), yh, core, ex)
    to_partner = (z, partner_h, core, ex)
    to_sibling = (z, yh, sibling_c, ex)
    barrier = pltpu.get_barrier_semaphore()
    for dev in (to_right, to_left, to_partner, to_sibling):
        pl.semaphore_signal(barrier, 1, device_id=dev, device_id_type=MESH)
    pl.semaphore_wait(barrier, 4)

    me = slot(z, yh, core)
    own = pltpu.make_async_copy(shard_ref, out_ref.at[me], local_sem)
    own.start()
    sends = []

    def send(src, s, dev, k):
        copy = pltpu.make_async_remote_copy(
            src, out_ref.at[s], send_sem.at[k, s], recv_sem.at[s], device_id=dev, device_id_type=MESH
        )
        copy.start()
        sends.append(copy)

    def arrive(s):
        pltpu.make_async_remote_copy(
            out_ref.at[s], out_ref.at[s], send_sem.at[0, s], recv_sem.at[s],
            device_id=to_right, device_id_type=MESH,
        ).wait_recv()

    for k, dev in enumerate((to_right, to_left, to_partner, to_sibling)):
        send(shard_ref, me, dev, k)
    half = n_z // 2
    for t in range(1, half + 1):
        s = slot(ring(-t), yh, core)
        arrive(s)
        if t < half:
            send(out_ref.at[s], s, to_right, 0)
        send(out_ref.at[s], s, to_partner, 2)
        send(out_ref.at[s], s, to_sibling, 3)
        if t < n_z - half:
            s = slot(ring(t), yh, core)
            arrive(s)
            if t < n_z - half - 1:
                send(out_ref.at[s], s, to_left, 1)
            send(out_ref.at[s], s, to_partner, 2)
            send(out_ref.at[s], s, to_sibling, 3)
    partner_order = [0]
    for t in range(1, half + 1):
        partner_order.append(-t)
        if t < n_z - half:
            partner_order.append(t)
    for offset in partner_order:
        s = slot(ring(offset), partner_h, core)
        arrive(s)
        send(out_ref.at[s], s, to_sibling, 3)
    for hh in (yh, partner_h):
        for offset in partner_order:
            arrive(slot(ring(offset), hh, sibling_c))
    own.wait()
    for copy in sends:
        copy.wait_send()


def gather_ctx_kernel(block):
    n_z = lax.axis_size("z")
    n_all = n_z * 4
    return pl.pallas_call(
        functools.partial(gather_kernel, n_z),
        out_shape=jax.ShapeDtypeStruct((n_all,) + block.shape, block.dtype),
        in_specs=[pl.BlockSpec(memory_space=pl.ANY)],
        out_specs=pl.BlockSpec(memory_space=pl.ANY),
        scratch_shapes=[
            pltpu.SemaphoreType.DMA(()),
            pltpu.SemaphoreType.DMA((4, n_all)),
            pltpu.SemaphoreType.DMA((n_all,)),
        ],
        compiler_params=pltpu.CompilerParams(collective_id=0, has_side_effects=True),
    )(block)


def exchange_kernel(n_exp, chunk_ref, out_ref, local_sem, send_sem, recv_sem):
    me = lax.axis_index("exp")
    z = lax.axis_index("z")
    yh = lax.axis_index("yh")
    core = lax.axis_index("core")

    def peer(offset):
        return lax.rem(me + offset, n_exp)

    barrier = pltpu.get_barrier_semaphore()
    for offset in range(1, n_exp):
        pl.semaphore_signal(barrier, 1, device_id=(z, yh, core, peer(offset)), device_id_type=MESH)
    pl.semaphore_wait(barrier, n_exp - 1)
    own = pltpu.make_async_copy(chunk_ref.at[me], out_ref.at[me], local_sem)
    own.start()
    sends = []
    for offset in range(1, n_exp):
        target = peer(offset)
        copy = pltpu.make_async_remote_copy(
            chunk_ref.at[target], out_ref.at[me], send_sem.at[offset], recv_sem.at[me],
            device_id=(z, yh, core, target), device_id_type=MESH,
        )
        copy.start()
        sends.append(copy)
    for offset in range(1, n_exp):
        source = peer(n_exp - offset)
        pltpu.make_async_remote_copy(
            out_ref.at[source], out_ref.at[source], send_sem.at[offset], recv_sem.at[source],
            device_id=(z, yh, core, source), device_id_type=MESH,
        ).wait_recv()
    own.wait()
    for copy in sends:
        copy.wait_send()


def exchange_exp(chunks, collective_id):
    n_exp = chunks.shape[0]
    return pl.pallas_call(
        functools.partial(exchange_kernel, n_exp),
        out_shape=jax.ShapeDtypeStruct(chunks.shape, chunks.dtype),
        in_specs=[pl.BlockSpec(memory_space=pl.ANY)],
        out_specs=pl.BlockSpec(memory_space=pl.ANY),
        scratch_shapes=[
            pltpu.SemaphoreType.DMA(()),
            pltpu.SemaphoreType.DMA((n_exp,)),
            pltpu.SemaphoreType.DMA((n_exp,)),
        ],
        compiler_params=pltpu.CompilerParams(collective_id=collective_id, has_side_effects=True),
    )(chunks)


KEY_BLOCK = 128


def attention_kernel(groups, head_size, flag_ref, q_ref, kv_ref, mask_ref, out_ref, top_ref, sum_ref, acc_ref):
    n_blocks = flag_ref.shape[0]
    kv_heads = kv_ref.shape[1] // (2 * head_size)
    heads = kv_heads * groups
    value_at = kv_heads * head_size
    scale = head_size ** (-0.5)
    top_ref[...] = jnp.full(top_ref.shape, -1e30, jnp.float32)
    sum_ref[...] = jnp.zeros(sum_ref.shape, jnp.float32)
    acc_ref[...] = jnp.zeros(acc_ref.shape, jnp.float32)

    def allowed_block(j):
        tile_count = mask_ref.shape[1]
        tile_at = lax.broadcasted_iota(jnp.int32, (tile_count, KEY_BLOCK), 0)
        column_tile = lax.broadcasted_iota(jnp.int32, (tile_count, KEY_BLOCK), 1) // TILE
        spread = (tile_at == j * (KEY_BLOCK // TILE) + column_tile).astype(jnp.bfloat16)
        return jnp.dot(mask_ref[...], spread, preferred_element_type=jnp.float32) > 0

    def scores(j, h):
        rows = pl.ds(pl.multiple_of(j * KEY_BLOCK, KEY_BLOCK), KEY_BLOCK)
        key = kv_ref[rows, pl.ds((h // groups) * head_size, head_size)]
        query = q_ref[:, pl.ds(h * head_size, head_size)]
        raw = lax.dot_general(
            query, key, (((1,), (1,)), ((), ())), preferred_element_type=jnp.float32
        )
        return raw * scale, allowed_block(j)

    def first_pass(j, carry):
        @pl.when(flag_ref[j] > 0)
        def _():
            for h in range(heads):
                s, allowed = scores(j, h)
                top_ref[h] = jnp.maximum(top_ref[h], jnp.where(allowed, s, -1e30))
        return carry

    lax.fori_loop(0, n_blocks, first_pass, 0)
    for h in range(heads):
        top_ref[h] = jnp.broadcast_to(jnp.max(top_ref[h], axis=1, keepdims=True), top_ref.shape[1:])

    def second_pass(j, carry):
        @pl.when(flag_ref[j] > 0)
        def _():
            rows = pl.ds(pl.multiple_of(j * KEY_BLOCK, KEY_BLOCK), KEY_BLOCK)
            for h in range(heads):
                s, allowed = scores(j, h)
                weights = jnp.where(allowed, jnp.exp(s - top_ref[h]), 0.0)
                sum_ref[h] += weights
                value = kv_ref[rows, pl.ds(value_at + (h // groups) * head_size, head_size)]
                acc_ref[h] += jnp.dot(
                    weights.astype(jnp.bfloat16), value, preferred_element_type=jnp.float32
                )
        return carry

    lax.fori_loop(0, n_blocks, second_pass, 0)
    for h in range(heads):
        denominator = jnp.sum(sum_ref[h], axis=1, keepdims=True)
        out_ref[:, pl.ds(h * head_size, head_size)] = (acc_ref[h] / denominator).astype(out_ref.dtype)


def block_attention(query_rows, kv_rows, mask_block, groups, head_size):
    row_count = query_rows.shape[0]
    key_count = kv_rows.shape[0]
    heads = query_rows.shape[1] // head_size
    allowed = jnp.repeat(mask_block, TILE, axis=0).astype(jnp.bfloat16)
    tiles_per_block = KEY_BLOCK // TILE
    flags = jnp.max(
        mask_block.reshape(mask_block.shape[0], -1, tiles_per_block), axis=(0, 2)
    ).astype(jnp.int32)
    vmem = pl.BlockSpec(memory_space=pltpu.VMEM)
    return pl.pallas_call(
        functools.partial(attention_kernel, groups, head_size),
        out_shape=jax.ShapeDtypeStruct((row_count, heads * head_size), jnp.bfloat16),
        in_specs=[pl.BlockSpec(memory_space=pltpu.SMEM), vmem, vmem, vmem],
        out_specs=vmem,
        scratch_shapes=[
            pltpu.VMEM((heads, row_count, KEY_BLOCK), jnp.float32),
            pltpu.VMEM((heads, row_count, KEY_BLOCK), jnp.float32),
            pltpu.VMEM((heads, row_count, head_size), jnp.float32),
        ],
    )(flags, query_rows, kv_rows, allowed)


def shards(
    hidden_in,
    queries,
    key_proj,
    value_proj,
    tile_mask,
    out_weight,
    moe_gain,
    gate_weight,
    up_weight,
    down_weight,
    expert_ids,
    gate_probs,
):
    query_rows = queries[0]
    row_count = query_rows.shape[0]
    groups = HEADS // KV_HEADS
    head_size = D // HEADS
    query_heads = query_rows.reshape(row_count, KV_HEADS, groups, head_size)
    mask_block = tile_mask[0]
    kv_width = key_proj.shape[-1]
    kv_local = jnp.concatenate([key_proj[0], value_proj[0]], axis=-1)
    kv_piece = gather_ctx_kernel(kv_local).reshape(-1, 2 * kv_width)
    attended = block_attention(query_rows, kv_piece, mask_block, groups, head_size)
    projected = jnp.dot(attended, out_weight, preferred_element_type=jnp.float32)
    attention_out = projected.astype(jnp.bfloat16)
    residual = (hidden_in[0].astype(jnp.float32) + projected).astype(jnp.bfloat16)
    normed = rms_scale(residual, moe_gain).astype(jnp.bfloat16)
    id_row = expert_ids[0].reshape(-1)
    onehot = (id_row[:, None] == jnp.arange(EXPERTS, dtype=jnp.int32)[None, :]).astype(jnp.int32)
    before = jnp.cumsum(onehot, axis=0) - onehot
    slot_index = jnp.sum(before * onehot, axis=1)
    target = id_row * CAP + slot_index
    selector = (jnp.arange(EXPERTS * CAP, dtype=jnp.int32)[:, None] == target[None, :]).astype(
        jnp.bfloat16
    )
    repeated = jnp.repeat(normed, TOP, axis=0)
    outgoing = (
        jnp.dot(selector, repeated, preferred_element_type=jnp.float32)
        .astype(jnp.bfloat16)
        .reshape(EXPERTS, CAP, D)
    )
    arrived = exchange_exp(outgoing, 1).reshape(1, EXPERTS * CAP, D)
    ff = gate_weight.shape[-1]
    weight_piece = lax.all_gather(
        jnp.concatenate([gate_weight, up_weight, down_weight], axis=-1), CTX_AXES, axis=1, tiled=True
    )
    gate_piece = weight_piece[..., :ff]
    up_piece = weight_piece[..., ff : 2 * ff]
    down_piece = weight_piece[..., 2 * ff :]
    gate_sum = jnp.einsum("esd,edf->esf", arrived, gate_piece, preferred_element_type=jnp.float32)
    up_sum = jnp.einsum("esd,edf->esf", arrived, up_piece, preferred_element_type=jnp.float32)
    hidden = (jax.nn.silu(gate_sum) * up_sum).astype(jnp.bfloat16)
    expert_rows = jnp.einsum(
        "esf,edf->esd",
        hidden,
        down_piece,
        preferred_element_type=jnp.float32,
    ).astype(jnp.bfloat16)
    returned = exchange_exp(expert_rows.reshape(EXPERTS, CAP, D), 2)
    combine = jnp.sum(
        jnp.where(
            jnp.arange(EXPERTS * CAP, dtype=jnp.int32)[None, None, :] == target.reshape(row_count, TOP)[:, :, None],
            gate_probs[0][:, :, None],
            0.0,
        ),
        axis=1,
    )
    mixture = jnp.dot(
        combine,
        returned.reshape(EXPERTS * CAP, D).astype(jnp.float32),
        precision=lax.Precision.HIGHEST,
        preferred_element_type=jnp.float32,
    )
    layer_out = (residual.astype(jnp.float32) + mixture).astype(jnp.bfloat16)
    return (attention_out[None], layer_out[None])


def solution(mesh):
    n_ctx = mesh.shape["ctx"]
    split = jax.sharding.Mesh(
        mesh.devices.reshape(n_ctx // 4, 2, 2, mesh.shape["exp"]), CTX_AXES + ("exp",)
    )
    return jax.shard_map(
        shards,
        mesh=split,
        in_specs=(
            P("exp", CTX_AXES, None),
            P("exp", CTX_AXES, None),
            P("exp", CTX_AXES, None),
            P("exp", CTX_AXES, None),
            P("exp", CTX_AXES, None),
            P(),
            P(),
            P("exp", CTX_AXES, None),
            P("exp", CTX_AXES, None),
            P("exp", CTX_AXES, None),
            P("exp", CTX_AXES, None),
            P("exp", CTX_AXES, None),
        ),
        out_specs=(P("exp", CTX_AXES, None), P("exp", CTX_AXES, None)),
        check_vma=False,
    )
```

```python
import functools

import jax
import jax.numpy as jnp
from jax import lax
from jax.experimental import pallas as pl
from jax.experimental.pallas import tpu as pltpu
from jax.sharding import PartitionSpec as P

D = 1024
HEADS = 8
KV_HEADS = 2
EXPERTS = 8
TOP = 2
TILE = 32
CAP = 72


def rms_scale(row_block, gain):
    widened = row_block.astype(jnp.float32)
    inverse = lax.rsqrt(jnp.mean(widened * widened, axis=-1, keepdims=True) + 1e-05)
    return widened * inverse * gain


CTX_AXES = ("z", "yh", "core")


MESH = pl.DeviceIdType.MESH


def gather_kernel(n_z, shard_ref, out_ref, local_sem, send_sem, recv_sem):
    z = lax.axis_index("z")
    yh = lax.axis_index("yh")
    core = lax.axis_index("core")
    ex = lax.axis_index("exp")

    def slot(zz, hh, cc):
        return (zz * 2 + hh) * 2 + cc

    def ring(offset):
        return lax.rem(z + offset + 4 * n_z, n_z)

    partner_h = 1 - yh
    sibling_c = 1 - core
    to_right = (ring(1), yh, core, ex)
    to_left = (ring(-1), yh, core, ex)
    to_partner = (z, partner_h, core, ex)
    to_sibling = (z, yh, sibling_c, ex)
    barrier = pltpu.get_barrier_semaphore()
    for dev in (to_right, to_left, to_partner, to_sibling):
        pl.semaphore_signal(barrier, 1, device_id=dev, device_id_type=MESH)
    pl.semaphore_wait(barrier, 4)

    me = slot(z, yh, core)
    own = pltpu.make_async_copy(shard_ref, out_ref.at[me], local_sem)
    own.start()
    sends = []

    def send(src, s, dev, k):
        copy = pltpu.make_async_remote_copy(
            src, out_ref.at[s], send_sem.at[k, s], recv_sem.at[s], device_id=dev, device_id_type=MESH
        )
        copy.start()
        sends.append(copy)

    def arrive(s):
        pltpu.make_async_remote_copy(
            out_ref.at[s], out_ref.at[s], send_sem.at[0, s], recv_sem.at[s],
            device_id=to_right, device_id_type=MESH,
        ).wait_recv()

    for k, dev in enumerate((to_right, to_left, to_partner, to_sibling)):
        send(shard_ref, me, dev, k)
    half = n_z // 2
    for t in range(1, half + 1):
        s = slot(ring(-t), yh, core)
        arrive(s)
        if t < half:
            send(out_ref.at[s], s, to_right, 0)
        send(out_ref.at[s], s, to_partner, 2)
        send(out_ref.at[s], s, to_sibling, 3)
        if t < n_z - half:
            s = slot(ring(t), yh, core)
            arrive(s)
            if t < n_z - half - 1:
                send(out_ref.at[s], s, to_left, 1)
            send(out_ref.at[s], s, to_partner, 2)
            send(out_ref.at[s], s, to_sibling, 3)
    partner_order = [0]
    for t in range(1, half + 1):
        partner_order.append(-t)
        if t < n_z - half:
            partner_order.append(t)
    for offset in partner_order:
        s = slot(ring(offset), partner_h, core)
        arrive(s)
        send(out_ref.at[s], s, to_sibling, 3)
    for hh in (yh, partner_h):
        for offset in partner_order:
            arrive(slot(ring(offset), hh, sibling_c))
    own.wait()
    for copy in sends:
        copy.wait_send()


def gather_ctx_kernel(block):
    n_z = lax.axis_size("z")
    n_all = n_z * 4
    return pl.pallas_call(
        functools.partial(gather_kernel, n_z),
        out_shape=jax.ShapeDtypeStruct((n_all,) + block.shape, block.dtype),
        in_specs=[pl.BlockSpec(memory_space=pl.ANY)],
        out_specs=pl.BlockSpec(memory_space=pl.ANY),
        scratch_shapes=[
            pltpu.SemaphoreType.DMA(()),
            pltpu.SemaphoreType.DMA((4, n_all)),
            pltpu.SemaphoreType.DMA((n_all,)),
        ],
        compiler_params=pltpu.CompilerParams(collective_id=0, has_side_effects=True),
    )(block)


def exchange_kernel(n_exp, chunk_ref, out_ref, local_sem, send_sem, recv_sem):
    me = lax.axis_index("exp")
    z = lax.axis_index("z")
    yh = lax.axis_index("yh")
    core = lax.axis_index("core")

    def peer(offset):
        return lax.rem(me + offset, n_exp)

    barrier = pltpu.get_barrier_semaphore()
    for offset in range(1, n_exp):
        pl.semaphore_signal(barrier, 1, device_id=(z, yh, core, peer(offset)), device_id_type=MESH)
    pl.semaphore_wait(barrier, n_exp - 1)
    own = pltpu.make_async_copy(chunk_ref.at[me], out_ref.at[me], local_sem)
    own.start()
    sends = []
    for offset in range(1, n_exp):
        target = peer(offset)
        copy = pltpu.make_async_remote_copy(
            chunk_ref.at[target], out_ref.at[me], send_sem.at[offset], recv_sem.at[me],
            device_id=(z, yh, core, target), device_id_type=MESH,
        )
        copy.start()
        sends.append(copy)
    for offset in range(1, n_exp):
        source = peer(n_exp - offset)
        pltpu.make_async_remote_copy(
            out_ref.at[source], out_ref.at[source], send_sem.at[offset], recv_sem.at[source],
            device_id=(z, yh, core, source), device_id_type=MESH,
        ).wait_recv()
    own.wait()
    for copy in sends:
        copy.wait_send()


def exchange_exp(chunks, collective_id):
    n_exp = chunks.shape[0]
    return pl.pallas_call(
        functools.partial(exchange_kernel, n_exp),
        out_shape=jax.ShapeDtypeStruct(chunks.shape, chunks.dtype),
        in_specs=[pl.BlockSpec(memory_space=pl.ANY)],
        out_specs=pl.BlockSpec(memory_space=pl.ANY),
        scratch_shapes=[
            pltpu.SemaphoreType.DMA(()),
            pltpu.SemaphoreType.DMA((n_exp,)),
            pltpu.SemaphoreType.DMA((n_exp,)),
        ],
        compiler_params=pltpu.CompilerParams(collective_id=collective_id, has_side_effects=True),
    )(chunks)


KEY_BLOCK = 128


def attention_kernel(groups, head_size, flag_ref, q_ref, kv_ref, mask_ref, out_ref, top_ref, sum_ref, acc_ref):
    n_blocks = flag_ref.shape[0]
    kv_heads = kv_ref.shape[1] // (2 * head_size)
    heads = kv_heads * groups
    value_at = kv_heads * head_size
    scale = head_size ** (-0.5)
    top_ref[...] = jnp.full(top_ref.shape, -1e30, jnp.float32)
    sum_ref[...] = jnp.zeros(sum_ref.shape, jnp.float32)
    acc_ref[...] = jnp.zeros(acc_ref.shape, jnp.float32)

    def allowed_block(j):
        tile_count = mask_ref.shape[1]
        tile_at = lax.broadcasted_iota(jnp.int32, (tile_count, KEY_BLOCK), 0)
        column_tile = lax.broadcasted_iota(jnp.int32, (tile_count, KEY_BLOCK), 1) // TILE
        spread = (tile_at == j * (KEY_BLOCK // TILE) + column_tile).astype(jnp.bfloat16)
        return jnp.dot(mask_ref[...], spread, preferred_element_type=jnp.float32) > 0

    def scores(j, h):
        rows = pl.ds(pl.multiple_of(j * KEY_BLOCK, KEY_BLOCK), KEY_BLOCK)
        key = kv_ref[rows, pl.ds((h // groups) * head_size, head_size)]
        query = q_ref[:, pl.ds(h * head_size, head_size)]
        raw = lax.dot_general(
            query, key, (((1,), (1,)), ((), ())), preferred_element_type=jnp.float32
        )
        return raw * scale

    def first_pass(j, carry):
        @pl.when(flag_ref[j] > 0)
        def _():
            allowed = allowed_block(j)
            for h in range(heads):
                s = scores(j, h)
                top_ref[h] = jnp.maximum(top_ref[h], jnp.where(allowed, s, -1e30))
        return carry

    lax.fori_loop(0, n_blocks, first_pass, 0)
    for h in range(heads):
        top_ref[h] = jnp.broadcast_to(jnp.max(top_ref[h], axis=1, keepdims=True), top_ref.shape[1:])

    def second_pass(j, carry):
        @pl.when(flag_ref[j] > 0)
        def _():
            rows = pl.ds(pl.multiple_of(j * KEY_BLOCK, KEY_BLOCK), KEY_BLOCK)
            allowed = allowed_block(j)
            for h in range(heads):
                s = scores(j, h)
                weights = jnp.where(allowed, jnp.exp(s - top_ref[h]), 0.0)
                sum_ref[h] += weights
                value = kv_ref[rows, pl.ds(value_at + (h // groups) * head_size, head_size)]
                acc_ref[h] += jnp.dot(
                    weights.astype(jnp.bfloat16), value, preferred_element_type=jnp.float32
                )
        return carry

    lax.fori_loop(0, n_blocks, second_pass, 0)
    for h in range(heads):
        denominator = jnp.sum(sum_ref[h], axis=1, keepdims=True)
        out_ref[:, pl.ds(h * head_size, head_size)] = (acc_ref[h] / denominator).astype(out_ref.dtype)


def block_attention(query_rows, kv_rows, mask_block, groups, head_size):
    row_count = query_rows.shape[0]
    key_count = kv_rows.shape[0]
    heads = query_rows.shape[1] // head_size
    allowed = jnp.repeat(mask_block, TILE, axis=0).astype(jnp.bfloat16)
    tiles_per_block = KEY_BLOCK // TILE
    flags = jnp.max(
        mask_block.reshape(mask_block.shape[0], -1, tiles_per_block), axis=(0, 2)
    ).astype(jnp.int32)
    vmem = pl.BlockSpec(memory_space=pltpu.VMEM)
    return pl.pallas_call(
        functools.partial(attention_kernel, groups, head_size),
        out_shape=jax.ShapeDtypeStruct((row_count, heads * head_size), jnp.bfloat16),
        in_specs=[pl.BlockSpec(memory_space=pltpu.SMEM), vmem, vmem, vmem],
        out_specs=vmem,
        scratch_shapes=[
            pltpu.VMEM((heads, row_count, KEY_BLOCK), jnp.float32),
            pltpu.VMEM((heads, row_count, KEY_BLOCK), jnp.float32),
            pltpu.VMEM((heads, row_count, head_size), jnp.float32),
        ],
    )(flags, query_rows, kv_rows, allowed)


def shards(
    hidden_in,
    queries,
    key_proj,
    value_proj,
    tile_mask,
    out_weight,
    moe_gain,
    gate_weight,
    up_weight,
    down_weight,
    expert_ids,
    gate_probs,
):
    query_rows = queries[0]
    row_count = query_rows.shape[0]
    groups = HEADS // KV_HEADS
    head_size = D // HEADS
    query_heads = query_rows.reshape(row_count, KV_HEADS, groups, head_size)
    mask_block = tile_mask[0]
    kv_width = key_proj.shape[-1]
    kv_local = jnp.concatenate([key_proj[0], value_proj[0]], axis=-1)
    kv_piece = gather_ctx_kernel(kv_local).reshape(-1, 2 * kv_width)
    attended = block_attention(query_rows, kv_piece, mask_block, groups, head_size)
    projected = jnp.dot(attended, out_weight, preferred_element_type=jnp.float32)
    attention_out = projected.astype(jnp.bfloat16)
    residual = (hidden_in[0].astype(jnp.float32) + projected).astype(jnp.bfloat16)
    normed = rms_scale(residual, moe_gain).astype(jnp.bfloat16)
    id_row = expert_ids[0].reshape(-1)
    onehot = (id_row[:, None] == jnp.arange(EXPERTS, dtype=jnp.int32)[None, :]).astype(jnp.int32)
    before = jnp.cumsum(onehot, axis=0) - onehot
    slot_index = jnp.sum(before * onehot, axis=1)
    target = id_row * CAP + slot_index
    selector = (jnp.arange(EXPERTS * CAP, dtype=jnp.int32)[:, None] == target[None, :]).astype(
        jnp.bfloat16
    )
    repeated = jnp.repeat(normed, TOP, axis=0)
    outgoing = (
        jnp.dot(selector, repeated, preferred_element_type=jnp.float32)
        .astype(jnp.bfloat16)
        .reshape(EXPERTS, CAP, D)
    )
    arrived = exchange_exp(outgoing, 1).reshape(1, EXPERTS * CAP, D)
    ff = gate_weight.shape[-1]
    weight_piece = lax.all_gather(
        jnp.concatenate([gate_weight, up_weight, down_weight], axis=-1), CTX_AXES, axis=1, tiled=True
    )
    gate_piece = weight_piece[..., :ff]
    up_piece = weight_piece[..., ff : 2 * ff]
    down_piece = weight_piece[..., 2 * ff :]
    gate_sum = jnp.einsum("esd,edf->esf", arrived, gate_piece, preferred_element_type=jnp.float32)
    up_sum = jnp.einsum("esd,edf->esf", arrived, up_piece, preferred_element_type=jnp.float32)
    hidden = (jax.nn.silu(gate_sum) * up_sum).astype(jnp.bfloat16)
    expert_rows = jnp.einsum(
        "esf,edf->esd",
        hidden,
        down_piece,
        preferred_element_type=jnp.float32,
    ).astype(jnp.bfloat16)
    returned = exchange_exp(expert_rows.reshape(EXPERTS, CAP, D), 2)
    combine = jnp.sum(
        jnp.where(
            jnp.arange(EXPERTS * CAP, dtype=jnp.int32)[None, None, :] == target.reshape(row_count, TOP)[:, :, None],
            gate_probs[0][:, :, None],
            0.0,
        ),
        axis=1,
    )
    mixture = jnp.dot(
        combine,
        returned.reshape(EXPERTS * CAP, D).astype(jnp.float32),
        precision=lax.Precision.HIGHEST,
        preferred_element_type=jnp.float32,
    )
    layer_out = (residual.astype(jnp.float32) + mixture).astype(jnp.bfloat16)
    return (attention_out[None], layer_out[None])


def solution(mesh):
    n_ctx = mesh.shape["ctx"]
    split = jax.sharding.Mesh(
        mesh.devices.reshape(n_ctx // 4, 2, 2, mesh.shape["exp"]), CTX_AXES + ("exp",)
    )
    return jax.shard_map(
        shards,
        mesh=split,
        in_specs=(
            P("exp", CTX_AXES, None),
            P("exp", CTX_AXES, None),
            P("exp", CTX_AXES, None),
            P("exp", CTX_AXES, None),
            P("exp", CTX_AXES, None),
            P(),
            P(),
            P("exp", CTX_AXES, None),
            P("exp", CTX_AXES, None),
            P("exp", CTX_AXES, None),
            P("exp", CTX_AXES, None),
            P("exp", CTX_AXES, None),
        ),
        out_specs=(P("exp", CTX_AXES, None), P("exp", CTX_AXES, None)),
        check_vma=False,
    )
```

```python
import functools

import jax
import jax.numpy as jnp
from jax import lax
from jax.experimental import pallas as pl
from jax.experimental.pallas import tpu as pltpu
from jax.sharding import PartitionSpec as P

D = 1024
HEADS = 8
KV_HEADS = 2
EXPERTS = 8
TOP = 2
TILE = 32
CAP = 72


def rms_scale(row_block, gain):
    widened = row_block.astype(jnp.float32)
    inverse = lax.rsqrt(jnp.mean(widened * widened, axis=-1, keepdims=True) + 1e-05)
    return widened * inverse * gain


CTX_AXES = ("z", "yh", "core")


MESH = pl.DeviceIdType.MESH


def gather_kernel(n_z, shard_ref, out_ref, local_sem, send_sem, recv_sem):
    z = lax.axis_index("z")
    yh = lax.axis_index("yh")
    core = lax.axis_index("core")
    ex = lax.axis_index("exp")

    def slot(zz, hh, cc):
        return (zz * 2 + hh) * 2 + cc

    def ring(offset):
        return lax.rem(z + offset + 4 * n_z, n_z)

    partner_h = 1 - yh
    sibling_c = 1 - core
    to_right = (ring(1), yh, core, ex)
    to_left = (ring(-1), yh, core, ex)
    to_partner = (z, partner_h, core, ex)
    to_sibling = (z, yh, sibling_c, ex)
    barrier = pltpu.get_barrier_semaphore()
    for dev in (to_right, to_left, to_partner, to_sibling):
        pl.semaphore_signal(barrier, 1, device_id=dev, device_id_type=MESH)
    pl.semaphore_wait(barrier, 4)

    me = slot(z, yh, core)
    own = pltpu.make_async_copy(shard_ref, out_ref.at[me], local_sem)
    own.start()
    sends = []

    def send(src, s, dev, k):
        copy = pltpu.make_async_remote_copy(
            src, out_ref.at[s], send_sem.at[k, s], recv_sem.at[s], device_id=dev, device_id_type=MESH
        )
        copy.start()
        sends.append(copy)

    def arrive(s):
        pltpu.make_async_remote_copy(
            out_ref.at[s], out_ref.at[s], send_sem.at[0, s], recv_sem.at[s],
            device_id=to_right, device_id_type=MESH,
        ).wait_recv()

    for k, dev in enumerate((to_right, to_left, to_partner, to_sibling)):
        send(shard_ref, me, dev, k)
    half = n_z // 2
    for t in range(1, half + 1):
        s = slot(ring(-t), yh, core)
        arrive(s)
        if t < half:
            send(out_ref.at[s], s, to_right, 0)
        send(out_ref.at[s], s, to_partner, 2)
        send(out_ref.at[s], s, to_sibling, 3)
        if t < n_z - half:
            s = slot(ring(t), yh, core)
            arrive(s)
            if t < n_z - half - 1:
                send(out_ref.at[s], s, to_left, 1)
            send(out_ref.at[s], s, to_partner, 2)
            send(out_ref.at[s], s, to_sibling, 3)
    partner_order = [0]
    for t in range(1, half + 1):
        partner_order.append(-t)
        if t < n_z - half:
            partner_order.append(t)
    for offset in partner_order:
        s = slot(ring(offset), partner_h, core)
        arrive(s)
        send(out_ref.at[s], s, to_sibling, 3)
    for hh in (yh, partner_h):
        for offset in partner_order:
            arrive(slot(ring(offset), hh, sibling_c))
    own.wait()
    for copy in sends:
        copy.wait_send()


def gather_ctx_kernel(block):
    n_z = lax.axis_size("z")
    n_all = n_z * 4
    return pl.pallas_call(
        functools.partial(gather_kernel, n_z),
        out_shape=jax.ShapeDtypeStruct((n_all,) + block.shape, block.dtype),
        in_specs=[pl.BlockSpec(memory_space=pl.ANY)],
        out_specs=pl.BlockSpec(memory_space=pl.ANY),
        scratch_shapes=[
            pltpu.SemaphoreType.DMA(()),
            pltpu.SemaphoreType.DMA((4, n_all)),
            pltpu.SemaphoreType.DMA((n_all,)),
        ],
        compiler_params=pltpu.CompilerParams(collective_id=0, has_side_effects=True),
    )(block)


def exchange_kernel(n_exp, chunk_ref, out_ref, local_sem, send_sem, recv_sem):
    me = lax.axis_index("exp")
    z = lax.axis_index("z")
    yh = lax.axis_index("yh")
    core = lax.axis_index("core")

    def peer(offset):
        return lax.rem(me + offset, n_exp)

    barrier = pltpu.get_barrier_semaphore()
    for offset in range(1, n_exp):
        pl.semaphore_signal(barrier, 1, device_id=(z, yh, core, peer(offset)), device_id_type=MESH)
    pl.semaphore_wait(barrier, n_exp - 1)
    own = pltpu.make_async_copy(chunk_ref.at[me], out_ref.at[me], local_sem)
    own.start()
    sends = []
    for offset in range(1, n_exp):
        target = peer(offset)
        copy = pltpu.make_async_remote_copy(
            chunk_ref.at[target], out_ref.at[me], send_sem.at[offset], recv_sem.at[me],
            device_id=(z, yh, core, target), device_id_type=MESH,
        )
        copy.start()
        sends.append(copy)
    for offset in range(1, n_exp):
        source = peer(n_exp - offset)
        pltpu.make_async_remote_copy(
            out_ref.at[source], out_ref.at[source], send_sem.at[offset], recv_sem.at[source],
            device_id=(z, yh, core, source), device_id_type=MESH,
        ).wait_recv()
    own.wait()
    for copy in sends:
        copy.wait_send()


def exchange_exp(chunks, collective_id):
    n_exp = chunks.shape[0]
    return pl.pallas_call(
        functools.partial(exchange_kernel, n_exp),
        out_shape=jax.ShapeDtypeStruct(chunks.shape, chunks.dtype),
        in_specs=[pl.BlockSpec(memory_space=pl.ANY)],
        out_specs=pl.BlockSpec(memory_space=pl.ANY),
        scratch_shapes=[
            pltpu.SemaphoreType.DMA(()),
            pltpu.SemaphoreType.DMA((n_exp,)),
            pltpu.SemaphoreType.DMA((n_exp,)),
        ],
        compiler_params=pltpu.CompilerParams(collective_id=collective_id, has_side_effects=True),
    )(chunks)


KEY_BLOCK = 128


def attention_kernel(groups, head_size, flag_ref, q_ref, kv_ref, mask_ref, out_ref, top_ref, sum_ref, acc_ref):
    n_blocks = flag_ref.shape[0]
    kv_heads = kv_ref.shape[1] // (2 * head_size)
    heads = kv_heads * groups
    value_at = kv_heads * head_size
    scale = head_size ** (-0.5)
    top_ref[...] = jnp.full(top_ref.shape, -1e30, jnp.float32)
    sum_ref[...] = jnp.zeros(sum_ref.shape, jnp.float32)
    acc_ref[...] = jnp.zeros(acc_ref.shape, jnp.float32)

    def allowed_block(j):
        tile_count = mask_ref.shape[1]
        tile_at = lax.broadcasted_iota(jnp.int32, (tile_count, KEY_BLOCK), 0)
        column_tile = lax.broadcasted_iota(jnp.int32, (tile_count, KEY_BLOCK), 1) // TILE
        spread = (tile_at == j * (KEY_BLOCK // TILE) + column_tile).astype(jnp.bfloat16)
        return jnp.dot(mask_ref[...], spread, preferred_element_type=jnp.float32) > 0

    def scores(j, h):
        rows = pl.ds(pl.multiple_of(j * KEY_BLOCK, KEY_BLOCK), KEY_BLOCK)
        key = kv_ref[rows, pl.ds((h // groups) * head_size, head_size)]
        query = q_ref[:, pl.ds(h * head_size, head_size)]
        raw = lax.dot_general(
            query, key, (((1,), (1,)), ((), ())), preferred_element_type=jnp.float32
        )
        return raw * scale

    def first_pass(j, carry):
        @pl.when(flag_ref[j] > 0)
        def _():
            allowed = allowed_block(j)
            for h in range(heads):
                s = scores(j, h)
                top_ref[h] = jnp.maximum(top_ref[h], jnp.where(allowed, s, -1e30))
        return carry

    lax.fori_loop(0, n_blocks, first_pass, 0)
    for h in range(heads):
        top_ref[h] = jnp.broadcast_to(jnp.max(top_ref[h], axis=1, keepdims=True), top_ref.shape[1:])

    def second_pass(j, carry):
        @pl.when(flag_ref[j] > 0)
        def _():
            rows = pl.ds(pl.multiple_of(j * KEY_BLOCK, KEY_BLOCK), KEY_BLOCK)
            allowed = allowed_block(j)
            for h in range(heads):
                s = scores(j, h)
                weights = jnp.where(allowed, jnp.exp(s - top_ref[h]), 0.0)
                sum_ref[h] += weights
                value = kv_ref[rows, pl.ds(value_at + (h // groups) * head_size, head_size)]
                acc_ref[h] += jnp.dot(
                    weights.astype(jnp.bfloat16), value, preferred_element_type=jnp.float32
                )
        return carry

    lax.fori_loop(0, n_blocks, second_pass, 0)
    for h in range(heads):
        denominator = jnp.sum(sum_ref[h], axis=1, keepdims=True)
        out_ref[:, pl.ds(h * head_size, head_size)] = (acc_ref[h] / denominator).astype(out_ref.dtype)


def block_attention(query_rows, kv_rows, mask_block, groups, head_size):
    row_count = query_rows.shape[0]
    key_count = kv_rows.shape[0]
    heads = query_rows.shape[1] // head_size
    allowed = jnp.repeat(mask_block, TILE, axis=0).astype(jnp.bfloat16)
    tiles_per_block = KEY_BLOCK // TILE
    flags = jnp.max(
        mask_block.reshape(mask_block.shape[0], -1, tiles_per_block), axis=(0, 2)
    ).astype(jnp.int32)
    vmem = pl.BlockSpec(memory_space=pltpu.VMEM)
    return pl.pallas_call(
        functools.partial(attention_kernel, groups, head_size),
        out_shape=jax.ShapeDtypeStruct((row_count, heads * head_size), jnp.bfloat16),
        in_specs=[pl.BlockSpec(memory_space=pltpu.SMEM), vmem, vmem, vmem],
        out_specs=vmem,
        scratch_shapes=[
            pltpu.VMEM((heads, row_count, KEY_BLOCK), jnp.float32),
            pltpu.VMEM((heads, row_count, KEY_BLOCK), jnp.float32),
            pltpu.VMEM((heads, row_count, head_size), jnp.float32),
        ],
    )(flags, query_rows, kv_rows, allowed)


def shards(
    hidden_in,
    queries,
    key_proj,
    value_proj,
    tile_mask,
    out_weight,
    moe_gain,
    gate_weight,
    up_weight,
    down_weight,
    expert_ids,
    gate_probs,
):
    query_rows = queries[0]
    row_count = query_rows.shape[0]
    groups = HEADS // KV_HEADS
    head_size = D // HEADS
    query_heads = query_rows.reshape(row_count, KV_HEADS, groups, head_size)
    mask_block = tile_mask[0]
    kv_width = key_proj.shape[-1]
    kv_local = jnp.concatenate([key_proj[0], value_proj[0]], axis=-1)
    kv_piece = gather_ctx_kernel(kv_local).reshape(-1, 2 * kv_width)
    attended = block_attention(query_rows, kv_piece, mask_block, groups, head_size)
    projected = jnp.dot(attended, out_weight, preferred_element_type=jnp.float32)
    attention_out = projected.astype(jnp.bfloat16)
    residual = (hidden_in[0].astype(jnp.float32) + projected).astype(jnp.bfloat16)
    normed = rms_scale(residual, moe_gain).astype(jnp.bfloat16)
    id_row = expert_ids[0].reshape(-1)
    onehot = (id_row[:, None] == jnp.arange(EXPERTS, dtype=jnp.int32)[None, :]).astype(jnp.int32)
    before = jnp.cumsum(onehot, axis=0) - onehot
    slot_index = jnp.sum(before * onehot, axis=1)
    target = id_row * CAP + slot_index
    selector = (jnp.arange(EXPERTS * CAP, dtype=jnp.int32)[:, None] == target[None, :]).astype(
        jnp.bfloat16
    )
    repeated = jnp.repeat(normed, TOP, axis=0)
    outgoing = (
        jnp.dot(selector, repeated, preferred_element_type=jnp.float32)
        .astype(jnp.bfloat16)
        .reshape(EXPERTS, CAP, D)
    )
    arrived = exchange_exp(outgoing, 1).reshape(1, EXPERTS * CAP, D)
    ff = gate_weight.shape[-1]
    half = ff // 2
    core = lax.axis_index("core")
    swap = [(0, 1), (1, 0)]

    def halves(part):
        columns = slice(part * half, (part + 1) * half)
        return jnp.concatenate([w[0][:, columns] for w in (gate_weight, up_weight, down_weight)], axis=-1)

    own_half = jnp.where(core == 0, halves(0), halves(1))
    other_half = jnp.where(core == 0, halves(1), halves(0))
    from_sibling = lax.ppermute(other_half, "core", swap)
    chip_rows = jnp.where(
        core == 0,
        jnp.concatenate([own_half, from_sibling], axis=0),
        jnp.concatenate([from_sibling, own_half], axis=0),
    )
    weight_piece = lax.all_gather(chip_rows, CTX_AXES[:2], axis=0, tiled=True)
    gate_piece = weight_piece[:, :half]
    up_piece = weight_piece[:, half : 2 * half]
    down_piece = weight_piece[:, 2 * half :]
    own_tokens = arrived[0]
    both_tokens = jnp.concatenate([own_tokens, lax.ppermute(own_tokens, "core", swap)], axis=0)
    gate_sum = jnp.dot(both_tokens, gate_piece, preferred_element_type=jnp.float32)
    up_sum = jnp.dot(both_tokens, up_piece, preferred_element_type=jnp.float32)
    hidden = (jax.nn.silu(gate_sum) * up_sum).astype(jnp.bfloat16)
    partial = lax.dot_general(
        hidden, down_piece, (((1,), (1,)), ((), ())), preferred_element_type=jnp.float32
    )
    slot_rows = own_tokens.shape[0]
    expert_rows = (
        partial[:slot_rows] + lax.ppermute(partial[slot_rows:], "core", swap)
    ).astype(jnp.bfloat16)
    returned = exchange_exp(expert_rows.reshape(EXPERTS, CAP, D), 2)
    combine = jnp.sum(
        jnp.where(
            jnp.arange(EXPERTS * CAP, dtype=jnp.int32)[None, None, :] == target.reshape(row_count, TOP)[:, :, None],
            gate_probs[0][:, :, None],
            0.0,
        ),
        axis=1,
    )
    mixture = jnp.dot(
        combine,
        returned.reshape(EXPERTS * CAP, D).astype(jnp.float32),
        precision=lax.Precision.HIGHEST,
        preferred_element_type=jnp.float32,
    )
    layer_out = (residual.astype(jnp.float32) + mixture).astype(jnp.bfloat16)
    return (attention_out[None], layer_out[None])


def solution(mesh):
    n_ctx = mesh.shape["ctx"]
    split = jax.sharding.Mesh(
        mesh.devices.reshape(n_ctx // 4, 2, 2, mesh.shape["exp"]), CTX_AXES + ("exp",)
    )
    return jax.shard_map(
        shards,
        mesh=split,
        in_specs=(
            P("exp", CTX_AXES, None),
            P("exp", CTX_AXES, None),
            P("exp", CTX_AXES, None),
            P("exp", CTX_AXES, None),
            P("exp", CTX_AXES, None),
            P(),
            P(),
            P("exp", CTX_AXES, None),
            P("exp", CTX_AXES, None),
            P("exp", CTX_AXES, None),
            P("exp", CTX_AXES, None),
            P("exp", CTX_AXES, None),
        ),
        out_specs=(P("exp", CTX_AXES, None), P("exp", CTX_AXES, None)),
        check_vma=False,
    )
```

```python
import functools

import jax
import jax.numpy as jnp
from jax import lax
from jax.experimental import pallas as pl
from jax.experimental.pallas import tpu as pltpu
from jax.sharding import PartitionSpec as P

D = 1024
HEADS = 8
KV_HEADS = 2
EXPERTS = 8
TOP = 2
TILE = 32
CAP = 72


def rms_scale(row_block, gain):
    widened = row_block.astype(jnp.float32)
    inverse = lax.rsqrt(jnp.mean(widened * widened, axis=-1, keepdims=True) + 1e-05)
    return widened * inverse * gain


CTX_AXES = ("z", "yh", "core")


MESH = pl.DeviceIdType.MESH


def gather_kernel(n_z, shard_ref, out_ref, local_sem, send_sem, recv_sem):
    z = lax.axis_index("z")
    yh = lax.axis_index("yh")
    core = lax.axis_index("core")
    ex = lax.axis_index("exp")

    def slot(zz, hh, cc):
        return (zz * 2 + hh) * 2 + cc

    def ring(offset):
        return lax.rem(z + offset + 4 * n_z, n_z)

    partner_h = 1 - yh
    sibling_c = 1 - core
    to_right = (ring(1), yh, core, ex)
    to_left = (ring(-1), yh, core, ex)
    to_partner = (z, partner_h, core, ex)
    to_sibling = (z, yh, sibling_c, ex)
    barrier = pltpu.get_barrier_semaphore()
    for dev in (to_right, to_left, to_partner, to_sibling):
        pl.semaphore_signal(barrier, 1, device_id=dev, device_id_type=MESH)
    pl.semaphore_wait(barrier, 4)

    me = slot(z, yh, core)
    own = pltpu.make_async_copy(shard_ref, out_ref.at[me], local_sem)
    own.start()
    sends = []

    def send(src, s, dev, k):
        copy = pltpu.make_async_remote_copy(
            src, out_ref.at[s], send_sem.at[k, s], recv_sem.at[s], device_id=dev, device_id_type=MESH
        )
        copy.start()
        sends.append(copy)

    def arrive(s):
        pltpu.make_async_remote_copy(
            out_ref.at[s], out_ref.at[s], send_sem.at[0, s], recv_sem.at[s],
            device_id=to_right, device_id_type=MESH,
        ).wait_recv()

    for k, dev in enumerate((to_right, to_left, to_partner, to_sibling)):
        send(shard_ref, me, dev, k)
    half = n_z // 2
    for t in range(1, half + 1):
        s = slot(ring(-t), yh, core)
        arrive(s)
        if t < half:
            send(out_ref.at[s], s, to_right, 0)
        send(out_ref.at[s], s, to_partner, 2)
        send(out_ref.at[s], s, to_sibling, 3)
        if t < n_z - half:
            s = slot(ring(t), yh, core)
            arrive(s)
            if t < n_z - half - 1:
                send(out_ref.at[s], s, to_left, 1)
            send(out_ref.at[s], s, to_partner, 2)
            send(out_ref.at[s], s, to_sibling, 3)
    partner_order = [0]
    for t in range(1, half + 1):
        partner_order.append(-t)
        if t < n_z - half:
            partner_order.append(t)
    for offset in partner_order:
        s = slot(ring(offset), partner_h, core)
        arrive(s)
        send(out_ref.at[s], s, to_sibling, 3)
    for hh in (yh, partner_h):
        for offset in partner_order:
            arrive(slot(ring(offset), hh, sibling_c))
    own.wait()
    for copy in sends:
        copy.wait_send()


def gather_ctx_kernel(block, collective_id=0):
    n_z = lax.axis_size("z")
    n_all = n_z * 4
    return pl.pallas_call(
        functools.partial(gather_kernel, n_z),
        out_shape=jax.ShapeDtypeStruct((n_all,) + block.shape, block.dtype),
        in_specs=[pl.BlockSpec(memory_space=pl.ANY)],
        out_specs=pl.BlockSpec(memory_space=pl.ANY),
        scratch_shapes=[
            pltpu.SemaphoreType.DMA(()),
            pltpu.SemaphoreType.DMA((4, n_all)),
            pltpu.SemaphoreType.DMA((n_all,)),
        ],
        compiler_params=pltpu.CompilerParams(collective_id=collective_id, has_side_effects=True),
    )(block)


def exchange_kernel(n_exp, chunk_ref, out_ref, local_sem, send_sem, recv_sem):
    me = lax.axis_index("exp")
    z = lax.axis_index("z")
    yh = lax.axis_index("yh")
    core = lax.axis_index("core")

    def peer(offset):
        return lax.rem(me + offset, n_exp)

    barrier = pltpu.get_barrier_semaphore()
    for offset in range(1, n_exp):
        pl.semaphore_signal(barrier, 1, device_id=(z, yh, core, peer(offset)), device_id_type=MESH)
    pl.semaphore_wait(barrier, n_exp - 1)
    own = pltpu.make_async_copy(chunk_ref.at[me], out_ref.at[me], local_sem)
    own.start()
    sends = []
    for offset in range(1, n_exp):
        target = peer(offset)
        copy = pltpu.make_async_remote_copy(
            chunk_ref.at[target], out_ref.at[me], send_sem.at[offset], recv_sem.at[me],
            device_id=(z, yh, core, target), device_id_type=MESH,
        )
        copy.start()
        sends.append(copy)
    for offset in range(1, n_exp):
        source = peer(n_exp - offset)
        pltpu.make_async_remote_copy(
            out_ref.at[source], out_ref.at[source], send_sem.at[offset], recv_sem.at[source],
            device_id=(z, yh, core, source), device_id_type=MESH,
        ).wait_recv()
    own.wait()
    for copy in sends:
        copy.wait_send()


def exchange_exp(chunks, collective_id):
    n_exp = chunks.shape[0]
    return pl.pallas_call(
        functools.partial(exchange_kernel, n_exp),
        out_shape=jax.ShapeDtypeStruct(chunks.shape, chunks.dtype),
        in_specs=[pl.BlockSpec(memory_space=pl.ANY)],
        out_specs=pl.BlockSpec(memory_space=pl.ANY),
        scratch_shapes=[
            pltpu.SemaphoreType.DMA(()),
            pltpu.SemaphoreType.DMA((n_exp,)),
            pltpu.SemaphoreType.DMA((n_exp,)),
        ],
        compiler_params=pltpu.CompilerParams(collective_id=collective_id, has_side_effects=True),
    )(chunks)


KEY_BLOCK = 128


def attention_kernel(groups, head_size, flag_ref, q_ref, kv_ref, mask_ref, out_ref, top_ref, sum_ref, acc_ref):
    n_blocks = flag_ref.shape[0]
    kv_heads = kv_ref.shape[1] // (2 * head_size)
    heads = kv_heads * groups
    value_at = kv_heads * head_size
    scale = head_size ** (-0.5)
    top_ref[...] = jnp.full(top_ref.shape, -1e30, jnp.float32)
    sum_ref[...] = jnp.zeros(sum_ref.shape, jnp.float32)
    acc_ref[...] = jnp.zeros(acc_ref.shape, jnp.float32)

    def allowed_block(j):
        tile_count = mask_ref.shape[1]
        tile_at = lax.broadcasted_iota(jnp.int32, (tile_count, KEY_BLOCK), 0)
        column_tile = lax.broadcasted_iota(jnp.int32, (tile_count, KEY_BLOCK), 1) // TILE
        spread = (tile_at == j * (KEY_BLOCK // TILE) + column_tile).astype(jnp.bfloat16)
        return jnp.dot(mask_ref[...], spread, preferred_element_type=jnp.float32) > 0

    def scores(j, h):
        rows = pl.ds(pl.multiple_of(j * KEY_BLOCK, KEY_BLOCK), KEY_BLOCK)
        key = kv_ref[rows, pl.ds((h // groups) * head_size, head_size)]
        query = q_ref[:, pl.ds(h * head_size, head_size)]
        raw = lax.dot_general(
            query, key, (((1,), (1,)), ((), ())), preferred_element_type=jnp.float32
        )
        return raw * scale

    def first_pass(j, carry):
        @pl.when(flag_ref[j] > 0)
        def _():
            allowed = allowed_block(j)
            for h in range(heads):
                s = scores(j, h)
                top_ref[h] = jnp.maximum(top_ref[h], jnp.where(allowed, s, -1e30))
        return carry

    lax.fori_loop(0, n_blocks, first_pass, 0)
    for h in range(heads):
        top_ref[h] = jnp.broadcast_to(jnp.max(top_ref[h], axis=1, keepdims=True), top_ref.shape[1:])

    def second_pass(j, carry):
        @pl.when(flag_ref[j] > 0)
        def _():
            rows = pl.ds(pl.multiple_of(j * KEY_BLOCK, KEY_BLOCK), KEY_BLOCK)
            allowed = allowed_block(j)
            for h in range(heads):
                s = scores(j, h)
                weights = jnp.where(allowed, jnp.exp(s - top_ref[h]), 0.0)
                sum_ref[h] += weights
                value = kv_ref[rows, pl.ds(value_at + (h // groups) * head_size, head_size)]
                acc_ref[h] += jnp.dot(
                    weights.astype(jnp.bfloat16), value, preferred_element_type=jnp.float32
                )
        return carry

    lax.fori_loop(0, n_blocks, second_pass, 0)
    for h in range(heads):
        denominator = jnp.sum(sum_ref[h], axis=1, keepdims=True)
        out_ref[:, pl.ds(h * head_size, head_size)] = (acc_ref[h] / denominator).astype(out_ref.dtype)


def block_attention(query_rows, kv_rows, mask_block, groups, head_size):
    row_count = query_rows.shape[0]
    key_count = kv_rows.shape[0]
    heads = query_rows.shape[1] // head_size
    allowed = jnp.repeat(mask_block, TILE, axis=0).astype(jnp.bfloat16)
    tiles_per_block = KEY_BLOCK // TILE
    flags = jnp.max(
        mask_block.reshape(mask_block.shape[0], -1, tiles_per_block), axis=(0, 2)
    ).astype(jnp.int32)
    vmem = pl.BlockSpec(memory_space=pltpu.VMEM)
    return pl.pallas_call(
        functools.partial(attention_kernel, groups, head_size),
        out_shape=jax.ShapeDtypeStruct((row_count, heads * head_size), jnp.bfloat16),
        in_specs=[pl.BlockSpec(memory_space=pltpu.SMEM), vmem, vmem, vmem],
        out_specs=vmem,
        scratch_shapes=[
            pltpu.VMEM((heads, row_count, KEY_BLOCK), jnp.float32),
            pltpu.VMEM((heads, row_count, KEY_BLOCK), jnp.float32),
            pltpu.VMEM((heads, row_count, head_size), jnp.float32),
        ],
    )(flags, query_rows, kv_rows, allowed)


def shards(
    hidden_in,
    queries,
    key_proj,
    value_proj,
    tile_mask,
    out_weight,
    moe_gain,
    gate_weight,
    up_weight,
    down_weight,
    expert_ids,
    gate_probs,
):
    query_rows = queries[0]
    row_count = query_rows.shape[0]
    groups = HEADS // KV_HEADS
    head_size = D // HEADS
    query_heads = query_rows.reshape(row_count, KV_HEADS, groups, head_size)
    mask_block = tile_mask[0]
    kv_width = key_proj.shape[-1]
    kv_local = jnp.concatenate([key_proj[0], value_proj[0]], axis=-1)
    kv_piece = gather_ctx_kernel(kv_local).reshape(-1, 2 * kv_width)
    attended = block_attention(query_rows, kv_piece, mask_block, groups, head_size)
    projected = jnp.dot(attended, out_weight, preferred_element_type=jnp.float32)
    attention_out = projected.astype(jnp.bfloat16)
    residual = (hidden_in[0].astype(jnp.float32) + projected).astype(jnp.bfloat16)
    normed = rms_scale(residual, moe_gain).astype(jnp.bfloat16)
    id_row = expert_ids[0].reshape(-1)
    onehot = (id_row[:, None] == jnp.arange(EXPERTS, dtype=jnp.int32)[None, :]).astype(jnp.int32)
    before = jnp.cumsum(onehot, axis=0) - onehot
    slot_index = jnp.sum(before * onehot, axis=1)
    target = id_row * CAP + slot_index
    selector = (jnp.arange(EXPERTS * CAP, dtype=jnp.int32)[:, None] == target[None, :]).astype(
        jnp.bfloat16
    )
    repeated = jnp.repeat(normed, TOP, axis=0)
    outgoing = (
        jnp.dot(selector, repeated, preferred_element_type=jnp.float32)
        .astype(jnp.bfloat16)
        .reshape(EXPERTS, CAP, D)
    )
    arrived = exchange_exp(outgoing, 1).reshape(1, EXPERTS * CAP, D)
    ff = gate_weight.shape[-1]
    weight_local = jnp.concatenate([gate_weight[0], up_weight[0], down_weight[0]], axis=-1)
    weight_piece = gather_ctx_kernel(weight_local, 3).reshape(1, -1, weight_local.shape[-1])
    gate_piece = weight_piece[..., :ff]
    up_piece = weight_piece[..., ff : 2 * ff]
    down_piece = weight_piece[..., 2 * ff :]
    gate_sum = jnp.einsum("esd,edf->esf", arrived, gate_piece, preferred_element_type=jnp.float32)
    up_sum = jnp.einsum("esd,edf->esf", arrived, up_piece, preferred_element_type=jnp.float32)
    hidden = (jax.nn.silu(gate_sum) * up_sum).astype(jnp.bfloat16)
    expert_rows = jnp.einsum(
        "esf,edf->esd",
        hidden,
        down_piece,
        preferred_element_type=jnp.float32,
    ).astype(jnp.bfloat16)
    returned = exchange_exp(expert_rows.reshape(EXPERTS, CAP, D), 2)
    combine = jnp.sum(
        jnp.where(
            jnp.arange(EXPERTS * CAP, dtype=jnp.int32)[None, None, :] == target.reshape(row_count, TOP)[:, :, None],
            gate_probs[0][:, :, None],
            0.0,
        ),
        axis=1,
    )
    mixture = jnp.dot(
        combine,
        returned.reshape(EXPERTS * CAP, D).astype(jnp.float32),
        precision=lax.Precision.HIGHEST,
        preferred_element_type=jnp.float32,
    )
    layer_out = (residual.astype(jnp.float32) + mixture).astype(jnp.bfloat16)
    return (attention_out[None], layer_out[None])


def solution(mesh):
    n_ctx = mesh.shape["ctx"]
    split = jax.sharding.Mesh(
        mesh.devices.reshape(n_ctx // 4, 2, 2, mesh.shape["exp"]), CTX_AXES + ("exp",)
    )
    return jax.shard_map(
        shards,
        mesh=split,
        in_specs=(
            P("exp", CTX_AXES, None),
            P("exp", CTX_AXES, None),
            P("exp", CTX_AXES, None),
            P("exp", CTX_AXES, None),
            P("exp", CTX_AXES, None),
            P(),
            P(),
            P("exp", CTX_AXES, None),
            P("exp", CTX_AXES, None),
            P("exp", CTX_AXES, None),
            P("exp", CTX_AXES, None),
            P("exp", CTX_AXES, None),
        ),
        out_specs=(P("exp", CTX_AXES, None), P("exp", CTX_AXES, None)),
        check_vma=False,
    )
```

```python
import functools

import jax
import jax.numpy as jnp
from jax import lax
from jax.experimental import pallas as pl
from jax.experimental.pallas import tpu as pltpu
from jax.sharding import PartitionSpec as P

D = 1024
HEADS = 8
KV_HEADS = 2
EXPERTS = 8
TOP = 2
TILE = 32
CAP = 72


def rms_scale(row_block, gain):
    widened = row_block.astype(jnp.float32)
    inverse = lax.rsqrt(jnp.mean(widened * widened, axis=-1, keepdims=True) + 1e-05)
    return widened * inverse * gain


CTX_AXES = ("z", "yh", "core")


MESH = pl.DeviceIdType.MESH


def gather_kernel(n_z, shard_ref, out_ref, local_sem, send_sem, recv_sem):
    z = lax.axis_index("z")
    yh = lax.axis_index("yh")
    core = lax.axis_index("core")
    ex = lax.axis_index("exp")

    def slot(zz, hh, cc):
        return (zz * 2 + hh) * 2 + cc

    def ring(offset):
        return lax.rem(z + offset + 4 * n_z, n_z)

    partner_h = 1 - yh
    sibling_c = 1 - core
    to_right = (ring(1), yh, core, ex)
    to_left = (ring(-1), yh, core, ex)
    to_partner = (z, partner_h, core, ex)
    to_sibling = (z, yh, sibling_c, ex)
    barrier = pltpu.get_barrier_semaphore()
    for dev in (to_right, to_left, to_partner, to_sibling):
        pl.semaphore_signal(barrier, 1, device_id=dev, device_id_type=MESH)
    pl.semaphore_wait(barrier, 4)

    me = slot(z, yh, core)
    own = pltpu.make_async_copy(shard_ref, out_ref.at[me], local_sem)
    own.start()
    sends = []

    def send(src, s, dev, k):
        copy = pltpu.make_async_remote_copy(
            src, out_ref.at[s], send_sem.at[k, s], recv_sem.at[s], device_id=dev, device_id_type=MESH
        )
        copy.start()
        sends.append(copy)

    def arrive(s):
        pltpu.make_async_remote_copy(
            out_ref.at[s], out_ref.at[s], send_sem.at[0, s], recv_sem.at[s],
            device_id=to_right, device_id_type=MESH,
        ).wait_recv()

    for k, dev in enumerate((to_right, to_left, to_partner, to_sibling)):
        send(shard_ref, me, dev, k)
    half = n_z // 2
    for t in range(1, half + 1):
        s = slot(ring(-t), yh, core)
        arrive(s)
        if t < half:
            send(out_ref.at[s], s, to_right, 0)
        send(out_ref.at[s], s, to_partner, 2)
        send(out_ref.at[s], s, to_sibling, 3)
        if t < n_z - half:
            s = slot(ring(t), yh, core)
            arrive(s)
            if t < n_z - half - 1:
                send(out_ref.at[s], s, to_left, 1)
            send(out_ref.at[s], s, to_partner, 2)
            send(out_ref.at[s], s, to_sibling, 3)
    partner_order = [0]
    for t in range(1, half + 1):
        partner_order.append(-t)
        if t < n_z - half:
            partner_order.append(t)
    for offset in partner_order:
        s = slot(ring(offset), partner_h, core)
        arrive(s)
        send(out_ref.at[s], s, to_sibling, 3)
    for hh in (yh, partner_h):
        for offset in partner_order:
            arrive(slot(ring(offset), hh, sibling_c))
    own.wait()
    for copy in sends:
        copy.wait_send()


def gather_ctx_kernel(block):
    n_z = lax.axis_size("z")
    n_all = n_z * 4
    return pl.pallas_call(
        functools.partial(gather_kernel, n_z),
        out_shape=jax.ShapeDtypeStruct((n_all,) + block.shape, block.dtype),
        in_specs=[pl.BlockSpec(memory_space=pl.ANY)],
        out_specs=pl.BlockSpec(memory_space=pl.ANY),
        scratch_shapes=[
            pltpu.SemaphoreType.DMA(()),
            pltpu.SemaphoreType.DMA((4, n_all)),
            pltpu.SemaphoreType.DMA((n_all,)),
        ],
        compiler_params=pltpu.CompilerParams(collective_id=0, has_side_effects=True),
    )(block)


def exchange_kernel(n_exp, chunk_ref, out_ref, local_sem, send_sem, recv_sem):
    me = lax.axis_index("exp")
    z = lax.axis_index("z")
    yh = lax.axis_index("yh")
    core = lax.axis_index("core")

    def peer(offset):
        return lax.rem(me + offset, n_exp)

    barrier = pltpu.get_barrier_semaphore()
    for offset in range(1, n_exp):
        pl.semaphore_signal(barrier, 1, device_id=(z, yh, core, peer(offset)), device_id_type=MESH)
    pl.semaphore_wait(barrier, n_exp - 1)
    own = pltpu.make_async_copy(chunk_ref.at[me], out_ref.at[me], local_sem)
    own.start()
    sends = []
    for offset in range(1, n_exp):
        target = peer(offset)
        copy = pltpu.make_async_remote_copy(
            chunk_ref.at[target], out_ref.at[me], send_sem.at[offset], recv_sem.at[me],
            device_id=(z, yh, core, target), device_id_type=MESH,
        )
        copy.start()
        sends.append(copy)
    for offset in range(1, n_exp):
        source = peer(n_exp - offset)
        pltpu.make_async_remote_copy(
            out_ref.at[source], out_ref.at[source], send_sem.at[offset], recv_sem.at[source],
            device_id=(z, yh, core, source), device_id_type=MESH,
        ).wait_recv()
    own.wait()
    for copy in sends:
        copy.wait_send()


def exchange_exp(chunks, collective_id):
    n_exp = chunks.shape[0]
    return pl.pallas_call(
        functools.partial(exchange_kernel, n_exp),
        out_shape=jax.ShapeDtypeStruct(chunks.shape, chunks.dtype),
        in_specs=[pl.BlockSpec(memory_space=pl.ANY)],
        out_specs=pl.BlockSpec(memory_space=pl.ANY),
        scratch_shapes=[
            pltpu.SemaphoreType.DMA(()),
            pltpu.SemaphoreType.DMA((n_exp,)),
            pltpu.SemaphoreType.DMA((n_exp,)),
        ],
        compiler_params=pltpu.CompilerParams(collective_id=collective_id, has_side_effects=True),
    )(chunks)


KEY_BLOCK = 128


def attention_kernel(groups, head_size, flag_ref, q_ref, kv_ref, mask_ref, out_ref, top_ref, sum_ref, acc_ref):
    n_blocks = flag_ref.shape[0]
    kv_heads = kv_ref.shape[1] // (2 * head_size)
    heads = kv_heads * groups
    value_at = kv_heads * head_size
    scale = head_size ** (-0.5)
    top_ref[...] = jnp.full(top_ref.shape, -1e30, jnp.float32)
    sum_ref[...] = jnp.zeros(sum_ref.shape, jnp.float32)
    acc_ref[...] = jnp.zeros(acc_ref.shape, jnp.float32)

    def allowed_block(j):
        tile_count = mask_ref.shape[1]
        tile_at = lax.broadcasted_iota(jnp.int32, (tile_count, KEY_BLOCK), 0)
        column_tile = lax.broadcasted_iota(jnp.int32, (tile_count, KEY_BLOCK), 1) // TILE
        spread = (tile_at == j * (KEY_BLOCK // TILE) + column_tile).astype(jnp.bfloat16)
        return jnp.dot(mask_ref[...], spread, preferred_element_type=jnp.float32) > 0

    def scores(j, h):
        rows = pl.ds(pl.multiple_of(j * KEY_BLOCK, KEY_BLOCK), KEY_BLOCK)
        key = kv_ref[rows, pl.ds((h // groups) * head_size, head_size)]
        query = q_ref[:, pl.ds(h * head_size, head_size)]
        raw = lax.dot_general(
            query, key, (((1,), (1,)), ((), ())), preferred_element_type=jnp.float32
        )
        return raw * scale

    def first_pass(j, carry):
        @pl.when(flag_ref[j] > 0)
        def _():
            allowed = allowed_block(j)
            for h in range(heads):
                s = scores(j, h)
                top_ref[h] = jnp.maximum(top_ref[h], jnp.where(allowed, s, -1e30))
        return carry

    lax.fori_loop(0, n_blocks, first_pass, 0)
    for h in range(heads):
        top_ref[h] = jnp.broadcast_to(jnp.max(top_ref[h], axis=1, keepdims=True), top_ref.shape[1:])

    def second_pass(j, carry):
        @pl.when(flag_ref[j] > 0)
        def _():
            rows = pl.ds(pl.multiple_of(j * KEY_BLOCK, KEY_BLOCK), KEY_BLOCK)
            allowed = allowed_block(j)
            for h in range(heads):
                s = scores(j, h)
                weights = jnp.where(allowed, jnp.exp(s - top_ref[h]), 0.0)
                sum_ref[h] += weights
                value = kv_ref[rows, pl.ds(value_at + (h // groups) * head_size, head_size)]
                acc_ref[h] += jnp.dot(
                    weights.astype(jnp.bfloat16), value, preferred_element_type=jnp.float32
                )
        return carry

    lax.fori_loop(0, n_blocks, second_pass, 0)
    for h in range(heads):
        denominator = jnp.sum(sum_ref[h], axis=1, keepdims=True)
        out_ref[:, pl.ds(h * head_size, head_size)] = (acc_ref[h] / denominator).astype(out_ref.dtype)


def block_attention(query_rows, kv_rows, mask_block, groups, head_size):
    row_count = query_rows.shape[0]
    key_count = kv_rows.shape[0]
    heads = query_rows.shape[1] // head_size
    allowed = jnp.repeat(mask_block, TILE, axis=0).astype(jnp.bfloat16)
    tiles_per_block = KEY_BLOCK // TILE
    flags = jnp.max(
        mask_block.reshape(mask_block.shape[0], -1, tiles_per_block), axis=(0, 2)
    ).astype(jnp.int32)
    vmem = pl.BlockSpec(memory_space=pltpu.VMEM)
    return pl.pallas_call(
        functools.partial(attention_kernel, groups, head_size),
        out_shape=jax.ShapeDtypeStruct((row_count, heads * head_size), jnp.bfloat16),
        in_specs=[pl.BlockSpec(memory_space=pltpu.SMEM), vmem, vmem, vmem],
        out_specs=vmem,
        scratch_shapes=[
            pltpu.VMEM((heads, row_count, KEY_BLOCK), jnp.float32),
            pltpu.VMEM((heads, row_count, KEY_BLOCK), jnp.float32),
            pltpu.VMEM((heads, row_count, head_size), jnp.float32),
        ],
    )(flags, query_rows, kv_rows, allowed)


def shards(
    hidden_in,
    queries,
    key_proj,
    value_proj,
    tile_mask,
    out_weight,
    moe_gain,
    gate_weight,
    up_weight,
    down_weight,
    expert_ids,
    gate_probs,
):
    query_rows = queries[0]
    row_count = query_rows.shape[0]
    groups = HEADS // KV_HEADS
    head_size = D // HEADS
    query_heads = query_rows.reshape(row_count, KV_HEADS, groups, head_size)
    mask_block = tile_mask[0]
    kv_width = key_proj.shape[-1]
    kv_local = jnp.concatenate([key_proj[0], value_proj[0]], axis=-1)
    kv_piece = gather_ctx_kernel(kv_local).reshape(-1, 2 * kv_width)
    attended = block_attention(query_rows, kv_piece, mask_block, groups, head_size)
    projected = jnp.dot(attended, out_weight, preferred_element_type=jnp.float32)
    attention_out = projected.astype(jnp.bfloat16)
    residual = (hidden_in[0].astype(jnp.float32) + projected).astype(jnp.bfloat16)
    normed = rms_scale(residual, moe_gain).astype(jnp.bfloat16)
    id_row = expert_ids[0].reshape(-1)
    onehot = (id_row[:, None] == jnp.arange(EXPERTS, dtype=jnp.int32)[None, :]).astype(jnp.int32)
    before = jnp.cumsum(onehot, axis=0) - onehot
    slot_index = jnp.sum(before * onehot, axis=1)
    target = id_row * CAP + slot_index
    selector = (jnp.arange(EXPERTS * CAP, dtype=jnp.int32)[:, None] == target[None, :]).astype(
        jnp.bfloat16
    )
    repeated = jnp.repeat(normed, TOP, axis=0)
    outgoing = (
        jnp.dot(selector, repeated, preferred_element_type=jnp.float32)
        .astype(jnp.bfloat16)
        .reshape(EXPERTS, CAP, D)
    )
    arrived = exchange_exp(outgoing, 1).reshape(1, EXPERTS * CAP, D)
    ff = gate_weight.shape[-1]
    half = ff // 2
    core = lax.axis_index("core")
    swap = [(0, 1), (1, 0)]

    def halves(part):
        columns = slice(part * half, (part + 1) * half)
        return jnp.concatenate([w[0][:, columns] for w in (gate_weight, up_weight, down_weight)], axis=-1)

    own_half = jnp.where(core == 0, halves(0), halves(1))
    other_half = jnp.where(core == 0, halves(1), halves(0))
    from_sibling = lax.ppermute(other_half, "core", swap)
    chip_rows = jnp.where(
        core == 0,
        jnp.concatenate([own_half, from_sibling], axis=0),
        jnp.concatenate([from_sibling, own_half], axis=0),
    )
    y_hi = lax.axis_index("yh")
    from_partner = lax.ppermute(chip_rows, "yh", swap)
    slice_rows = jnp.where(
        y_hi == 0,
        jnp.concatenate([chip_rows, from_partner], axis=0),
        jnp.concatenate([from_partner, chip_rows], axis=0),
    )
    weight_piece = lax.all_gather(slice_rows, "z", axis=0, tiled=True)
    gate_piece = weight_piece[:, :half]
    up_piece = weight_piece[:, half : 2 * half]
    down_piece = weight_piece[:, 2 * half :]
    own_tokens = arrived[0]
    both_tokens = jnp.concatenate([own_tokens, lax.ppermute(own_tokens, "core", swap)], axis=0)
    gate_sum = jnp.dot(both_tokens, gate_piece, preferred_element_type=jnp.float32)
    up_sum = jnp.dot(both_tokens, up_piece, preferred_element_type=jnp.float32)
    hidden = (jax.nn.silu(gate_sum) * up_sum).astype(jnp.bfloat16)
    partial = lax.dot_general(
        hidden, down_piece, (((1,), (1,)), ((), ())), preferred_element_type=jnp.float32
    )
    slot_rows = own_tokens.shape[0]
    expert_rows = (
        partial[:slot_rows] + lax.ppermute(partial[slot_rows:], "core", swap)
    ).astype(jnp.bfloat16)
    returned = exchange_exp(expert_rows.reshape(EXPERTS, CAP, D), 2)
    combine = jnp.sum(
        jnp.where(
            jnp.arange(EXPERTS * CAP, dtype=jnp.int32)[None, None, :] == target.reshape(row_count, TOP)[:, :, None],
            gate_probs[0][:, :, None],
            0.0,
        ),
        axis=1,
    )
    mixture = jnp.dot(
        combine,
        returned.reshape(EXPERTS * CAP, D).astype(jnp.float32),
        precision=lax.Precision.HIGHEST,
        preferred_element_type=jnp.float32,
    )
    layer_out = (residual.astype(jnp.float32) + mixture).astype(jnp.bfloat16)
    return (attention_out[None], layer_out[None])


def solution(mesh):
    n_ctx = mesh.shape["ctx"]
    split = jax.sharding.Mesh(
        mesh.devices.reshape(n_ctx // 4, 2, 2, mesh.shape["exp"]), CTX_AXES + ("exp",)
    )
    return jax.shard_map(
        shards,
        mesh=split,
        in_specs=(
            P("exp", CTX_AXES, None),
            P("exp", CTX_AXES, None),
            P("exp", CTX_AXES, None),
            P("exp", CTX_AXES, None),
            P("exp", CTX_AXES, None),
            P(),
            P(),
            P("exp", CTX_AXES, None),
            P("exp", CTX_AXES, None),
            P("exp", CTX_AXES, None),
            P("exp", CTX_AXES, None),
            P("exp", CTX_AXES, None),
        ),
        out_specs=(P("exp", CTX_AXES, None), P("exp", CTX_AXES, None)),
        check_vma=False,
    )
```

```python
import functools

import jax
import jax.numpy as jnp
from jax import lax
from jax.experimental import pallas as pl
from jax.experimental.pallas import tpu as pltpu
from jax.sharding import PartitionSpec as P

D = 1024
HEADS = 8
KV_HEADS = 2
EXPERTS = 8
TOP = 2
TILE = 32
CAP = 72


def rms_scale(row_block, gain):
    widened = row_block.astype(jnp.float32)
    inverse = lax.rsqrt(jnp.mean(widened * widened, axis=-1, keepdims=True) + 1e-05)
    return widened * inverse * gain


CTX_AXES = ("z", "yh", "core")


MESH = pl.DeviceIdType.MESH


def gather_kernel(n_z, shard_ref, out_ref, local_sem, send_sem, recv_sem):
    z = lax.axis_index("z")
    yh = lax.axis_index("yh")
    core = lax.axis_index("core")
    ex = lax.axis_index("exp")

    def slot(zz, hh, cc):
        return (zz * 2 + hh) * 2 + cc

    def ring(offset):
        return lax.rem(z + offset + 4 * n_z, n_z)

    partner_h = 1 - yh
    sibling_c = 1 - core
    to_right = (ring(1), yh, core, ex)
    to_left = (ring(-1), yh, core, ex)
    to_partner = (z, partner_h, core, ex)
    to_sibling = (z, yh, sibling_c, ex)
    barrier = pltpu.get_barrier_semaphore()
    for dev in (to_right, to_left, to_partner, to_sibling):
        pl.semaphore_signal(barrier, 1, device_id=dev, device_id_type=MESH)
    pl.semaphore_wait(barrier, 4)

    me = slot(z, yh, core)
    own = pltpu.make_async_copy(shard_ref, out_ref.at[me], local_sem)
    own.start()
    sends = []

    def send(src, s, dev, k):
        copy = pltpu.make_async_remote_copy(
            src, out_ref.at[s], send_sem.at[k, s], recv_sem.at[s], device_id=dev, device_id_type=MESH
        )
        copy.start()
        sends.append(copy)

    def arrive(s):
        pltpu.make_async_remote_copy(
            out_ref.at[s], out_ref.at[s], send_sem.at[0, s], recv_sem.at[s],
            device_id=to_right, device_id_type=MESH,
        ).wait_recv()

    for k, dev in enumerate((to_right, to_left, to_partner, to_sibling)):
        send(shard_ref, me, dev, k)
    half = n_z // 2
    for t in range(1, half + 1):
        s = slot(ring(-t), yh, core)
        arrive(s)
        if t < half:
            send(out_ref.at[s], s, to_right, 0)
        send(out_ref.at[s], s, to_partner, 2)
        send(out_ref.at[s], s, to_sibling, 3)
        if t < n_z - half:
            s = slot(ring(t), yh, core)
            arrive(s)
            if t < n_z - half - 1:
                send(out_ref.at[s], s, to_left, 1)
            send(out_ref.at[s], s, to_partner, 2)
            send(out_ref.at[s], s, to_sibling, 3)
    partner_order = [0]
    for t in range(1, half + 1):
        partner_order.append(-t)
        if t < n_z - half:
            partner_order.append(t)
    for offset in partner_order:
        s = slot(ring(offset), partner_h, core)
        arrive(s)
        send(out_ref.at[s], s, to_sibling, 3)
    for hh in (yh, partner_h):
        for offset in partner_order:
            arrive(slot(ring(offset), hh, sibling_c))
    own.wait()
    for copy in sends:
        copy.wait_send()


def gather_ctx_kernel(block):
    n_z = lax.axis_size("z")
    n_all = n_z * 4
    return pl.pallas_call(
        functools.partial(gather_kernel, n_z),
        out_shape=jax.ShapeDtypeStruct((n_all,) + block.shape, block.dtype),
        in_specs=[pl.BlockSpec(memory_space=pl.ANY)],
        out_specs=pl.BlockSpec(memory_space=pl.ANY),
        scratch_shapes=[
            pltpu.SemaphoreType.DMA(()),
            pltpu.SemaphoreType.DMA((4, n_all)),
            pltpu.SemaphoreType.DMA((n_all,)),
        ],
        compiler_params=pltpu.CompilerParams(collective_id=0, has_side_effects=True),
    )(block)


def exchange_kernel(n_exp, chunk_ref, out_ref, local_sem, send_sem, recv_sem):
    me = lax.axis_index("exp")
    z = lax.axis_index("z")
    yh = lax.axis_index("yh")
    core = lax.axis_index("core")

    def peer(offset):
        return lax.rem(me + offset, n_exp)

    barrier = pltpu.get_barrier_semaphore()
    for offset in range(1, n_exp):
        pl.semaphore_signal(barrier, 1, device_id=(z, yh, core, peer(offset)), device_id_type=MESH)
    pl.semaphore_wait(barrier, n_exp - 1)
    own = pltpu.make_async_copy(chunk_ref.at[me], out_ref.at[me], local_sem)
    own.start()
    sends = []
    for offset in range(1, n_exp):
        target = peer(offset)
        copy = pltpu.make_async_remote_copy(
            chunk_ref.at[target], out_ref.at[me], send_sem.at[offset], recv_sem.at[me],
            device_id=(z, yh, core, target), device_id_type=MESH,
        )
        copy.start()
        sends.append(copy)
    for offset in range(1, n_exp):
        source = peer(n_exp - offset)
        pltpu.make_async_remote_copy(
            out_ref.at[source], out_ref.at[source], send_sem.at[offset], recv_sem.at[source],
            device_id=(z, yh, core, source), device_id_type=MESH,
        ).wait_recv()
    own.wait()
    for copy in sends:
        copy.wait_send()


def exchange_exp(chunks, collective_id):
    n_exp = chunks.shape[0]
    return pl.pallas_call(
        functools.partial(exchange_kernel, n_exp),
        out_shape=jax.ShapeDtypeStruct(chunks.shape, chunks.dtype),
        in_specs=[pl.BlockSpec(memory_space=pl.ANY)],
        out_specs=pl.BlockSpec(memory_space=pl.ANY),
        scratch_shapes=[
            pltpu.SemaphoreType.DMA(()),
            pltpu.SemaphoreType.DMA((n_exp,)),
            pltpu.SemaphoreType.DMA((n_exp,)),
        ],
        compiler_params=pltpu.CompilerParams(collective_id=collective_id, has_side_effects=True),
    )(chunks)


KEY_BLOCK = 128


def attention_kernel(groups, head_size, flag_ref, q_ref, kv_ref, mask_ref, out_ref, top_ref, sum_ref, acc_ref):
    n_blocks = flag_ref.shape[0]
    kv_heads = kv_ref.shape[1] // (2 * head_size)
    heads = kv_heads * groups
    value_at = kv_heads * head_size
    scale = head_size ** (-0.5)
    top_ref[...] = jnp.full(top_ref.shape, -1e30, jnp.float32)
    sum_ref[...] = jnp.zeros(sum_ref.shape, jnp.float32)
    acc_ref[...] = jnp.zeros(acc_ref.shape, jnp.float32)

    def allowed_block(j):
        tile_count = mask_ref.shape[1]
        tile_at = lax.broadcasted_iota(jnp.int32, (tile_count, KEY_BLOCK), 0)
        column_tile = lax.broadcasted_iota(jnp.int32, (tile_count, KEY_BLOCK), 1) // TILE
        spread = (tile_at == j * (KEY_BLOCK // TILE) + column_tile).astype(jnp.bfloat16)
        return jnp.dot(mask_ref[...], spread, preferred_element_type=jnp.float32) > 0

    def scores(j, h):
        rows = pl.ds(pl.multiple_of(j * KEY_BLOCK, KEY_BLOCK), KEY_BLOCK)
        key = kv_ref[rows, pl.ds((h // groups) * head_size, head_size)]
        query = q_ref[:, pl.ds(h * head_size, head_size)]
        raw = lax.dot_general(
            query, key, (((1,), (1,)), ((), ())), preferred_element_type=jnp.float32
        )
        return raw * scale, allowed_block(j)

    def first_pass(j, carry):
        @pl.when(flag_ref[j] > 0)
        def _():
            for h in range(heads):
                s, allowed = scores(j, h)
                top_ref[h] = jnp.maximum(top_ref[h], jnp.where(allowed, s, -1e30))
        return carry

    lax.fori_loop(0, n_blocks, first_pass, 0)
    for h in range(heads):
        top_ref[h] = jnp.broadcast_to(jnp.max(top_ref[h], axis=1, keepdims=True), top_ref.shape[1:])

    def second_pass(j, carry):
        @pl.when(flag_ref[j] > 0)
        def _():
            rows = pl.ds(pl.multiple_of(j * KEY_BLOCK, KEY_BLOCK), KEY_BLOCK)
            for h in range(heads):
                s, allowed = scores(j, h)
                weights = jnp.where(allowed, jnp.exp(s - top_ref[h]), 0.0)
                sum_ref[h] += weights
                value = kv_ref[rows, pl.ds(value_at + (h // groups) * head_size, head_size)]
                acc_ref[h] += jnp.dot(
                    weights.astype(jnp.bfloat16), value, preferred_element_type=jnp.float32
                )
        return carry

    lax.fori_loop(0, n_blocks, second_pass, 0)
    for h in range(heads):
        denominator = jnp.sum(sum_ref[h], axis=1, keepdims=True)
        out_ref[:, pl.ds(h * head_size, head_size)] = (acc_ref[h] / denominator).astype(out_ref.dtype)


def block_attention(query_rows, kv_rows, mask_block, groups, head_size):
    row_count = query_rows.shape[0]
    key_count = kv_rows.shape[0]
    heads = query_rows.shape[1] // head_size
    allowed = jnp.repeat(mask_block, TILE, axis=0).astype(jnp.bfloat16)
    tiles_per_block = KEY_BLOCK // TILE
    flags = jnp.max(
        mask_block.reshape(mask_block.shape[0], -1, tiles_per_block), axis=(0, 2)
    ).astype(jnp.int32)
    vmem = pl.BlockSpec(memory_space=pltpu.VMEM)
    return pl.pallas_call(
        functools.partial(attention_kernel, groups, head_size),
        out_shape=jax.ShapeDtypeStruct((row_count, heads * head_size), jnp.bfloat16),
        in_specs=[pl.BlockSpec(memory_space=pltpu.SMEM), vmem, vmem, vmem],
        out_specs=vmem,
        scratch_shapes=[
            pltpu.VMEM((heads, row_count, KEY_BLOCK), jnp.float32),
            pltpu.VMEM((heads, row_count, KEY_BLOCK), jnp.float32),
            pltpu.VMEM((heads, row_count, head_size), jnp.float32),
        ],
    )(flags, query_rows, kv_rows, allowed)


def shards(
    hidden_in,
    queries,
    key_proj,
    value_proj,
    tile_mask,
    out_weight,
    moe_gain,
    gate_weight,
    up_weight,
    down_weight,
    expert_ids,
    gate_probs,
):
    query_rows = queries[0]
    row_count = query_rows.shape[0]
    groups = HEADS // KV_HEADS
    head_size = D // HEADS
    query_heads = query_rows.reshape(row_count, KV_HEADS, groups, head_size)
    mask_block = tile_mask[0]
    kv_width = key_proj.shape[-1]
    kv_local = jnp.concatenate([key_proj[0], value_proj[0]], axis=-1)
    kv_piece = gather_ctx_kernel(kv_local).reshape(-1, 2 * kv_width)
    attended = block_attention(query_rows, kv_piece, mask_block, groups, head_size)
    projected = jnp.dot(attended, out_weight, preferred_element_type=jnp.float32)
    attention_out = projected.astype(jnp.bfloat16)
    residual = (hidden_in[0].astype(jnp.float32) + projected).astype(jnp.bfloat16)
    normed = rms_scale(residual, moe_gain).astype(jnp.bfloat16)
    id_row = expert_ids[0].reshape(-1)
    onehot = (id_row[:, None] == jnp.arange(EXPERTS, dtype=jnp.int32)[None, :]).astype(jnp.int32)
    before = jnp.cumsum(onehot, axis=0) - onehot
    slot_index = jnp.sum(before * onehot, axis=1)
    target = id_row * CAP + slot_index
    selector = (jnp.arange(EXPERTS * CAP, dtype=jnp.int32)[:, None] == target[None, :]).astype(
        jnp.bfloat16
    )
    repeated = jnp.repeat(normed, TOP, axis=0)
    outgoing = (
        jnp.dot(selector, repeated, preferred_element_type=jnp.float32)
        .astype(jnp.bfloat16)
        .reshape(EXPERTS, CAP, D)
    )
    arrived = exchange_exp(outgoing, 1).reshape(1, EXPERTS * CAP, D)
    ff = gate_weight.shape[-1]
    weight_piece = lax.all_gather(
        jnp.concatenate([gate_weight, up_weight, down_weight], axis=-1), CTX_AXES, axis=1, tiled=True
    )
    gate_piece = weight_piece[..., :ff]
    up_piece = weight_piece[..., ff : 2 * ff]
    down_piece = weight_piece[..., 2 * ff :]
    me = lax.axis_index("exp")
    tokens_rot = jnp.roll(arrived.reshape(EXPERTS, CAP, D), -me, axis=0)

    def run_rows(chunk_tokens):
        flat = chunk_tokens.reshape(-1, D)
        gate_sum = jnp.dot(flat, gate_piece[0], preferred_element_type=jnp.float32)
        up_sum = jnp.dot(flat, up_piece[0], preferred_element_type=jnp.float32)
        hidden = (jax.nn.silu(gate_sum) * up_sum).astype(jnp.bfloat16)
        rows = lax.dot_general(
            hidden, down_piece[0], (((1,), (1,)), ((), ())), preferred_element_type=jnp.float32
        )
        return rows.astype(jnp.bfloat16).reshape(-1, CAP, D)

    split = EXPERTS // 2
    first_rows = run_rows(tokens_rot[:split])
    second_rows = run_rows(tokens_rot[split:])
    received = [first_rows[0]]
    for offset in range(1, EXPERTS):
        chunk = first_rows[offset] if offset < split else second_rows[offset - split]
        received.append(
            lax.ppermute(chunk, "exp", [(i, (i + offset) % EXPERTS) for i in range(EXPERTS)])
        )
    returned = jnp.stack(received)
    target_rot = lax.rem(me - id_row + EXPERTS, EXPERTS) * CAP + slot_index
    combine = jnp.sum(
        jnp.where(
            jnp.arange(EXPERTS * CAP, dtype=jnp.int32)[None, None, :] == target_rot.reshape(row_count, TOP)[:, :, None],
            gate_probs[0][:, :, None],
            0.0,
        ),
        axis=1,
    )
    mixture = jnp.dot(
        combine,
        returned.reshape(EXPERTS * CAP, D).astype(jnp.float32),
        precision=lax.Precision.HIGHEST,
        preferred_element_type=jnp.float32,
    )
    layer_out = (residual.astype(jnp.float32) + mixture).astype(jnp.bfloat16)
    return (attention_out[None], layer_out[None])


def solution(mesh):
    n_ctx = mesh.shape["ctx"]
    split = jax.sharding.Mesh(
        mesh.devices.reshape(n_ctx // 4, 2, 2, mesh.shape["exp"]), CTX_AXES + ("exp",)
    )
    return jax.shard_map(
        shards,
        mesh=split,
        in_specs=(
            P("exp", CTX_AXES, None),
            P("exp", CTX_AXES, None),
            P("exp", CTX_AXES, None),
            P("exp", CTX_AXES, None),
            P("exp", CTX_AXES, None),
            P(),
            P(),
            P("exp", CTX_AXES, None),
            P("exp", CTX_AXES, None),
            P("exp", CTX_AXES, None),
            P("exp", CTX_AXES, None),
            P("exp", CTX_AXES, None),
        ),
        out_specs=(P("exp", CTX_AXES, None), P("exp", CTX_AXES, None)),
        check_vma=False,
    )
```

```python
import functools

import jax
import jax.numpy as jnp
from jax import lax
from jax.experimental import pallas as pl
from jax.experimental.pallas import tpu as pltpu
from jax.sharding import PartitionSpec as P

D = 1024
HEADS = 8
KV_HEADS = 2
EXPERTS = 8
TOP = 2
TILE = 32
CAP = 72


def rms_scale(row_block, gain):
    widened = row_block.astype(jnp.float32)
    inverse = lax.rsqrt(jnp.mean(widened * widened, axis=-1, keepdims=True) + 1e-05)
    return widened * inverse * gain


CTX_AXES = ("z", "yh", "core")


MESH = pl.DeviceIdType.MESH


def gather_kernel(n_z, shard_ref, out_ref, local_sem, send_sem, recv_sem):
    z = lax.axis_index("z")
    yh = lax.axis_index("yh")
    core = lax.axis_index("core")
    ex = lax.axis_index("exp")

    def slot(zz, hh, cc):
        return (zz * 2 + hh) * 2 + cc

    def ring(offset):
        return lax.rem(z + offset + 4 * n_z, n_z)

    partner_h = 1 - yh
    sibling_c = 1 - core
    to_right = (ring(1), yh, core, ex)
    to_left = (ring(-1), yh, core, ex)
    to_partner = (z, partner_h, core, ex)
    to_sibling = (z, yh, sibling_c, ex)
    barrier = pltpu.get_barrier_semaphore()
    for dev in (to_right, to_left, to_partner, to_sibling):
        pl.semaphore_signal(barrier, 1, device_id=dev, device_id_type=MESH)
    pl.semaphore_wait(barrier, 4)

    me = slot(z, yh, core)
    own = pltpu.make_async_copy(shard_ref, out_ref.at[me], local_sem)
    own.start()
    sends = []

    def send(src, s, dev, k):
        copy = pltpu.make_async_remote_copy(
            src, out_ref.at[s], send_sem.at[k, s], recv_sem.at[s], device_id=dev, device_id_type=MESH
        )
        copy.start()
        sends.append(copy)

    def arrive(s):
        pltpu.make_async_remote_copy(
            out_ref.at[s], out_ref.at[s], send_sem.at[0, s], recv_sem.at[s],
            device_id=to_right, device_id_type=MESH,
        ).wait_recv()

    for k, dev in enumerate((to_right, to_left, to_partner, to_sibling)):
        send(shard_ref, me, dev, k)
    half = n_z // 2
    for t in range(1, half + 1):
        s = slot(ring(-t), yh, core)
        arrive(s)
        if t < half:
            send(out_ref.at[s], s, to_right, 0)
        send(out_ref.at[s], s, to_partner, 2)
        send(out_ref.at[s], s, to_sibling, 3)
        if t < n_z - half:
            s = slot(ring(t), yh, core)
            arrive(s)
            if t < n_z - half - 1:
                send(out_ref.at[s], s, to_left, 1)
            send(out_ref.at[s], s, to_partner, 2)
            send(out_ref.at[s], s, to_sibling, 3)
    partner_order = [0]
    for t in range(1, half + 1):
        partner_order.append(-t)
        if t < n_z - half:
            partner_order.append(t)
    for offset in partner_order:
        s = slot(ring(offset), partner_h, core)
        arrive(s)
        send(out_ref.at[s], s, to_sibling, 3)
    for hh in (yh, partner_h):
        for offset in partner_order:
            arrive(slot(ring(offset), hh, sibling_c))
    own.wait()
    for copy in sends:
        copy.wait_send()


def gather_ctx_kernel(block):
    n_z = lax.axis_size("z")
    n_all = n_z * 4
    return pl.pallas_call(
        functools.partial(gather_kernel, n_z),
        out_shape=jax.ShapeDtypeStruct((n_all,) + block.shape, block.dtype),
        in_specs=[pl.BlockSpec(memory_space=pl.ANY)],
        out_specs=pl.BlockSpec(memory_space=pl.ANY),
        scratch_shapes=[
            pltpu.SemaphoreType.DMA(()),
            pltpu.SemaphoreType.DMA((4, n_all)),
            pltpu.SemaphoreType.DMA((n_all,)),
        ],
        compiler_params=pltpu.CompilerParams(collective_id=0, has_side_effects=True),
    )(block)


def exchange_kernel(n_exp, chunk_ref, out_ref, local_sem, send_sem, recv_sem):
    me = lax.axis_index("exp")
    z = lax.axis_index("z")
    yh = lax.axis_index("yh")
    core = lax.axis_index("core")

    def peer(offset):
        return lax.rem(me + offset, n_exp)

    barrier = pltpu.get_barrier_semaphore()
    for offset in range(1, n_exp):
        pl.semaphore_signal(barrier, 1, device_id=(z, yh, core, peer(offset)), device_id_type=MESH)
    pl.semaphore_wait(barrier, n_exp - 1)
    own = pltpu.make_async_copy(chunk_ref.at[me], out_ref.at[me], local_sem)
    own.start()
    sends = []
    for offset in range(1, n_exp):
        target = peer(offset)
        copy = pltpu.make_async_remote_copy(
            chunk_ref.at[target], out_ref.at[me], send_sem.at[offset], recv_sem.at[me],
            device_id=(z, yh, core, target), device_id_type=MESH,
        )
        copy.start()
        sends.append(copy)
    for offset in range(1, n_exp):
        source = peer(n_exp - offset)
        pltpu.make_async_remote_copy(
            out_ref.at[source], out_ref.at[source], send_sem.at[offset], recv_sem.at[source],
            device_id=(z, yh, core, source), device_id_type=MESH,
        ).wait_recv()
    own.wait()
    for copy in sends:
        copy.wait_send()


def exchange_exp(chunks, collective_id):
    n_exp = chunks.shape[0]
    return pl.pallas_call(
        functools.partial(exchange_kernel, n_exp),
        out_shape=jax.ShapeDtypeStruct(chunks.shape, chunks.dtype),
        in_specs=[pl.BlockSpec(memory_space=pl.ANY)],
        out_specs=pl.BlockSpec(memory_space=pl.ANY),
        scratch_shapes=[
            pltpu.SemaphoreType.DMA(()),
            pltpu.SemaphoreType.DMA((n_exp,)),
            pltpu.SemaphoreType.DMA((n_exp,)),
        ],
        compiler_params=pltpu.CompilerParams(collective_id=collective_id, has_side_effects=True),
    )(chunks)


KEY_BLOCK = 128


def attention_kernel(groups, head_size, flag_ref, q_ref, kv_ref, mask_ref, out_ref, top_ref, sum_ref, acc_ref):
    n_blocks = flag_ref.shape[0]
    kv_heads = kv_ref.shape[1] // (2 * head_size)
    heads = kv_heads * groups
    value_at = kv_heads * head_size
    scale = head_size ** (-0.5)
    top_ref[...] = jnp.full(top_ref.shape, -1e30, jnp.float32)
    sum_ref[...] = jnp.zeros(sum_ref.shape, jnp.float32)
    acc_ref[...] = jnp.zeros(acc_ref.shape, jnp.float32)

    def allowed_block(j):
        tile_count = mask_ref.shape[1]
        tile_at = lax.broadcasted_iota(jnp.int32, (tile_count, KEY_BLOCK), 0)
        column_tile = lax.broadcasted_iota(jnp.int32, (tile_count, KEY_BLOCK), 1) // TILE
        spread = (tile_at == j * (KEY_BLOCK // TILE) + column_tile).astype(jnp.bfloat16)
        return jnp.dot(mask_ref[...], spread, preferred_element_type=jnp.float32) > 0

    def scores(j, h):
        rows = pl.ds(pl.multiple_of(j * KEY_BLOCK, KEY_BLOCK), KEY_BLOCK)
        key = kv_ref[rows, pl.ds((h // groups) * head_size, head_size)]
        query = q_ref[:, pl.ds(h * head_size, head_size)]
        raw = lax.dot_general(
            query, key, (((1,), (1,)), ((), ())), preferred_element_type=jnp.float32
        )
        return raw * scale, allowed_block(j)

    def first_pass(j, carry):
        @pl.when(flag_ref[j] > 0)
        def _():
            for h in range(heads):
                s, allowed = scores(j, h)
                top_ref[h] = jnp.maximum(top_ref[h], jnp.where(allowed, s, -1e30))
        return carry

    lax.fori_loop(0, n_blocks, first_pass, 0)
    for h in range(heads):
        top_ref[h] = jnp.broadcast_to(jnp.max(top_ref[h], axis=1, keepdims=True), top_ref.shape[1:])

    def second_pass(j, carry):
        @pl.when(flag_ref[j] > 0)
        def _():
            rows = pl.ds(pl.multiple_of(j * KEY_BLOCK, KEY_BLOCK), KEY_BLOCK)
            for h in range(heads):
                s, allowed = scores(j, h)
                weights = jnp.where(allowed, jnp.exp(s - top_ref[h]), 0.0)
                sum_ref[h] += weights
                value = kv_ref[rows, pl.ds(value_at + (h // groups) * head_size, head_size)]
                acc_ref[h] += jnp.dot(
                    weights.astype(jnp.bfloat16), value, preferred_element_type=jnp.float32
                )
        return carry

    lax.fori_loop(0, n_blocks, second_pass, 0)
    for h in range(heads):
        denominator = jnp.sum(sum_ref[h], axis=1, keepdims=True)
        out_ref[:, pl.ds(h * head_size, head_size)] = (acc_ref[h] / denominator).astype(out_ref.dtype)


def block_attention(query_rows, kv_rows, mask_block, groups, head_size):
    row_count = query_rows.shape[0]
    key_count = kv_rows.shape[0]
    heads = query_rows.shape[1] // head_size
    allowed = jnp.repeat(mask_block, TILE, axis=0).astype(jnp.bfloat16)
    tiles_per_block = KEY_BLOCK // TILE
    flags = jnp.max(
        mask_block.reshape(mask_block.shape[0], -1, tiles_per_block), axis=(0, 2)
    ).astype(jnp.int32)
    vmem = pl.BlockSpec(memory_space=pltpu.VMEM)
    return pl.pallas_call(
        functools.partial(attention_kernel, groups, head_size),
        out_shape=jax.ShapeDtypeStruct((row_count, heads * head_size), jnp.bfloat16),
        in_specs=[pl.BlockSpec(memory_space=pltpu.SMEM), vmem, vmem, vmem],
        out_specs=vmem,
        scratch_shapes=[
            pltpu.VMEM((heads, row_count, KEY_BLOCK), jnp.float32),
            pltpu.VMEM((heads, row_count, KEY_BLOCK), jnp.float32),
            pltpu.VMEM((heads, row_count, head_size), jnp.float32),
        ],
    )(flags, query_rows, kv_rows, allowed)


def shards(
    hidden_in,
    queries,
    key_proj,
    value_proj,
    tile_mask,
    out_weight,
    moe_gain,
    gate_weight,
    up_weight,
    down_weight,
    expert_ids,
    gate_probs,
):
    query_rows = queries[0]
    row_count = query_rows.shape[0]
    groups = HEADS // KV_HEADS
    head_size = D // HEADS
    query_heads = query_rows.reshape(row_count, KV_HEADS, groups, head_size)
    mask_block = tile_mask[0]
    kv_width = key_proj.shape[-1]
    kv_local = jnp.concatenate([key_proj[0], value_proj[0]], axis=-1)
    kv_piece = gather_ctx_kernel(kv_local).reshape(-1, 2 * kv_width)
    attended = block_attention(query_rows, kv_piece, mask_block, groups, head_size)
    projected = jnp.dot(attended, out_weight, preferred_element_type=jnp.float32)
    attention_out = projected.astype(jnp.bfloat16)
    residual = (hidden_in[0].astype(jnp.float32) + projected).astype(jnp.bfloat16)
    normed = rms_scale(residual, moe_gain).astype(jnp.bfloat16)
    id_row = expert_ids[0].reshape(-1)
    onehot = (id_row[:, None] == jnp.arange(EXPERTS, dtype=jnp.int32)[None, :]).astype(jnp.int32)
    before = jnp.cumsum(onehot, axis=0) - onehot
    slot_index = jnp.sum(before * onehot, axis=1)
    target = id_row * CAP + slot_index
    selector = (jnp.arange(EXPERTS * CAP, dtype=jnp.int32)[:, None] == target[None, :]).astype(
        jnp.bfloat16
    )
    repeated = jnp.repeat(normed, TOP, axis=0)
    outgoing = (
        jnp.dot(selector, repeated, preferred_element_type=jnp.float32)
        .astype(jnp.bfloat16)
        .reshape(EXPERTS, CAP, D)
    )
    arrived = exchange_exp(outgoing, 1).reshape(1, EXPERTS * CAP, D)
    ff = gate_weight.shape[-1]
    weight_piece = lax.all_gather(
        jnp.concatenate([gate_weight, up_weight, down_weight], axis=-1), CTX_AXES, axis=1, tiled=True
    )
    gate_piece = weight_piece[..., :ff]
    up_piece = weight_piece[..., ff : 2 * ff]
    down_piece = weight_piece[..., 2 * ff :]
    both_sums = jnp.dot(arrived[0], weight_piece[0, :, : 2 * ff], preferred_element_type=jnp.float32)
    gate_sum = both_sums[None, :, :ff]
    up_sum = both_sums[None, :, ff:]
    hidden = (jax.nn.silu(gate_sum) * up_sum).astype(jnp.bfloat16)
    expert_rows = jnp.einsum(
        "esf,edf->esd",
        hidden,
        down_piece,
        preferred_element_type=jnp.float32,
    ).astype(jnp.bfloat16)
    returned = exchange_exp(expert_rows.reshape(EXPERTS, CAP, D), 2)
    combine = jnp.sum(
        jnp.where(
            jnp.arange(EXPERTS * CAP, dtype=jnp.int32)[None, None, :] == target.reshape(row_count, TOP)[:, :, None],
            gate_probs[0][:, :, None],
            0.0,
        ),
        axis=1,
    )
    mixture = jnp.dot(
        combine,
        returned.reshape(EXPERTS * CAP, D).astype(jnp.float32),
        precision=lax.Precision.HIGHEST,
        preferred_element_type=jnp.float32,
    )
    layer_out = (residual.astype(jnp.float32) + mixture).astype(jnp.bfloat16)
    return (attention_out[None], layer_out[None])


def solution(mesh):
    n_ctx = mesh.shape["ctx"]
    split = jax.sharding.Mesh(
        mesh.devices.reshape(n_ctx // 4, 2, 2, mesh.shape["exp"]), CTX_AXES + ("exp",)
    )
    return jax.shard_map(
        shards,
        mesh=split,
        in_specs=(
            P("exp", CTX_AXES, None),
            P("exp", CTX_AXES, None),
            P("exp", CTX_AXES, None),
            P("exp", CTX_AXES, None),
            P("exp", CTX_AXES, None),
            P(),
            P(),
            P("exp", CTX_AXES, None),
            P("exp", CTX_AXES, None),
            P("exp", CTX_AXES, None),
            P("exp", CTX_AXES, None),
            P("exp", CTX_AXES, None),
        ),
        out_specs=(P("exp", CTX_AXES, None), P("exp", CTX_AXES, None)),
        check_vma=False,
    )
```

```python
import functools

import jax
import jax.numpy as jnp
from jax import lax
from jax.experimental import pallas as pl
from jax.experimental.pallas import tpu as pltpu
from jax.sharding import PartitionSpec as P

D = 1024
HEADS = 8
KV_HEADS = 2
EXPERTS = 8
TOP = 2
TILE = 32
CAP = 72


def rms_scale(row_block, gain):
    widened = row_block.astype(jnp.float32)
    inverse = lax.rsqrt(jnp.mean(widened * widened, axis=-1, keepdims=True) + 1e-05)
    return widened * inverse * gain


CTX_AXES = ("z", "yh", "core")


MESH = pl.DeviceIdType.MESH


def gather_kernel(n_z, shard_ref, out_ref, local_sem, send_sem, recv_sem):
    z = lax.axis_index("z")
    yh = lax.axis_index("yh")
    core = lax.axis_index("core")
    ex = lax.axis_index("exp")

    def slot(zz, hh, cc):
        return (zz * 2 + hh) * 2 + cc

    def ring(offset):
        return lax.rem(z + offset + 4 * n_z, n_z)

    partner_h = 1 - yh
    sibling_c = 1 - core
    to_right = (ring(1), yh, core, ex)
    to_left = (ring(-1), yh, core, ex)
    to_partner = (z, partner_h, core, ex)
    to_sibling = (z, yh, sibling_c, ex)
    barrier = pltpu.get_barrier_semaphore()
    for dev in (to_right, to_left, to_partner, to_sibling):
        pl.semaphore_signal(barrier, 1, device_id=dev, device_id_type=MESH)
    pl.semaphore_wait(barrier, 4)

    me = slot(z, yh, core)
    own = pltpu.make_async_copy(shard_ref, out_ref.at[me], local_sem)
    own.start()
    sends = []

    def send(src, s, dev, k):
        copy = pltpu.make_async_remote_copy(
            src, out_ref.at[s], send_sem.at[k, s], recv_sem.at[s], device_id=dev, device_id_type=MESH
        )
        copy.start()
        sends.append(copy)

    def arrive(s):
        pltpu.make_async_remote_copy(
            out_ref.at[s], out_ref.at[s], send_sem.at[0, s], recv_sem.at[s],
            device_id=to_right, device_id_type=MESH,
        ).wait_recv()

    for k, dev in enumerate((to_right, to_left, to_partner, to_sibling)):
        send(shard_ref, me, dev, k)
    half = n_z // 2
    for t in range(1, half + 1):
        s = slot(ring(-t), yh, core)
        arrive(s)
        if t < half:
            send(out_ref.at[s], s, to_right, 0)
        send(out_ref.at[s], s, to_partner, 2)
        send(out_ref.at[s], s, to_sibling, 3)
        if t < n_z - half:
            s = slot(ring(t), yh, core)
            arrive(s)
            if t < n_z - half - 1:
                send(out_ref.at[s], s, to_left, 1)
            send(out_ref.at[s], s, to_partner, 2)
            send(out_ref.at[s], s, to_sibling, 3)
    partner_order = [0]
    for t in range(1, half + 1):
        partner_order.append(-t)
        if t < n_z - half:
            partner_order.append(t)
    for offset in partner_order:
        s = slot(ring(offset), partner_h, core)
        arrive(s)
        send(out_ref.at[s], s, to_sibling, 3)
    for hh in (yh, partner_h):
        for offset in partner_order:
            arrive(slot(ring(offset), hh, sibling_c))
    own.wait()
    for copy in sends:
        copy.wait_send()


def gather_ctx_kernel(block):
    n_z = lax.axis_size("z")
    n_all = n_z * 4
    return pl.pallas_call(
        functools.partial(gather_kernel, n_z),
        out_shape=jax.ShapeDtypeStruct((n_all,) + block.shape, block.dtype),
        in_specs=[pl.BlockSpec(memory_space=pl.ANY)],
        out_specs=pl.BlockSpec(memory_space=pl.ANY),
        scratch_shapes=[
            pltpu.SemaphoreType.DMA(()),
            pltpu.SemaphoreType.DMA((4, n_all)),
            pltpu.SemaphoreType.DMA((n_all,)),
        ],
        compiler_params=pltpu.CompilerParams(collective_id=0, has_side_effects=True),
    )(block)


def exchange_kernel(n_exp, chunk_ref, out_ref, local_sem, send_sem, recv_sem):
    me = lax.axis_index("exp")
    z = lax.axis_index("z")
    yh = lax.axis_index("yh")
    core = lax.axis_index("core")

    def peer(offset):
        return lax.rem(me + offset, n_exp)

    barrier = pltpu.get_barrier_semaphore()
    for offset in range(1, n_exp):
        pl.semaphore_signal(barrier, 1, device_id=(z, yh, core, peer(offset)), device_id_type=MESH)
    pl.semaphore_wait(barrier, n_exp - 1)
    own = pltpu.make_async_copy(chunk_ref.at[me], out_ref.at[me], local_sem)
    own.start()
    sends = []
    for offset in range(1, n_exp):
        target = peer(offset)
        copy = pltpu.make_async_remote_copy(
            chunk_ref.at[target], out_ref.at[me], send_sem.at[offset], recv_sem.at[me],
            device_id=(z, yh, core, target), device_id_type=MESH,
        )
        copy.start()
        sends.append(copy)
    for offset in range(1, n_exp):
        source = peer(n_exp - offset)
        pltpu.make_async_remote_copy(
            out_ref.at[source], out_ref.at[source], send_sem.at[offset], recv_sem.at[source],
            device_id=(z, yh, core, source), device_id_type=MESH,
        ).wait_recv()
    own.wait()
    for copy in sends:
        copy.wait_send()


def exchange_exp(chunks, collective_id):
    n_exp = chunks.shape[0]
    return pl.pallas_call(
        functools.partial(exchange_kernel, n_exp),
        out_shape=jax.ShapeDtypeStruct(chunks.shape, chunks.dtype),
        in_specs=[pl.BlockSpec(memory_space=pl.ANY)],
        out_specs=pl.BlockSpec(memory_space=pl.ANY),
        scratch_shapes=[
            pltpu.SemaphoreType.DMA(()),
            pltpu.SemaphoreType.DMA((n_exp,)),
            pltpu.SemaphoreType.DMA((n_exp,)),
        ],
        compiler_params=pltpu.CompilerParams(collective_id=collective_id, has_side_effects=True),
    )(chunks)


KEY_BLOCK = 128


def attention_kernel(groups, head_size, flag_ref, q_ref, kv_ref, mask_ref, out_ref, top_ref, sum_ref, acc_ref):
    n_blocks = flag_ref.shape[0]
    kv_heads = kv_ref.shape[1] // (2 * head_size)
    heads = kv_heads * groups
    value_at = kv_heads * head_size
    scale = head_size ** (-0.5)
    top_ref[...] = jnp.full(top_ref.shape, -1e30, jnp.float32)
    sum_ref[...] = jnp.zeros(sum_ref.shape, jnp.float32)
    acc_ref[...] = jnp.zeros(acc_ref.shape, jnp.float32)

    def allowed_block(j):
        tile_count = mask_ref.shape[1]
        tile_at = lax.broadcasted_iota(jnp.int32, (tile_count, KEY_BLOCK), 0)
        column_tile = lax.broadcasted_iota(jnp.int32, (tile_count, KEY_BLOCK), 1) // TILE
        spread = (tile_at == j * (KEY_BLOCK // TILE) + column_tile).astype(jnp.bfloat16)
        return jnp.dot(mask_ref[...], spread, preferred_element_type=jnp.float32) > 0

    def scores(j, h):
        rows = pl.ds(pl.multiple_of(j * KEY_BLOCK, KEY_BLOCK), KEY_BLOCK)
        key = kv_ref[rows, pl.ds((h // groups) * head_size, head_size)]
        query = q_ref[:, pl.ds(h * head_size, head_size)]
        raw = lax.dot_general(
            query, key, (((1,), (1,)), ((), ())), preferred_element_type=jnp.float32
        )
        return raw * scale, allowed_block(j)

    def first_pass(j, carry):
        @pl.when(flag_ref[j] > 0)
        def _():
            for h in range(heads):
                s, allowed = scores(j, h)
                top_ref[h] = jnp.maximum(top_ref[h], jnp.where(allowed, s, -1e30))
        return carry

    lax.fori_loop(0, n_blocks, first_pass, 0)
    for h in range(heads):
        top_ref[h] = jnp.broadcast_to(jnp.max(top_ref[h], axis=1, keepdims=True), top_ref.shape[1:])

    def second_pass(j, carry):
        @pl.when(flag_ref[j] > 0)
        def _():
            rows = pl.ds(pl.multiple_of(j * KEY_BLOCK, KEY_BLOCK), KEY_BLOCK)
            for h in range(heads):
                s, allowed = scores(j, h)
                weights = jnp.where(allowed, jnp.exp(s - top_ref[h]), 0.0)
                sum_ref[h] += weights
                value = kv_ref[rows, pl.ds(value_at + (h // groups) * head_size, head_size)]
                acc_ref[h] += jnp.dot(
                    weights.astype(jnp.bfloat16), value, preferred_element_type=jnp.float32
                )
        return carry

    lax.fori_loop(0, n_blocks, second_pass, 0)
    for h in range(heads):
        denominator = jnp.sum(sum_ref[h], axis=1, keepdims=True)
        out_ref[:, pl.ds(h * head_size, head_size)] = (acc_ref[h] / denominator).astype(out_ref.dtype)


def block_attention(query_rows, kv_rows, mask_block, groups, head_size):
    row_count = query_rows.shape[0]
    key_count = kv_rows.shape[0]
    heads = query_rows.shape[1] // head_size
    allowed = jnp.repeat(mask_block, TILE, axis=0).astype(jnp.bfloat16)
    tiles_per_block = KEY_BLOCK // TILE
    flags = jnp.max(
        mask_block.reshape(mask_block.shape[0], -1, tiles_per_block), axis=(0, 2)
    ).astype(jnp.int32)
    vmem = pl.BlockSpec(memory_space=pltpu.VMEM)
    return pl.pallas_call(
        functools.partial(attention_kernel, groups, head_size),
        out_shape=jax.ShapeDtypeStruct((row_count, heads * head_size), jnp.bfloat16),
        in_specs=[pl.BlockSpec(memory_space=pltpu.SMEM), vmem, vmem, vmem],
        out_specs=vmem,
        scratch_shapes=[
            pltpu.VMEM((heads, row_count, KEY_BLOCK), jnp.float32),
            pltpu.VMEM((heads, row_count, KEY_BLOCK), jnp.float32),
            pltpu.VMEM((heads, row_count, head_size), jnp.float32),
        ],
    )(flags, query_rows, kv_rows, allowed)


def shards(
    hidden_in,
    queries,
    key_proj,
    value_proj,
    tile_mask,
    out_weight,
    moe_gain,
    gate_weight,
    up_weight,
    down_weight,
    expert_ids,
    gate_probs,
):
    query_rows = queries[0]
    row_count = query_rows.shape[0]
    groups = HEADS // KV_HEADS
    head_size = D // HEADS
    query_heads = query_rows.reshape(row_count, KV_HEADS, groups, head_size)
    mask_block = tile_mask[0]
    kv_width = key_proj.shape[-1]
    kv_local = jnp.concatenate([key_proj[0], value_proj[0]], axis=-1)
    kv_piece = gather_ctx_kernel(kv_local).reshape(-1, 2 * kv_width)
    attended = block_attention(query_rows, kv_piece, mask_block, groups, head_size)
    projected = jnp.dot(attended, out_weight, preferred_element_type=jnp.float32)
    attention_out = projected.astype(jnp.bfloat16)
    residual = (hidden_in[0].astype(jnp.float32) + projected).astype(jnp.bfloat16)
    normed = rms_scale(residual, moe_gain).astype(jnp.bfloat16)
    id_row = expert_ids[0].reshape(-1)
    onehot = (id_row[:, None] == jnp.arange(EXPERTS, dtype=jnp.int32)[None, :]).astype(jnp.int32)
    before = jnp.cumsum(onehot, axis=0) - onehot
    slot_index = jnp.sum(before * onehot, axis=1)
    target = id_row * CAP + slot_index
    selector = (jnp.arange(EXPERTS * CAP, dtype=jnp.int32)[:, None] == target[None, :]).astype(
        jnp.bfloat16
    )
    repeated = jnp.repeat(normed, TOP, axis=0)
    outgoing = (
        jnp.dot(selector, repeated, preferred_element_type=jnp.float32)
        .astype(jnp.bfloat16)
        .reshape(EXPERTS, CAP, D)
    )
    arrived = exchange_exp(outgoing, 1).reshape(1, EXPERTS * CAP, D)
    ff = gate_weight.shape[-1]
    weight_piece = lax.all_gather(
        jnp.concatenate([gate_weight, up_weight, down_weight], axis=-1), CTX_AXES, axis=1, tiled=True
    )
    gate_piece = weight_piece[..., :ff]
    up_piece = weight_piece[..., ff : 2 * ff]
    down_piece = weight_piece[..., 2 * ff :]
    both_sums = jnp.dot(arrived[0], weight_piece[0, :, : 2 * ff], preferred_element_type=jnp.float32)
    gate_sum = both_sums[None, :, :ff]
    up_sum = both_sums[None, :, ff:]
    hidden = (jax.nn.silu(gate_sum) * up_sum).astype(jnp.bfloat16)
    expert_rows = jnp.einsum(
        "esf,edf->esd",
        hidden,
        down_piece,
        preferred_element_type=jnp.float32,
    ).astype(jnp.bfloat16)
    returned = exchange_exp(expert_rows.reshape(EXPERTS, CAP, D), 2)
    combine = jnp.sum(
        jnp.where(
            jnp.arange(EXPERTS * CAP, dtype=jnp.int32)[None, None, :] == target.reshape(row_count, TOP)[:, :, None],
            gate_probs[0][:, :, None],
            0.0,
        ),
        axis=1,
    )
    returned_rows = returned.reshape(EXPERTS * CAP, D)
    mixture = jnp.zeros((row_count, D), jnp.float32)
    remainder = combine
    for _ in range(3):
        part = remainder.astype(jnp.bfloat16)
        remainder = remainder - part.astype(jnp.float32)
        mixture = mixture + jnp.dot(part, returned_rows, preferred_element_type=jnp.float32)
    layer_out = (residual.astype(jnp.float32) + mixture).astype(jnp.bfloat16)
    return (attention_out[None], layer_out[None])


def solution(mesh):
    n_ctx = mesh.shape["ctx"]
    split = jax.sharding.Mesh(
        mesh.devices.reshape(n_ctx // 4, 2, 2, mesh.shape["exp"]), CTX_AXES + ("exp",)
    )
    return jax.shard_map(
        shards,
        mesh=split,
        in_specs=(
            P("exp", CTX_AXES, None),
            P("exp", CTX_AXES, None),
            P("exp", CTX_AXES, None),
            P("exp", CTX_AXES, None),
            P("exp", CTX_AXES, None),
            P(),
            P(),
            P("exp", CTX_AXES, None),
            P("exp", CTX_AXES, None),
            P("exp", CTX_AXES, None),
            P("exp", CTX_AXES, None),
            P("exp", CTX_AXES, None),
        ),
        out_specs=(P("exp", CTX_AXES, None), P("exp", CTX_AXES, None)),
        check_vma=False,
    )
```

```python
import functools

import jax
import jax.numpy as jnp
from jax import lax
from jax.experimental import pallas as pl
from jax.experimental.pallas import tpu as pltpu
from jax.sharding import PartitionSpec as P

D = 1024
HEADS = 8
KV_HEADS = 2
EXPERTS = 8
TOP = 2
TILE = 32
CAP = 72


def rms_scale(row_block, gain):
    widened = row_block.astype(jnp.float32)
    inverse = lax.rsqrt(jnp.mean(widened * widened, axis=-1, keepdims=True) + 1e-05)
    return widened * inverse * gain


CTX_AXES = ("z", "yh", "core")


MESH = pl.DeviceIdType.MESH


def gather_kernel(n_z, shard_ref, out_ref, local_sem, send_sem, recv_sem):
    z = lax.axis_index("z")
    yh = lax.axis_index("yh")
    core = lax.axis_index("core")
    ex = lax.axis_index("exp")

    def slot(zz, hh, cc):
        return (zz * 2 + hh) * 2 + cc

    def ring(offset):
        return lax.rem(z + offset + 4 * n_z, n_z)

    partner_h = 1 - yh
    sibling_c = 1 - core
    to_right = (ring(1), yh, core, ex)
    to_left = (ring(-1), yh, core, ex)
    to_partner = (z, partner_h, core, ex)
    to_sibling = (z, yh, sibling_c, ex)
    barrier = pltpu.get_barrier_semaphore()
    for dev in (to_right, to_left, to_partner, to_sibling):
        pl.semaphore_signal(barrier, 1, device_id=dev, device_id_type=MESH)
    pl.semaphore_wait(barrier, 4)

    me = slot(z, yh, core)
    own = pltpu.make_async_copy(shard_ref, out_ref.at[me], local_sem)
    own.start()
    sends = []

    def send(src, s, dev, k):
        copy = pltpu.make_async_remote_copy(
            src, out_ref.at[s], send_sem.at[k, s], recv_sem.at[s], device_id=dev, device_id_type=MESH
        )
        copy.start()
        sends.append(copy)

    def arrive(s):
        pltpu.make_async_remote_copy(
            out_ref.at[s], out_ref.at[s], send_sem.at[0, s], recv_sem.at[s],
            device_id=to_right, device_id_type=MESH,
        ).wait_recv()

    for k, dev in enumerate((to_right, to_left, to_partner, to_sibling)):
        send(shard_ref, me, dev, k)
    half = n_z // 2
    for t in range(1, half + 1):
        s = slot(ring(-t), yh, core)
        arrive(s)
        if t < half:
            send(out_ref.at[s], s, to_right, 0)
        send(out_ref.at[s], s, to_partner, 2)
        send(out_ref.at[s], s, to_sibling, 3)
        if t < n_z - half:
            s = slot(ring(t), yh, core)
            arrive(s)
            if t < n_z - half - 1:
                send(out_ref.at[s], s, to_left, 1)
            send(out_ref.at[s], s, to_partner, 2)
            send(out_ref.at[s], s, to_sibling, 3)
    partner_order = [0]
    for t in range(1, half + 1):
        partner_order.append(-t)
        if t < n_z - half:
            partner_order.append(t)
    for offset in partner_order:
        s = slot(ring(offset), partner_h, core)
        arrive(s)
        send(out_ref.at[s], s, to_sibling, 3)
    for hh in (yh, partner_h):
        for offset in partner_order:
            arrive(slot(ring(offset), hh, sibling_c))
    own.wait()
    for copy in sends:
        copy.wait_send()


def gather_ctx_kernel(block):
    n_z = lax.axis_size("z")
    n_all = n_z * 4
    return pl.pallas_call(
        functools.partial(gather_kernel, n_z),
        out_shape=jax.ShapeDtypeStruct((n_all,) + block.shape, block.dtype),
        in_specs=[pl.BlockSpec(memory_space=pl.ANY)],
        out_specs=pl.BlockSpec(memory_space=pl.ANY),
        scratch_shapes=[
            pltpu.SemaphoreType.DMA(()),
            pltpu.SemaphoreType.DMA((4, n_all)),
            pltpu.SemaphoreType.DMA((n_all,)),
        ],
        compiler_params=pltpu.CompilerParams(collective_id=0, has_side_effects=True),
    )(block)


RELAY_ROWS = 32


def exchange_kernel(n_exp, chunk_ref, out_ref, relay_buf, local_sem, send_sem, recv_sem, relay_send, relay_in, fwd_send, relay_recv):
    me = lax.axis_index("exp")
    z = lax.axis_index("z")
    yh = lax.axis_index("yh")
    core = lax.axis_index("core")
    n_x = n_exp // 2
    x = me % n_x
    row = me // n_x
    rows = chunk_ref.shape[1]
    near = pl.ds(0, RELAY_ROWS)
    far = pl.ds(RELAY_ROWS, rows - RELAY_ROWS)

    def device(r, xx):
        return (z, yh, core, r * n_x + lax.rem(xx + 2 * n_x, n_x))

    barrier = pltpu.get_barrier_semaphore()
    for offset in range(1, n_exp):
        pl.semaphore_signal(barrier, 1, device_id=(z, yh, core, lax.rem(me + offset, n_exp)), device_id_type=MESH)
    pl.semaphore_wait(barrier, n_exp - 1)
    own = pltpu.make_async_copy(chunk_ref.at[me], out_ref.at[me], local_sem)
    own.start()
    sends = []
    relay_at = device(row, x - 1)
    for r_off in range(2):
        target_row = lax.rem(row + r_off, 2)
        for dx in range(n_x):
            if r_off == 0 and dx == 0:
                continue
            target = device(target_row, x + dx)
            target_index = target[3]
            slot = r_off * n_x + dx
            if dx == n_x // 2:
                copy = pltpu.make_async_remote_copy(
                    chunk_ref.at[target_index, far], out_ref.at[me, far], send_sem.at[slot], recv_sem.at[me],
                    device_id=target, device_id_type=MESH,
                )
                copy.start()
                sends.append(copy)
                copy = pltpu.make_async_remote_copy(
                    chunk_ref.at[target_index, near], relay_buf.at[r_off], relay_send.at[r_off], relay_in.at[r_off],
                    device_id=relay_at, device_id_type=MESH,
                )
                copy.start()
                sends.append(copy)
            else:
                copy = pltpu.make_async_remote_copy(
                    chunk_ref.at[target_index], out_ref.at[me], send_sem.at[slot], recv_sem.at[me],
                    device_id=target, device_id_type=MESH,
                )
                copy.start()
                sends.append(copy)
    relayed_source = device(row, x + 1)[3]
    for r_off in range(2):
        pltpu.make_async_remote_copy(
            relay_buf.at[r_off], relay_buf.at[r_off], relay_send.at[r_off], relay_in.at[r_off],
            device_id=relay_at, device_id_type=MESH,
        ).wait_recv()
        target = device(lax.rem(row + r_off, 2), x - 1)
        copy = pltpu.make_async_remote_copy(
            relay_buf.at[r_off], out_ref.at[relayed_source, near], fwd_send.at[r_off], relay_recv.at[relayed_source],
            device_id=target, device_id_type=MESH,
        )
        copy.start()
        sends.append(copy)
    for r_off in range(2):
        source_row = lax.rem(row + r_off, 2)
        for dx in range(n_x):
            if r_off == 0 and dx == 0:
                continue
            source = device(source_row, x + dx)[3]
            if dx == n_x // 2:
                pltpu.make_async_remote_copy(
                    out_ref.at[source, far], out_ref.at[source, far], send_sem.at[0], recv_sem.at[source],
                    device_id=relay_at, device_id_type=MESH,
                ).wait_recv()
                pltpu.make_async_remote_copy(
                    out_ref.at[source, near], out_ref.at[source, near], send_sem.at[0], relay_recv.at[source],
                    device_id=relay_at, device_id_type=MESH,
                ).wait_recv()
            else:
                pltpu.make_async_remote_copy(
                    out_ref.at[source], out_ref.at[source], send_sem.at[0], recv_sem.at[source],
                    device_id=relay_at, device_id_type=MESH,
                ).wait_recv()
    own.wait()
    for copy in sends:
        copy.wait_send()


def exchange_exp(chunks, collective_id):
    n_exp = chunks.shape[0]
    return pl.pallas_call(
        functools.partial(exchange_kernel, n_exp),
        out_shape=jax.ShapeDtypeStruct(chunks.shape, chunks.dtype),
        in_specs=[pl.BlockSpec(memory_space=pl.ANY)],
        out_specs=pl.BlockSpec(memory_space=pl.ANY),
        scratch_shapes=[
            pltpu.VMEM((2, RELAY_ROWS) + chunks.shape[2:], chunks.dtype),
            pltpu.SemaphoreType.DMA(()),
            pltpu.SemaphoreType.DMA((n_exp,)),
            pltpu.SemaphoreType.DMA((n_exp,)),
            pltpu.SemaphoreType.DMA((2,)),
            pltpu.SemaphoreType.DMA((2,)),
            pltpu.SemaphoreType.DMA((2,)),
            pltpu.SemaphoreType.DMA((n_exp,)),
        ],
        compiler_params=pltpu.CompilerParams(collective_id=collective_id, has_side_effects=True),
    )(chunks)


KEY_BLOCK = 128


def attention_kernel(groups, head_size, flag_ref, q_ref, kv_ref, mask_ref, out_ref, top_ref, sum_ref, acc_ref):
    n_blocks = flag_ref.shape[0]
    kv_heads = kv_ref.shape[1] // (2 * head_size)
    heads = kv_heads * groups
    value_at = kv_heads * head_size
    scale = head_size ** (-0.5)
    top_ref[...] = jnp.full(top_ref.shape, -1e30, jnp.float32)
    sum_ref[...] = jnp.zeros(sum_ref.shape, jnp.float32)
    acc_ref[...] = jnp.zeros(acc_ref.shape, jnp.float32)

    def allowed_block(j):
        tile_count = mask_ref.shape[1]
        tile_at = lax.broadcasted_iota(jnp.int32, (tile_count, KEY_BLOCK), 0)
        column_tile = lax.broadcasted_iota(jnp.int32, (tile_count, KEY_BLOCK), 1) // TILE
        spread = (tile_at == j * (KEY_BLOCK // TILE) + column_tile).astype(jnp.bfloat16)
        return jnp.dot(mask_ref[...], spread, preferred_element_type=jnp.float32) > 0

    def scores(j, h):
        rows = pl.ds(pl.multiple_of(j * KEY_BLOCK, KEY_BLOCK), KEY_BLOCK)
        key = kv_ref[rows, pl.ds((h // groups) * head_size, head_size)]
        query = q_ref[:, pl.ds(h * head_size, head_size)]
        raw = lax.dot_general(
            query, key, (((1,), (1,)), ((), ())), preferred_element_type=jnp.float32
        )
        return raw * scale, allowed_block(j)

    def first_pass(j, carry):
        @pl.when(flag_ref[j] > 0)
        def _():
            for h in range(heads):
                s, allowed = scores(j, h)
                top_ref[h] = jnp.maximum(top_ref[h], jnp.where(allowed, s, -1e30))
        return carry

    lax.fori_loop(0, n_blocks, first_pass, 0)
    for h in range(heads):
        top_ref[h] = jnp.broadcast_to(jnp.max(top_ref[h], axis=1, keepdims=True), top_ref.shape[1:])

    def second_pass(j, carry):
        @pl.when(flag_ref[j] > 0)
        def _():
            rows = pl.ds(pl.multiple_of(j * KEY_BLOCK, KEY_BLOCK), KEY_BLOCK)
            for h in range(heads):
                s, allowed = scores(j, h)
                weights = jnp.where(allowed, jnp.exp(s - top_ref[h]), 0.0)
                sum_ref[h] += weights
                value = kv_ref[rows, pl.ds(value_at + (h // groups) * head_size, head_size)]
                acc_ref[h] += jnp.dot(
                    weights.astype(jnp.bfloat16), value, preferred_element_type=jnp.float32
                )
        return carry

    lax.fori_loop(0, n_blocks, second_pass, 0)
    for h in range(heads):
        denominator = jnp.sum(sum_ref[h], axis=1, keepdims=True)
        out_ref[:, pl.ds(h * head_size, head_size)] = (acc_ref[h] / denominator).astype(out_ref.dtype)


def block_attention(query_rows, kv_rows, mask_block, groups, head_size):
    row_count = query_rows.shape[0]
    key_count = kv_rows.shape[0]
    heads = query_rows.shape[1] // head_size
    allowed = jnp.repeat(mask_block, TILE, axis=0).astype(jnp.bfloat16)
    tiles_per_block = KEY_BLOCK // TILE
    flags = jnp.max(
        mask_block.reshape(mask_block.shape[0], -1, tiles_per_block), axis=(0, 2)
    ).astype(jnp.int32)
    vmem = pl.BlockSpec(memory_space=pltpu.VMEM)
    return pl.pallas_call(
        functools.partial(attention_kernel, groups, head_size),
        out_shape=jax.ShapeDtypeStruct((row_count, heads * head_size), jnp.bfloat16),
        in_specs=[pl.BlockSpec(memory_space=pltpu.SMEM), vmem, vmem, vmem],
        out_specs=vmem,
        scratch_shapes=[
            pltpu.VMEM((heads, row_count, KEY_BLOCK), jnp.float32),
            pltpu.VMEM((heads, row_count, KEY_BLOCK), jnp.float32),
            pltpu.VMEM((heads, row_count, head_size), jnp.float32),
        ],
    )(flags, query_rows, kv_rows, allowed)


def shards(
    hidden_in,
    queries,
    key_proj,
    value_proj,
    tile_mask,
    out_weight,
    moe_gain,
    gate_weight,
    up_weight,
    down_weight,
    expert_ids,
    gate_probs,
):
    query_rows = queries[0]
    row_count = query_rows.shape[0]
    groups = HEADS // KV_HEADS
    head_size = D // HEADS
    query_heads = query_rows.reshape(row_count, KV_HEADS, groups, head_size)
    mask_block = tile_mask[0]
    kv_width = key_proj.shape[-1]
    kv_local = jnp.concatenate([key_proj[0], value_proj[0]], axis=-1)
    kv_piece = gather_ctx_kernel(kv_local).reshape(-1, 2 * kv_width)
    attended = block_attention(query_rows, kv_piece, mask_block, groups, head_size)
    projected = jnp.dot(attended, out_weight, preferred_element_type=jnp.float32)
    attention_out = projected.astype(jnp.bfloat16)
    residual = (hidden_in[0].astype(jnp.float32) + projected).astype(jnp.bfloat16)
    normed = rms_scale(residual, moe_gain).astype(jnp.bfloat16)
    id_row = expert_ids[0].reshape(-1)
    onehot = (id_row[:, None] == jnp.arange(EXPERTS, dtype=jnp.int32)[None, :]).astype(jnp.int32)
    before = jnp.cumsum(onehot, axis=0) - onehot
    slot_index = jnp.sum(before * onehot, axis=1)
    target = id_row * CAP + slot_index
    selector = (jnp.arange(EXPERTS * CAP, dtype=jnp.int32)[:, None] == target[None, :]).astype(
        jnp.bfloat16
    )
    repeated = jnp.repeat(normed, TOP, axis=0)
    outgoing = (
        jnp.dot(selector, repeated, preferred_element_type=jnp.float32)
        .astype(jnp.bfloat16)
        .reshape(EXPERTS, CAP, D)
    )
    arrived = exchange_exp(outgoing, 1).reshape(1, EXPERTS * CAP, D)
    ff = gate_weight.shape[-1]
    weight_piece = lax.all_gather(
        jnp.concatenate([gate_weight, up_weight, down_weight], axis=-1), CTX_AXES, axis=1, tiled=True
    )
    gate_piece = weight_piece[..., :ff]
    up_piece = weight_piece[..., ff : 2 * ff]
    down_piece = weight_piece[..., 2 * ff :]
    both_sums = jnp.dot(arrived[0], weight_piece[0, :, : 2 * ff], preferred_element_type=jnp.float32)
    gate_sum = both_sums[None, :, :ff]
    up_sum = both_sums[None, :, ff:]
    hidden = (jax.nn.silu(gate_sum) * up_sum).astype(jnp.bfloat16)
    expert_rows = jnp.einsum(
        "esf,edf->esd",
        hidden,
        down_piece,
        preferred_element_type=jnp.float32,
    ).astype(jnp.bfloat16)
    returned = exchange_exp(expert_rows.reshape(EXPERTS, CAP, D), 2)
    combine = jnp.sum(
        jnp.where(
            jnp.arange(EXPERTS * CAP, dtype=jnp.int32)[None, None, :] == target.reshape(row_count, TOP)[:, :, None],
            gate_probs[0][:, :, None],
            0.0,
        ),
        axis=1,
    )
    mixture = jnp.dot(
        combine,
        returned.reshape(EXPERTS * CAP, D).astype(jnp.float32),
        precision=lax.Precision.HIGHEST,
        preferred_element_type=jnp.float32,
    )
    layer_out = (residual.astype(jnp.float32) + mixture).astype(jnp.bfloat16)
    return (attention_out[None], layer_out[None])


def solution(mesh):
    n_ctx = mesh.shape["ctx"]
    split = jax.sharding.Mesh(
        mesh.devices.reshape(n_ctx // 4, 2, 2, mesh.shape["exp"]), CTX_AXES + ("exp",)
    )
    return jax.shard_map(
        shards,
        mesh=split,
        in_specs=(
            P("exp", CTX_AXES, None),
            P("exp", CTX_AXES, None),
            P("exp", CTX_AXES, None),
            P("exp", CTX_AXES, None),
            P("exp", CTX_AXES, None),
            P(),
            P(),
            P("exp", CTX_AXES, None),
            P("exp", CTX_AXES, None),
            P("exp", CTX_AXES, None),
            P("exp", CTX_AXES, None),
            P("exp", CTX_AXES, None),
        ),
        out_specs=(P("exp", CTX_AXES, None), P("exp", CTX_AXES, None)),
        check_vma=False,
    )
```

```python
import functools

import jax
import jax.numpy as jnp
from jax import lax
from jax.experimental import pallas as pl
from jax.experimental.pallas import tpu as pltpu
from jax.sharding import PartitionSpec as P

D = 1024
HEADS = 8
KV_HEADS = 2
EXPERTS = 8
TOP = 2
TILE = 32
CAP = 72


def rms_scale(row_block, gain):
    widened = row_block.astype(jnp.float32)
    inverse = lax.rsqrt(jnp.mean(widened * widened, axis=-1, keepdims=True) + 1e-05)
    return widened * inverse * gain


CTX_AXES = ("z", "yh", "core")


MESH = pl.DeviceIdType.MESH


def gather_kernel(n_z, shard_ref, out_ref, local_sem, send_sem, recv_sem):
    z = lax.axis_index("z")
    yh = lax.axis_index("yh")
    core = lax.axis_index("core")
    ex = lax.axis_index("exp")

    def slot(zz, hh, cc):
        return (zz * 2 + hh) * 2 + cc

    def ring(offset):
        return lax.rem(z + offset + 4 * n_z, n_z)

    partner_h = 1 - yh
    sibling_c = 1 - core
    to_right = (ring(1), yh, core, ex)
    to_left = (ring(-1), yh, core, ex)
    to_partner = (z, partner_h, core, ex)
    to_sibling = (z, yh, sibling_c, ex)
    barrier = pltpu.get_barrier_semaphore()
    for dev in (to_right, to_left, to_partner, to_sibling):
        pl.semaphore_signal(barrier, 1, device_id=dev, device_id_type=MESH)
    pl.semaphore_wait(barrier, 4)

    me = slot(z, yh, core)
    own = pltpu.make_async_copy(shard_ref, out_ref.at[me], local_sem)
    own.start()
    sends = []

    def send(src, s, dev, k):
        copy = pltpu.make_async_remote_copy(
            src, out_ref.at[s], send_sem.at[k, s], recv_sem.at[s], device_id=dev, device_id_type=MESH
        )
        copy.start()
        sends.append(copy)

    def arrive(s):
        pltpu.make_async_remote_copy(
            out_ref.at[s], out_ref.at[s], send_sem.at[0, s], recv_sem.at[s],
            device_id=to_right, device_id_type=MESH,
        ).wait_recv()

    for k, dev in enumerate((to_right, to_left, to_partner, to_sibling)):
        send(shard_ref, me, dev, k)
    half = n_z // 2
    for t in range(1, half + 1):
        s = slot(ring(-t), yh, core)
        arrive(s)
        if t < half:
            send(out_ref.at[s], s, to_right, 0)
        send(out_ref.at[s], s, to_partner, 2)
        send(out_ref.at[s], s, to_sibling, 3)
        if t < n_z - half:
            s = slot(ring(t), yh, core)
            arrive(s)
            if t < n_z - half - 1:
                send(out_ref.at[s], s, to_left, 1)
            send(out_ref.at[s], s, to_partner, 2)
            send(out_ref.at[s], s, to_sibling, 3)
    partner_order = [0]
    for t in range(1, half + 1):
        partner_order.append(-t)
        if t < n_z - half:
            partner_order.append(t)
    for offset in partner_order:
        s = slot(ring(offset), partner_h, core)
        arrive(s)
        send(out_ref.at[s], s, to_sibling, 3)
    for hh in (yh, partner_h):
        for offset in partner_order:
            arrive(slot(ring(offset), hh, sibling_c))
    own.wait()
    for copy in sends:
        copy.wait_send()


def gather_ctx_kernel(block):
    n_z = lax.axis_size("z")
    n_all = n_z * 4
    return pl.pallas_call(
        functools.partial(gather_kernel, n_z),
        out_shape=jax.ShapeDtypeStruct((n_all,) + block.shape, block.dtype),
        in_specs=[pl.BlockSpec(memory_space=pl.ANY)],
        out_specs=pl.BlockSpec(memory_space=pl.ANY),
        scratch_shapes=[
            pltpu.SemaphoreType.DMA(()),
            pltpu.SemaphoreType.DMA((4, n_all)),
            pltpu.SemaphoreType.DMA((n_all,)),
        ],
        compiler_params=pltpu.CompilerParams(collective_id=0, has_side_effects=True),
    )(block)


def exchange_kernel(n_exp, chunk_ref, out_ref, local_sem, send_sem, recv_sem):
    me = lax.axis_index("exp")
    z = lax.axis_index("z")
    yh = lax.axis_index("yh")
    core = lax.axis_index("core")

    def peer(offset):
        return lax.rem(me + offset, n_exp)

    barrier = pltpu.get_barrier_semaphore()
    for offset in range(1, n_exp):
        pl.semaphore_signal(barrier, 1, device_id=(z, yh, core, peer(offset)), device_id_type=MESH)
    pl.semaphore_wait(barrier, n_exp - 1)
    own = pltpu.make_async_copy(chunk_ref.at[me], out_ref.at[me], local_sem)
    own.start()
    sends = []
    for offset in range(1, n_exp):
        target = peer(offset)
        copy = pltpu.make_async_remote_copy(
            chunk_ref.at[target], out_ref.at[me], send_sem.at[offset], recv_sem.at[me],
            device_id=(z, yh, core, target), device_id_type=MESH,
        )
        copy.start()
        sends.append(copy)
    for offset in range(1, n_exp):
        source = peer(n_exp - offset)
        pltpu.make_async_remote_copy(
            out_ref.at[source], out_ref.at[source], send_sem.at[offset], recv_sem.at[source],
            device_id=(z, yh, core, source), device_id_type=MESH,
        ).wait_recv()
    own.wait()
    for copy in sends:
        copy.wait_send()


def exchange_exp(chunks, collective_id):
    n_exp = chunks.shape[0]
    return pl.pallas_call(
        functools.partial(exchange_kernel, n_exp),
        out_shape=jax.ShapeDtypeStruct(chunks.shape, chunks.dtype),
        in_specs=[pl.BlockSpec(memory_space=pl.ANY)],
        out_specs=pl.BlockSpec(memory_space=pl.ANY),
        scratch_shapes=[
            pltpu.SemaphoreType.DMA(()),
            pltpu.SemaphoreType.DMA((n_exp,)),
            pltpu.SemaphoreType.DMA((n_exp,)),
        ],
        compiler_params=pltpu.CompilerParams(collective_id=collective_id, has_side_effects=True),
    )(chunks)


KEY_BLOCK = 128


def attention_kernel(groups, head_size, flag_ref, q_ref, kv_ref, mask_ref, out_ref, top_ref, sum_ref, acc_ref):
    n_blocks = flag_ref.shape[0]
    kv_heads = kv_ref.shape[1] // (2 * head_size)
    heads = kv_heads * groups
    value_at = kv_heads * head_size
    scale = head_size ** (-0.5)
    top_ref[...] = jnp.full(top_ref.shape, -1e30, jnp.float32)
    sum_ref[...] = jnp.zeros(sum_ref.shape, jnp.float32)
    acc_ref[...] = jnp.zeros(acc_ref.shape, jnp.float32)

    def allowed_block(j):
        tile_count = mask_ref.shape[1]
        tile_at = lax.broadcasted_iota(jnp.int32, (tile_count, KEY_BLOCK), 0)
        column_tile = lax.broadcasted_iota(jnp.int32, (tile_count, KEY_BLOCK), 1) // TILE
        spread = (tile_at == j * (KEY_BLOCK // TILE) + column_tile).astype(jnp.bfloat16)
        return jnp.dot(mask_ref[...], spread, preferred_element_type=jnp.float32) > 0

    def scores(j, h):
        rows = pl.ds(pl.multiple_of(j * KEY_BLOCK, KEY_BLOCK), KEY_BLOCK)
        key = kv_ref[rows, pl.ds((h // groups) * head_size, head_size)]
        query = q_ref[:, pl.ds(h * head_size, head_size)]
        raw = lax.dot_general(
            query, key, (((1,), (1,)), ((), ())), preferred_element_type=jnp.float32
        )
        return raw * scale, allowed_block(j)

    def first_pass(j, carry):
        @pl.when(flag_ref[j] > 0)
        def _():
            for h in range(heads):
                s, allowed = scores(j, h)
                top_ref[h] = jnp.maximum(top_ref[h], jnp.where(allowed, s, -1e30))
        return carry

    lax.fori_loop(0, n_blocks, first_pass, 0)
    for h in range(heads):
        top_ref[h] = jnp.broadcast_to(jnp.max(top_ref[h], axis=1, keepdims=True), top_ref.shape[1:])

    def second_pass(j, carry):
        @pl.when(flag_ref[j] > 0)
        def _():
            rows = pl.ds(pl.multiple_of(j * KEY_BLOCK, KEY_BLOCK), KEY_BLOCK)
            for h in range(heads):
                s, allowed = scores(j, h)
                weights = jnp.where(allowed, jnp.exp(s - top_ref[h]), 0.0)
                sum_ref[h] += weights
                value = kv_ref[rows, pl.ds(value_at + (h // groups) * head_size, head_size)]
                acc_ref[h] += jnp.dot(
                    weights.astype(jnp.bfloat16), value, preferred_element_type=jnp.float32
                )
        return carry

    lax.fori_loop(0, n_blocks, second_pass, 0)
    for h in range(heads):
        denominator = jnp.sum(sum_ref[h], axis=1, keepdims=True)
        out_ref[:, pl.ds(h * head_size, head_size)] = (acc_ref[h] / denominator).astype(out_ref.dtype)


def block_attention(query_rows, kv_rows, mask_block, groups, head_size):
    row_count = query_rows.shape[0]
    key_count = kv_rows.shape[0]
    heads = query_rows.shape[1] // head_size
    allowed = jnp.repeat(mask_block, TILE, axis=0).astype(jnp.bfloat16)
    tiles_per_block = KEY_BLOCK // TILE
    flags = jnp.max(
        mask_block.reshape(mask_block.shape[0], -1, tiles_per_block), axis=(0, 2)
    ).astype(jnp.int32)
    vmem = pl.BlockSpec(memory_space=pltpu.VMEM)
    return pl.pallas_call(
        functools.partial(attention_kernel, groups, head_size),
        out_shape=jax.ShapeDtypeStruct((row_count, heads * head_size), jnp.bfloat16),
        in_specs=[pl.BlockSpec(memory_space=pltpu.SMEM), vmem, vmem, vmem],
        out_specs=vmem,
        scratch_shapes=[
            pltpu.VMEM((heads, row_count, KEY_BLOCK), jnp.float32),
            pltpu.VMEM((heads, row_count, KEY_BLOCK), jnp.float32),
            pltpu.VMEM((heads, row_count, head_size), jnp.float32),
        ],
    )(flags, query_rows, kv_rows, allowed)


def shards(
    hidden_in,
    queries,
    key_proj,
    value_proj,
    tile_mask,
    out_weight,
    moe_gain,
    gate_weight,
    up_weight,
    down_weight,
    expert_ids,
    gate_probs,
):
    query_rows = queries[0]
    row_count = query_rows.shape[0]
    groups = HEADS // KV_HEADS
    head_size = D // HEADS
    query_heads = query_rows.reshape(row_count, KV_HEADS, groups, head_size)
    mask_block = tile_mask[0]
    kv_width = key_proj.shape[-1]
    kv_local = jnp.concatenate([key_proj[0], value_proj[0]], axis=-1)
    kv_piece = gather_ctx_kernel(kv_local).reshape(-1, 2 * kv_width)
    attended = block_attention(query_rows, kv_piece, mask_block, groups, head_size)
    projected = jnp.dot(attended, out_weight, preferred_element_type=jnp.float32)
    attention_out = projected.astype(jnp.bfloat16)
    residual = (hidden_in[0].astype(jnp.float32) + projected).astype(jnp.bfloat16)
    normed = rms_scale(residual, moe_gain).astype(jnp.bfloat16)
    id_row = expert_ids[0].reshape(-1)
    onehot = (id_row[:, None] == jnp.arange(EXPERTS, dtype=jnp.int32)[None, :]).astype(jnp.int32)
    before = jnp.cumsum(onehot, axis=0) - onehot
    slot_index = jnp.sum(before * onehot, axis=1)
    target = id_row * CAP + slot_index
    selector = (jnp.arange(EXPERTS * CAP, dtype=jnp.int32)[:, None] == target[None, :]).astype(
        jnp.bfloat16
    )
    repeated = jnp.repeat(normed, TOP, axis=0)
    outgoing = (
        jnp.dot(selector, repeated, preferred_element_type=jnp.float32)
        .astype(jnp.bfloat16)
        .reshape(EXPERTS, CAP, D)
    )
    arrived = exchange_exp(outgoing, 1).reshape(1, EXPERTS * CAP, D)
    ff = gate_weight.shape[-1]
    weight_piece = lax.all_gather(
        jnp.concatenate([gate_weight, up_weight, down_weight], axis=-1), CTX_AXES, axis=1, tiled=True
    )
    gate_piece = weight_piece[..., :ff]
    up_piece = weight_piece[..., ff : 2 * ff]
    down_piece = weight_piece[..., 2 * ff :]
    both_sums = jnp.dot(arrived[0], weight_piece[0, :, : 2 * ff], preferred_element_type=jnp.float32)
    gate_sum = both_sums[None, :, :ff]
    up_sum = both_sums[None, :, ff:]
    hidden = (jax.nn.silu(gate_sum) * up_sum).astype(jnp.bfloat16)
    expert_rows = jnp.einsum(
        "esf,edf->esd",
        hidden,
        down_piece,
        preferred_element_type=jnp.float32,
    ).astype(jnp.bfloat16)
    returned = exchange_exp(expert_rows.reshape(EXPERTS, CAP, D), 2)
    combine = jnp.sum(
        jnp.where(
            jnp.arange(EXPERTS * CAP, dtype=jnp.int32)[None, None, :] == target.reshape(row_count, TOP)[:, :, None],
            gate_probs[0][:, :, None],
            0.0,
        ),
        axis=1,
    )
    mixture = jnp.dot(
        combine,
        returned.reshape(EXPERTS * CAP, D).astype(jnp.float32),
        precision=lax.Precision.HIGH,
        preferred_element_type=jnp.float32,
    )
    layer_out = (residual.astype(jnp.float32) + mixture).astype(jnp.bfloat16)
    return (attention_out[None], layer_out[None])


def solution(mesh):
    n_ctx = mesh.shape["ctx"]
    split = jax.sharding.Mesh(
        mesh.devices.reshape(n_ctx // 4, 2, 2, mesh.shape["exp"]), CTX_AXES + ("exp",)
    )
    return jax.shard_map(
        shards,
        mesh=split,
        in_specs=(
            P("exp", CTX_AXES, None),
            P("exp", CTX_AXES, None),
            P("exp", CTX_AXES, None),
            P("exp", CTX_AXES, None),
            P("exp", CTX_AXES, None),
            P(),
            P(),
            P("exp", CTX_AXES, None),
            P("exp", CTX_AXES, None),
            P("exp", CTX_AXES, None),
            P("exp", CTX_AXES, None),
            P("exp", CTX_AXES, None),
        ),
        out_specs=(P("exp", CTX_AXES, None), P("exp", CTX_AXES, None)),
        check_vma=False,
    )
```

```python
import functools

import jax
import jax.numpy as jnp
from jax import lax
from jax.experimental import pallas as pl
from jax.experimental.pallas import tpu as pltpu
from jax.sharding import PartitionSpec as P

D = 1024
HEADS = 8
KV_HEADS = 2
EXPERTS = 8
TOP = 2
TILE = 32
CAP = 72


def rms_scale(row_block, gain):
    widened = row_block.astype(jnp.float32)
    inverse = lax.rsqrt(jnp.mean(widened * widened, axis=-1, keepdims=True) + 1e-05)
    return widened * inverse * gain


CTX_AXES = ("z", "yh", "core")


MESH = pl.DeviceIdType.MESH


def gather_kernel(n_z, shard_ref, out_ref, local_sem, send_sem, recv_sem):
    z = lax.axis_index("z")
    yh = lax.axis_index("yh")
    core = lax.axis_index("core")
    ex = lax.axis_index("exp")

    def slot(zz, hh, cc):
        return (zz * 2 + hh) * 2 + cc

    def ring(offset):
        return lax.rem(z + offset + 4 * n_z, n_z)

    partner_h = 1 - yh
    sibling_c = 1 - core
    to_right = (ring(1), yh, core, ex)
    to_left = (ring(-1), yh, core, ex)
    to_partner = (z, partner_h, core, ex)
    to_sibling = (z, yh, sibling_c, ex)
    barrier = pltpu.get_barrier_semaphore()
    for dev in (to_right, to_left, to_partner, to_sibling):
        pl.semaphore_signal(barrier, 1, device_id=dev, device_id_type=MESH)
    pl.semaphore_wait(barrier, 4)

    me = slot(z, yh, core)
    own = pltpu.make_async_copy(shard_ref, out_ref.at[me], local_sem)
    own.start()
    sends = []

    def send(src, s, dev, k):
        copy = pltpu.make_async_remote_copy(
            src, out_ref.at[s], send_sem.at[k, s], recv_sem.at[s], device_id=dev, device_id_type=MESH
        )
        copy.start()
        sends.append(copy)

    def arrive(s):
        pltpu.make_async_remote_copy(
            out_ref.at[s], out_ref.at[s], send_sem.at[0, s], recv_sem.at[s],
            device_id=to_right, device_id_type=MESH,
        ).wait_recv()

    for k, dev in enumerate((to_right, to_left, to_partner, to_sibling)):
        send(shard_ref, me, dev, k)
    half = n_z // 2
    for t in range(1, half + 1):
        s = slot(ring(-t), yh, core)
        arrive(s)
        if t < half:
            send(out_ref.at[s], s, to_right, 0)
        send(out_ref.at[s], s, to_partner, 2)
        send(out_ref.at[s], s, to_sibling, 3)
        if t < n_z - half:
            s = slot(ring(t), yh, core)
            arrive(s)
            if t < n_z - half - 1:
                send(out_ref.at[s], s, to_left, 1)
            send(out_ref.at[s], s, to_partner, 2)
            send(out_ref.at[s], s, to_sibling, 3)
    partner_order = [0]
    for t in range(1, half + 1):
        partner_order.append(-t)
        if t < n_z - half:
            partner_order.append(t)
    for offset in partner_order:
        s = slot(ring(offset), partner_h, core)
        arrive(s)
        send(out_ref.at[s], s, to_sibling, 3)
    for hh in (yh, partner_h):
        for offset in partner_order:
            arrive(slot(ring(offset), hh, sibling_c))
    own.wait()
    for copy in sends:
        copy.wait_send()


def gather_ctx_kernel(block):
    n_z = lax.axis_size("z")
    n_all = n_z * 4
    return pl.pallas_call(
        functools.partial(gather_kernel, n_z),
        out_shape=jax.ShapeDtypeStruct((n_all,) + block.shape, block.dtype),
        in_specs=[pl.BlockSpec(memory_space=pl.ANY)],
        out_specs=pl.BlockSpec(memory_space=pl.ANY),
        scratch_shapes=[
            pltpu.SemaphoreType.DMA(()),
            pltpu.SemaphoreType.DMA((4, n_all)),
            pltpu.SemaphoreType.DMA((n_all,)),
        ],
        compiler_params=pltpu.CompilerParams(collective_id=0, has_side_effects=True),
    )(block)


def exchange_kernel(n_exp, chunk_ref, out_ref, send_sem, recv_sem):
    me = lax.axis_index("exp")
    z = lax.axis_index("z")
    yh = lax.axis_index("yh")
    core = lax.axis_index("core")

    def peer(offset):
        return lax.rem(me + offset, n_exp)

    barrier = pltpu.get_barrier_semaphore()
    for offset in range(1, n_exp):
        pl.semaphore_signal(barrier, 1, device_id=(z, yh, core, peer(offset)), device_id_type=MESH)
    pl.semaphore_wait(barrier, n_exp - 1)
    sends = []
    for offset in range(1, n_exp):
        target = peer(offset)
        copy = pltpu.make_async_remote_copy(
            chunk_ref.at[target], out_ref.at[me], send_sem.at[offset], recv_sem.at[me],
            device_id=(z, yh, core, target), device_id_type=MESH,
        )
        copy.start()
        sends.append(copy)
    for offset in range(1, n_exp):
        source = peer(n_exp - offset)
        pltpu.make_async_remote_copy(
            out_ref.at[source], out_ref.at[source], send_sem.at[offset], recv_sem.at[source],
            device_id=(z, yh, core, source), device_id_type=MESH,
        ).wait_recv()
    for copy in sends:
        copy.wait_send()


def exchange_exp(chunks, collective_id):
    n_exp = chunks.shape[0]
    exchanged = pl.pallas_call(
        functools.partial(exchange_kernel, n_exp),
        out_shape=jax.ShapeDtypeStruct(chunks.shape, chunks.dtype),
        in_specs=[pl.BlockSpec(memory_space=pl.ANY)],
        out_specs=pl.BlockSpec(memory_space=pl.ANY),
        scratch_shapes=[
            pltpu.SemaphoreType.DMA((n_exp,)),
            pltpu.SemaphoreType.DMA((n_exp,)),
        ],
        compiler_params=pltpu.CompilerParams(collective_id=collective_id, has_side_effects=True),
    )(chunks)
    me = lax.axis_index("exp")
    return lax.dynamic_update_slice(exchanged, lax.dynamic_slice_in_dim(chunks, me, 1, 0), (me, 0, 0))


KEY_BLOCK = 128


def attention_kernel(groups, head_size, flag_ref, q_ref, kv_ref, mask_ref, out_ref, top_ref, sum_ref, acc_ref):
    n_blocks = flag_ref.shape[0]
    kv_heads = kv_ref.shape[1] // (2 * head_size)
    heads = kv_heads * groups
    value_at = kv_heads * head_size
    scale = head_size ** (-0.5)
    top_ref[...] = jnp.full(top_ref.shape, -1e30, jnp.float32)
    sum_ref[...] = jnp.zeros(sum_ref.shape, jnp.float32)
    acc_ref[...] = jnp.zeros(acc_ref.shape, jnp.float32)

    def allowed_block(j):
        tile_count = mask_ref.shape[1]
        tile_at = lax.broadcasted_iota(jnp.int32, (tile_count, KEY_BLOCK), 0)
        column_tile = lax.broadcasted_iota(jnp.int32, (tile_count, KEY_BLOCK), 1) // TILE
        spread = (tile_at == j * (KEY_BLOCK // TILE) + column_tile).astype(jnp.bfloat16)
        return jnp.dot(mask_ref[...], spread, preferred_element_type=jnp.float32) > 0

    def scores(j, h):
        rows = pl.ds(pl.multiple_of(j * KEY_BLOCK, KEY_BLOCK), KEY_BLOCK)
        key = kv_ref[rows, pl.ds((h // groups) * head_size, head_size)]
        query = q_ref[:, pl.ds(h * head_size, head_size)]
        raw = lax.dot_general(
            query, key, (((1,), (1,)), ((), ())), preferred_element_type=jnp.float32
        )
        return raw * scale, allowed_block(j)

    def first_pass(j, carry):
        @pl.when(flag_ref[j] > 0)
        def _():
            for h in range(heads):
                s, allowed = scores(j, h)
                top_ref[h] = jnp.maximum(top_ref[h], jnp.where(allowed, s, -1e30))
        return carry

    lax.fori_loop(0, n_blocks, first_pass, 0)
    for h in range(heads):
        top_ref[h] = jnp.broadcast_to(jnp.max(top_ref[h], axis=1, keepdims=True), top_ref.shape[1:])

    def second_pass(j, carry):
        @pl.when(flag_ref[j] > 0)
        def _():
            rows = pl.ds(pl.multiple_of(j * KEY_BLOCK, KEY_BLOCK), KEY_BLOCK)
            for h in range(heads):
                s, allowed = scores(j, h)
                weights = jnp.where(allowed, jnp.exp(s - top_ref[h]), 0.0)
                sum_ref[h] += weights
                value = kv_ref[rows, pl.ds(value_at + (h // groups) * head_size, head_size)]
                acc_ref[h] += jnp.dot(
                    weights.astype(jnp.bfloat16), value, preferred_element_type=jnp.float32
                )
        return carry

    lax.fori_loop(0, n_blocks, second_pass, 0)
    for h in range(heads):
        denominator = jnp.sum(sum_ref[h], axis=1, keepdims=True)
        out_ref[:, pl.ds(h * head_size, head_size)] = (acc_ref[h] / denominator).astype(out_ref.dtype)


def block_attention(query_rows, kv_rows, mask_block, groups, head_size):
    row_count = query_rows.shape[0]
    key_count = kv_rows.shape[0]
    heads = query_rows.shape[1] // head_size
    allowed = jnp.repeat(mask_block, TILE, axis=0).astype(jnp.bfloat16)
    tiles_per_block = KEY_BLOCK // TILE
    flags = jnp.max(
        mask_block.reshape(mask_block.shape[0], -1, tiles_per_block), axis=(0, 2)
    ).astype(jnp.int32)
    vmem = pl.BlockSpec(memory_space=pltpu.VMEM)
    return pl.pallas_call(
        functools.partial(attention_kernel, groups, head_size),
        out_shape=jax.ShapeDtypeStruct((row_count, heads * head_size), jnp.bfloat16),
        in_specs=[pl.BlockSpec(memory_space=pltpu.SMEM), vmem, vmem, vmem],
        out_specs=vmem,
        scratch_shapes=[
            pltpu.VMEM((heads, row_count, KEY_BLOCK), jnp.float32),
            pltpu.VMEM((heads, row_count, KEY_BLOCK), jnp.float32),
            pltpu.VMEM((heads, row_count, head_size), jnp.float32),
        ],
    )(flags, query_rows, kv_rows, allowed)


def shards(
    hidden_in,
    queries,
    key_proj,
    value_proj,
    tile_mask,
    out_weight,
    moe_gain,
    gate_weight,
    up_weight,
    down_weight,
    expert_ids,
    gate_probs,
):
    query_rows = queries[0]
    row_count = query_rows.shape[0]
    groups = HEADS // KV_HEADS
    head_size = D // HEADS
    query_heads = query_rows.reshape(row_count, KV_HEADS, groups, head_size)
    mask_block = tile_mask[0]
    kv_width = key_proj.shape[-1]
    kv_local = jnp.concatenate([key_proj[0], value_proj[0]], axis=-1)
    kv_piece = gather_ctx_kernel(kv_local).reshape(-1, 2 * kv_width)
    attended = block_attention(query_rows, kv_piece, mask_block, groups, head_size)
    projected = jnp.dot(attended, out_weight, preferred_element_type=jnp.float32)
    attention_out = projected.astype(jnp.bfloat16)
    residual = (hidden_in[0].astype(jnp.float32) + projected).astype(jnp.bfloat16)
    normed = rms_scale(residual, moe_gain).astype(jnp.bfloat16)
    id_row = expert_ids[0].reshape(-1)
    onehot = (id_row[:, None] == jnp.arange(EXPERTS, dtype=jnp.int32)[None, :]).astype(jnp.int32)
    before = jnp.cumsum(onehot, axis=0) - onehot
    slot_index = jnp.sum(before * onehot, axis=1)
    target = id_row * CAP + slot_index
    selector = (jnp.arange(EXPERTS * CAP, dtype=jnp.int32)[:, None] == target[None, :]).astype(
        jnp.bfloat16
    )
    repeated = jnp.repeat(normed, TOP, axis=0)
    outgoing = (
        jnp.dot(selector, repeated, preferred_element_type=jnp.float32)
        .astype(jnp.bfloat16)
        .reshape(EXPERTS, CAP, D)
    )
    arrived = exchange_exp(outgoing, 1).reshape(1, EXPERTS * CAP, D)
    ff = gate_weight.shape[-1]
    weight_piece = lax.all_gather(
        jnp.concatenate([gate_weight, up_weight, down_weight], axis=-1), CTX_AXES, axis=1, tiled=True
    )
    gate_piece = weight_piece[..., :ff]
    up_piece = weight_piece[..., ff : 2 * ff]
    down_piece = weight_piece[..., 2 * ff :]
    both_sums = jnp.dot(arrived[0], weight_piece[0, :, : 2 * ff], preferred_element_type=jnp.float32)
    gate_sum = both_sums[None, :, :ff]
    up_sum = both_sums[None, :, ff:]
    hidden = (jax.nn.silu(gate_sum) * up_sum).astype(jnp.bfloat16)
    expert_rows = jnp.einsum(
        "esf,edf->esd",
        hidden,
        down_piece,
        preferred_element_type=jnp.float32,
    ).astype(jnp.bfloat16)
    returned = exchange_exp(expert_rows.reshape(EXPERTS, CAP, D), 2)
    combine = jnp.sum(
        jnp.where(
            jnp.arange(EXPERTS * CAP, dtype=jnp.int32)[None, None, :] == target.reshape(row_count, TOP)[:, :, None],
            gate_probs[0][:, :, None],
            0.0,
        ),
        axis=1,
    )
    mixture = jnp.dot(
        combine,
        returned.reshape(EXPERTS * CAP, D).astype(jnp.float32),
        precision=lax.Precision.HIGHEST,
        preferred_element_type=jnp.float32,
    )
    layer_out = (residual.astype(jnp.float32) + mixture).astype(jnp.bfloat16)
    return (attention_out[None], layer_out[None])


def solution(mesh):
    n_ctx = mesh.shape["ctx"]
    split = jax.sharding.Mesh(
        mesh.devices.reshape(n_ctx // 4, 2, 2, mesh.shape["exp"]), CTX_AXES + ("exp",)
    )
    return jax.shard_map(
        shards,
        mesh=split,
        in_specs=(
            P("exp", CTX_AXES, None),
            P("exp", CTX_AXES, None),
            P("exp", CTX_AXES, None),
            P("exp", CTX_AXES, None),
            P("exp", CTX_AXES, None),
            P(),
            P(),
            P("exp", CTX_AXES, None),
            P("exp", CTX_AXES, None),
            P("exp", CTX_AXES, None),
            P("exp", CTX_AXES, None),
            P("exp", CTX_AXES, None),
        ),
        out_specs=(P("exp", CTX_AXES, None), P("exp", CTX_AXES, None)),
        check_vma=False,
    )
```

```python
import functools

import jax
import jax.numpy as jnp
from jax import lax
from jax.experimental import pallas as pl
from jax.experimental.pallas import tpu as pltpu
from jax.sharding import PartitionSpec as P

D = 1024
HEADS = 8
KV_HEADS = 2
EXPERTS = 8
TOP = 2
TILE = 32
CAP = 72


def rms_scale(row_block, gain):
    widened = row_block.astype(jnp.float32)
    inverse = lax.rsqrt(jnp.mean(widened * widened, axis=-1, keepdims=True) + 1e-05)
    return widened * inverse * gain


CTX_AXES = ("z", "yh", "core")


MESH = pl.DeviceIdType.MESH


def gather_kernel(n_z, shard_ref, out_ref, local_sem, send_sem, recv_sem):
    z = lax.axis_index("z")
    yh = lax.axis_index("yh")
    core = lax.axis_index("core")
    ex = lax.axis_index("exp")

    def slot(zz, hh, cc):
        return (zz * 2 + hh) * 2 + cc

    def ring(offset):
        return lax.rem(z + offset + 4 * n_z, n_z)

    partner_h = 1 - yh
    sibling_c = 1 - core
    to_right = (ring(1), yh, core, ex)
    to_left = (ring(-1), yh, core, ex)
    to_partner = (z, partner_h, core, ex)
    to_sibling = (z, yh, sibling_c, ex)
    barrier = pltpu.get_barrier_semaphore()
    for dev in (to_right, to_left, to_partner, to_sibling):
        pl.semaphore_signal(barrier, 1, device_id=dev, device_id_type=MESH)
    pl.semaphore_wait(barrier, 4)

    me = slot(z, yh, core)
    own = pltpu.make_async_copy(shard_ref, out_ref.at[me], local_sem)
    own.start()
    sends = []

    def send(src, s, dev, k):
        copy = pltpu.make_async_remote_copy(
            src, out_ref.at[s], send_sem.at[k, s], recv_sem.at[s], device_id=dev, device_id_type=MESH
        )
        copy.start()
        sends.append(copy)

    def arrive(s):
        pltpu.make_async_remote_copy(
            out_ref.at[s], out_ref.at[s], send_sem.at[0, s], recv_sem.at[s],
            device_id=to_right, device_id_type=MESH,
        ).wait_recv()

    for k, dev in enumerate((to_right, to_left, to_partner, to_sibling)):
        send(shard_ref, me, dev, k)
    half = n_z // 2
    for t in range(1, half + 1):
        s = slot(ring(-t), yh, core)
        arrive(s)
        if t < half:
            send(out_ref.at[s], s, to_right, 0)
        send(out_ref.at[s], s, to_partner, 2)
        send(out_ref.at[s], s, to_sibling, 3)
        if t < n_z - half:
            s = slot(ring(t), yh, core)
            arrive(s)
            if t < n_z - half - 1:
                send(out_ref.at[s], s, to_left, 1)
            send(out_ref.at[s], s, to_partner, 2)
            send(out_ref.at[s], s, to_sibling, 3)
    partner_order = [0]
    for t in range(1, half + 1):
        partner_order.append(-t)
        if t < n_z - half:
            partner_order.append(t)
    for offset in partner_order:
        s = slot(ring(offset), partner_h, core)
        arrive(s)
        send(out_ref.at[s], s, to_sibling, 3)
    for hh in (yh, partner_h):
        for offset in partner_order:
            arrive(slot(ring(offset), hh, sibling_c))
    own.wait()
    for copy in sends:
        copy.wait_send()


def gather_ctx_kernel(block):
    n_z = lax.axis_size("z")
    n_all = n_z * 4
    return pl.pallas_call(
        functools.partial(gather_kernel, n_z),
        out_shape=jax.ShapeDtypeStruct((n_all,) + block.shape, block.dtype),
        in_specs=[pl.BlockSpec(memory_space=pl.ANY)],
        out_specs=pl.BlockSpec(memory_space=pl.ANY),
        scratch_shapes=[
            pltpu.SemaphoreType.DMA(()),
            pltpu.SemaphoreType.DMA((4, n_all)),
            pltpu.SemaphoreType.DMA((n_all,)),
        ],
        compiler_params=pltpu.CompilerParams(collective_id=0, has_side_effects=True),
    )(block)


def exchange_kernel(n_exp, chunk_ref, out_ref, local_sem, send_sem, recv_sem):
    me = lax.axis_index("exp")
    z = lax.axis_index("z")
    yh = lax.axis_index("yh")
    core = lax.axis_index("core")

    def peer(offset):
        return lax.rem(me + offset, n_exp)

    barrier = pltpu.get_barrier_semaphore()
    for offset in range(1, n_exp):
        pl.semaphore_signal(barrier, 1, device_id=(z, yh, core, peer(offset)), device_id_type=MESH)
    pl.semaphore_wait(barrier, n_exp - 1)
    own = pltpu.make_async_copy(chunk_ref.at[me], out_ref.at[me], local_sem)
    own.start()
    sends = []
    for offset in range(1, n_exp):
        target = peer(offset)
        copy = pltpu.make_async_remote_copy(
            chunk_ref.at[target], out_ref.at[me], send_sem.at[offset], recv_sem.at[me],
            device_id=(z, yh, core, target), device_id_type=MESH,
        )
        copy.start()
        sends.append(copy)
    for offset in range(1, n_exp):
        source = peer(n_exp - offset)
        pltpu.make_async_remote_copy(
            out_ref.at[source], out_ref.at[source], send_sem.at[offset], recv_sem.at[source],
            device_id=(z, yh, core, source), device_id_type=MESH,
        ).wait_recv()
    own.wait()
    for copy in sends:
        copy.wait_send()


def exchange_exp(chunks, collective_id):
    n_exp = chunks.shape[0]
    return pl.pallas_call(
        functools.partial(exchange_kernel, n_exp),
        out_shape=jax.ShapeDtypeStruct(chunks.shape, chunks.dtype),
        in_specs=[pl.BlockSpec(memory_space=pltpu.VMEM)],
        out_specs=pl.BlockSpec(memory_space=pl.ANY),
        scratch_shapes=[
            pltpu.SemaphoreType.DMA(()),
            pltpu.SemaphoreType.DMA((n_exp,)),
            pltpu.SemaphoreType.DMA((n_exp,)),
        ],
        compiler_params=pltpu.CompilerParams(collective_id=collective_id, has_side_effects=True),
    )(chunks)


KEY_BLOCK = 128


def attention_kernel(groups, head_size, flag_ref, q_ref, kv_ref, mask_ref, out_ref, top_ref, sum_ref, acc_ref):
    n_blocks = flag_ref.shape[0]
    kv_heads = kv_ref.shape[1] // (2 * head_size)
    heads = kv_heads * groups
    value_at = kv_heads * head_size
    scale = head_size ** (-0.5)
    top_ref[...] = jnp.full(top_ref.shape, -1e30, jnp.float32)
    sum_ref[...] = jnp.zeros(sum_ref.shape, jnp.float32)
    acc_ref[...] = jnp.zeros(acc_ref.shape, jnp.float32)

    def allowed_block(j):
        tile_count = mask_ref.shape[1]
        tile_at = lax.broadcasted_iota(jnp.int32, (tile_count, KEY_BLOCK), 0)
        column_tile = lax.broadcasted_iota(jnp.int32, (tile_count, KEY_BLOCK), 1) // TILE
        spread = (tile_at == j * (KEY_BLOCK // TILE) + column_tile).astype(jnp.bfloat16)
        return jnp.dot(mask_ref[...], spread, preferred_element_type=jnp.float32) > 0

    def scores(j, h):
        rows = pl.ds(pl.multiple_of(j * KEY_BLOCK, KEY_BLOCK), KEY_BLOCK)
        key = kv_ref[rows, pl.ds((h // groups) * head_size, head_size)]
        query = q_ref[:, pl.ds(h * head_size, head_size)]
        raw = lax.dot_general(
            query, key, (((1,), (1,)), ((), ())), preferred_element_type=jnp.float32
        )
        return raw * scale, allowed_block(j)

    def first_pass(j, carry):
        @pl.when(flag_ref[j] > 0)
        def _():
            for h in range(heads):
                s, allowed = scores(j, h)
                top_ref[h] = jnp.maximum(top_ref[h], jnp.where(allowed, s, -1e30))
        return carry

    lax.fori_loop(0, n_blocks, first_pass, 0)
    for h in range(heads):
        top_ref[h] = jnp.broadcast_to(jnp.max(top_ref[h], axis=1, keepdims=True), top_ref.shape[1:])

    def second_pass(j, carry):
        @pl.when(flag_ref[j] > 0)
        def _():
            rows = pl.ds(pl.multiple_of(j * KEY_BLOCK, KEY_BLOCK), KEY_BLOCK)
            for h in range(heads):
                s, allowed = scores(j, h)
                weights = jnp.where(allowed, jnp.exp(s - top_ref[h]), 0.0)
                sum_ref[h] += weights
                value = kv_ref[rows, pl.ds(value_at + (h // groups) * head_size, head_size)]
                acc_ref[h] += jnp.dot(
                    weights.astype(jnp.bfloat16), value, preferred_element_type=jnp.float32
                )
        return carry

    lax.fori_loop(0, n_blocks, second_pass, 0)
    for h in range(heads):
        denominator = jnp.sum(sum_ref[h], axis=1, keepdims=True)
        out_ref[:, pl.ds(h * head_size, head_size)] = (acc_ref[h] / denominator).astype(out_ref.dtype)


def block_attention(query_rows, kv_rows, mask_block, groups, head_size):
    row_count = query_rows.shape[0]
    key_count = kv_rows.shape[0]
    heads = query_rows.shape[1] // head_size
    allowed = jnp.repeat(mask_block, TILE, axis=0).astype(jnp.bfloat16)
    tiles_per_block = KEY_BLOCK // TILE
    flags = jnp.max(
        mask_block.reshape(mask_block.shape[0], -1, tiles_per_block), axis=(0, 2)
    ).astype(jnp.int32)
    vmem = pl.BlockSpec(memory_space=pltpu.VMEM)
    return pl.pallas_call(
        functools.partial(attention_kernel, groups, head_size),
        out_shape=jax.ShapeDtypeStruct((row_count, heads * head_size), jnp.bfloat16),
        in_specs=[pl.BlockSpec(memory_space=pltpu.SMEM), vmem, vmem, vmem],
        out_specs=vmem,
        scratch_shapes=[
            pltpu.VMEM((heads, row_count, KEY_BLOCK), jnp.float32),
            pltpu.VMEM((heads, row_count, KEY_BLOCK), jnp.float32),
            pltpu.VMEM((heads, row_count, head_size), jnp.float32),
        ],
    )(flags, query_rows, kv_rows, allowed)


def shards(
    hidden_in,
    queries,
    key_proj,
    value_proj,
    tile_mask,
    out_weight,
    moe_gain,
    gate_weight,
    up_weight,
    down_weight,
    expert_ids,
    gate_probs,
):
    query_rows = queries[0]
    row_count = query_rows.shape[0]
    groups = HEADS // KV_HEADS
    head_size = D // HEADS
    query_heads = query_rows.reshape(row_count, KV_HEADS, groups, head_size)
    mask_block = tile_mask[0]
    kv_width = key_proj.shape[-1]
    kv_local = jnp.concatenate([key_proj[0], value_proj[0]], axis=-1)
    kv_piece = gather_ctx_kernel(kv_local).reshape(-1, 2 * kv_width)
    attended = block_attention(query_rows, kv_piece, mask_block, groups, head_size)
    projected = jnp.dot(attended, out_weight, preferred_element_type=jnp.float32)
    attention_out = projected.astype(jnp.bfloat16)
    residual = (hidden_in[0].astype(jnp.float32) + projected).astype(jnp.bfloat16)
    normed = rms_scale(residual, moe_gain).astype(jnp.bfloat16)
    id_row = expert_ids[0].reshape(-1)
    onehot = (id_row[:, None] == jnp.arange(EXPERTS, dtype=jnp.int32)[None, :]).astype(jnp.int32)
    before = jnp.cumsum(onehot, axis=0) - onehot
    slot_index = jnp.sum(before * onehot, axis=1)
    target = id_row * CAP + slot_index
    selector = (jnp.arange(EXPERTS * CAP, dtype=jnp.int32)[:, None] == target[None, :]).astype(
        jnp.bfloat16
    )
    repeated = jnp.repeat(normed, TOP, axis=0)
    outgoing = (
        jnp.dot(selector, repeated, preferred_element_type=jnp.float32)
        .astype(jnp.bfloat16)
        .reshape(EXPERTS, CAP, D)
    )
    arrived = exchange_exp(outgoing, 1).reshape(1, EXPERTS * CAP, D)
    ff = gate_weight.shape[-1]
    weight_piece = lax.all_gather(
        jnp.concatenate([gate_weight, up_weight, down_weight], axis=-1), CTX_AXES, axis=1, tiled=True
    )
    gate_piece = weight_piece[..., :ff]
    up_piece = weight_piece[..., ff : 2 * ff]
    down_piece = weight_piece[..., 2 * ff :]
    both_sums = jnp.dot(arrived[0], weight_piece[0, :, : 2 * ff], preferred_element_type=jnp.float32)
    gate_sum = both_sums[None, :, :ff]
    up_sum = both_sums[None, :, ff:]
    hidden = (jax.nn.silu(gate_sum) * up_sum).astype(jnp.bfloat16)
    expert_rows = jnp.einsum(
        "esf,edf->esd",
        hidden,
        down_piece,
        preferred_element_type=jnp.float32,
    ).astype(jnp.bfloat16)
    returned = exchange_exp(expert_rows.reshape(EXPERTS, CAP, D), 2)
    combine = jnp.sum(
        jnp.where(
            jnp.arange(EXPERTS * CAP, dtype=jnp.int32)[None, None, :] == target.reshape(row_count, TOP)[:, :, None],
            gate_probs[0][:, :, None],
            0.0,
        ),
        axis=1,
    )
    mixture = jnp.dot(
        combine,
        returned.reshape(EXPERTS * CAP, D).astype(jnp.float32),
        precision=lax.Precision.HIGHEST,
        preferred_element_type=jnp.float32,
    )
    layer_out = (residual.astype(jnp.float32) + mixture).astype(jnp.bfloat16)
    return (attention_out[None], layer_out[None])


def solution(mesh):
    n_ctx = mesh.shape["ctx"]
    split = jax.sharding.Mesh(
        mesh.devices.reshape(n_ctx // 4, 2, 2, mesh.shape["exp"]), CTX_AXES + ("exp",)
    )
    return jax.shard_map(
        shards,
        mesh=split,
        in_specs=(
            P("exp", CTX_AXES, None),
            P("exp", CTX_AXES, None),
            P("exp", CTX_AXES, None),
            P("exp", CTX_AXES, None),
            P("exp", CTX_AXES, None),
            P(),
            P(),
            P("exp", CTX_AXES, None),
            P("exp", CTX_AXES, None),
            P("exp", CTX_AXES, None),
            P("exp", CTX_AXES, None),
            P("exp", CTX_AXES, None),
        ),
        out_specs=(P("exp", CTX_AXES, None), P("exp", CTX_AXES, None)),
        check_vma=False,
    )
```
